512 devices in a mesh: grp: 32 (over x, z), voc: 16 (over y, core).
Axes of the slice: x: 4, y: 8, z: 8, core: 2. Of those that a mesh axis runs over, the one named last changes fastest.
Arguments:
- hidden: bfloat16 [24576, 4096], P('grp', 'voc'), may hold values from -50 to 50
- targets: int32 [24576], P('grp'), may hold values from 0 to 15999
- row_count: int32 [32], P('grp'), may hold values from 96 to 768, as said below
- norm_gain: bfloat16 [4096], replicated, may hold values from 0.099609375 to 1.8984375
- head_weight: bfloat16 [4096, 16000], P('grp', 'voc'), may hold values from -0.71 to 0.71
- return_from: int32 [24576], P('grp'), may hold values from 0 to 24575, each once
Outputs:
- token_logp: float32 [24576], P('grp')
- token_entropy: float32 [24576], P('grp')
The draws below stay inside these ranges and needn't reach their ends.
Inputs may be any that keep to these rules, and one draw needn't show every extreme that they name: `row_count`: the live rows of a group are its first ones. `return_from`: every slot index appears once.
All inputs are finite; a program needn't handle non-finite values.
Results may differ from the reference program's by a relative error of at most 0.0088.
Values may be sent and summed in bfloat16 or wider, within the bound.
A program may use at most 64 MiB of HBM per device.

```python
import math
import jax
import jax.numpy as jnp
import numpy as np
from jax import lax

D = 4096
VOCAB = 16000
TOK_GRP = 768
BLOCK = 128
ROWS = 24576
N_GRP = 32


def draw_hidden(key, part):
    keys = jax.random.split(jax.random.fold_in(key, 1), 2)
    total_rows = N_GRP * TOK_GRP
    base = jnp.clip(jax.random.normal(keys[0], (total_rows, D), jnp.float32), -5.0, 5.0)
    scales = jnp.exp(jax.random.uniform(keys[1], (total_rows, 1), jnp.float32, 0.0, math.log(10.0)))
    values = base * scales
    return values.astype(jnp.bfloat16)


def draw_head_weight(key, part):
    keys = jax.random.split(jax.random.fold_in(key, 2), 1)
    ramp = 1.0 + 2.0 * jnp.arange(VOCAB, dtype=jnp.float32) / (VOCAB - 1)
    factor = 3.0 / math.sqrt(D)
    base = jnp.clip(jax.random.normal(keys[0], (D, VOCAB), jnp.float32), -5.0, 5.0)
    values = base * factor * ramp[None, :]
    return values.astype(jnp.bfloat16)


def draw_row_count(key, part):
    keys = jax.random.split(jax.random.fold_in(key, 3), 2)
    counts = jax.random.randint(keys[0], (N_GRP,), max(TOK_GRP // 8, 1), TOK_GRP // 2 + 1)
    chosen = jax.random.permutation(keys[1], N_GRP)[:4]
    return counts.at[chosen].set(TOK_GRP).astype(jnp.int32)


def with_ends(result, rng, least, largest):
    place = [jax.random.randint(jax.random.fold_in(rng, axis), (), 0, length) for axis, length in enumerate(result.shape)]
    longest = result.shape.index(max(result.shape))
    beside = place[:longest] + [(place[longest] + 1) % result.shape[longest]] + place[longest + 1:]
    return result.at[tuple(place)].set(least).at[tuple(beside)].set(largest)


def rank_bounds(count, slope):
    weights = [(1 << 20) // math.isqrt(rank ** slope) + 1 for rank in range(1, count + 1)]
    width = 1 + sum(weights) // (1 << 30)
    return np.cumsum(np.array([max(1, weight // width) for weight in weights]))


def ranked_ids(own_key, dims, count, lean):
    grid = rank_bounds(count, lean)
    pick = jax.random.randint(jax.random.fold_in(own_key, 1), dims, 0, int(grid[count - 1]))
    standing = jnp.searchsorted(jnp.asarray(grid, jnp.int32), pick, side="right")
    return jax.random.permutation(jax.random.fold_in(own_key, 2), count)[standing].astype(jnp.int32)


def setup_inputs(seed: int = 0) -> dict:
    splits = jax.random.split(jax.random.key(seed), 7)
    hidden = draw_hidden(jax.random.fold_in(splits[6], 71), 0)
    targets = with_ends(ranked_ids(splits[1], (ROWS,), VOCAB, 2), jax.random.fold_in(splits[1], 3), 0, VOCAB - 1).astype(jnp.int32)
    row_count = draw_row_count(jax.random.fold_in(splits[6], 71), 0)
    norm_gain = jnp.clip(1.0 + 0.18 * jax.random.normal(splits[3], (D,), jnp.float32), 0.099609375, 1.8984375).astype(jnp.bfloat16)
    head_weight = draw_head_weight(jax.random.fold_in(splits[6], 71), 0)
    return_from = jax.random.permutation(splits[5], ROWS).astype(jnp.int32)
    return {"hidden": hidden, "targets": targets, "row_count": row_count, "norm_gain": norm_gain, "head_weight": head_weight, "return_from": return_from}


EPSILON = 1e-05

def normalize(raw, norm_gain):
    values = raw.astype(jnp.float32)
    scale = lax.rsqrt(lax.optimization_barrier(jnp.mean(values * values, axis=1, keepdims=True)) + EPSILON)
    return (values * scale * norm_gain.astype(jnp.float32)[None, :]).astype(jnp.bfloat16)

def reference(hidden, targets, row_count, norm_gain, head_weight, return_from):
    grouped = hidden.reshape(N_GRP, TOK_GRP, D)
    goals = targets.reshape(N_GRP, TOK_GRP)
    starts = jnp.arange(TOK_GRP // BLOCK, dtype=jnp.int32) * BLOCK

    def one_group(item):
        raw, goal, live = item
        normed = normalize(raw, norm_gain)

        def compute(begin):
            section = lax.dynamic_slice_in_dim(normed, begin, BLOCK, 0)
            wanted = lax.dynamic_slice_in_dim(goal, begin, BLOCK, 0)
            logits = jnp.dot(section, head_weight, preferred_element_type=jnp.float32)
            peak = lax.optimization_barrier(jnp.max(logits, axis=1))
            shifted = jnp.exp(logits - peak[:, None])
            total = lax.optimization_barrier(jnp.sum(shifted, axis=1))
            weighted = lax.optimization_barrier(jnp.sum(shifted * logits, axis=1))
            log_total = peak + jnp.log(total)
            picked = jnp.take_along_axis(logits, wanted[:, None], axis=1)[:, 0]
            return (picked - log_total, log_total - weighted / total)

        def skip(begin):
            empty = jnp.zeros((BLOCK,), jnp.float32)
            return (empty, empty)

        def one_block(begin):
            return lax.cond(begin < live, compute, skip, begin)
        logp, entropy = lax.map(one_block, starts)
        mask = jnp.arange(TOK_GRP, dtype=jnp.int32) < live
        logp = jnp.where(mask, logp.reshape(TOK_GRP), jnp.zeros((TOK_GRP,), jnp.float32))
        entropy = jnp.where(mask, entropy.reshape(TOK_GRP), jnp.zeros((TOK_GRP,), jnp.float32))
        return (logp, entropy)
    own_logp, own_entropy = lax.map(one_group, (grouped, goals, row_count))
    own_logp = own_logp.reshape(N_GRP * TOK_GRP)
    own_entropy = own_entropy.reshape(N_GRP * TOK_GRP)
    return (jnp.take(own_logp, return_from, axis=0), jnp.take(own_entropy, return_from, axis=0))
```

```python
import functools

import jax
import jax.numpy as jnp
from jax import lax
from jax.experimental import pallas as pl
from jax.experimental.pallas import tpu as pltpu
from jax.sharding import PartitionSpec as P

MESH = pl.DeviceIdType.MESH

EPSILON = 1e-05


def normalize(raw, norm_gain):
    values = raw.astype(jnp.float32)
    scale = lax.rsqrt(jnp.mean(values * values, axis=1, keepdims=True) + EPSILON)
    return (values * scale * norm_gain.astype(jnp.float32)[None, :]).astype(jnp.bfloat16)


def _share_kernel(axis, other, n, x_ref, o_ref, send_sem, recv_sem):
    me = lax.axis_index(axis)
    fixed = lax.axis_index(other)

    def dev(t):
        return (fixed, t) if axis == "voc" else (t, fixed)

    barrier = pltpu.get_barrier_semaphore()
    for k in range(1, n):
        pl.semaphore_signal(barrier, inc=1, device_id=dev(lax.rem(me + k, n)), device_id_type=MESH)
    pl.semaphore_wait(barrier, n - 1)
    copies = []
    for k in range(1, n):
        copy = pltpu.make_async_remote_copy(
            src_ref=x_ref,
            dst_ref=o_ref.at[pl.ds(me, 1)],
            send_sem=send_sem.at[k],
            recv_sem=recv_sem.at[k],
            device_id=dev(lax.rem(me + k, n)),
            device_id_type=MESH,
        )
        copy.start()
        copies.append(copy)
    o_ref[pl.ds(me, 1), :] = x_ref[...]
    for k in range(1, n):
        source = lax.rem(me + n - k, n)
        incoming = pltpu.make_async_remote_copy(
            src_ref=x_ref,
            dst_ref=o_ref.at[pl.ds(source, 1)],
            send_sem=send_sem.at[k],
            recv_sem=recv_sem.at[k],
            device_id=dev(source),
            device_id_type=MESH,
        )
        copies[k - 1].wait_send()
        incoming.wait_recv()


def share(row, axis, other, n, collective_id):
    width = row.shape[1]
    return pl.pallas_call(
        functools.partial(_share_kernel, axis, other, n),
        out_shape=jax.ShapeDtypeStruct((n, width), row.dtype),
        in_specs=[pl.BlockSpec(memory_space=pltpu.VMEM)],
        out_specs=pl.BlockSpec(memory_space=pltpu.VMEM),
        scratch_shapes=[pltpu.SemaphoreType.DMA((n,)), pltpu.SemaphoreType.DMA((n,))],
        compiler_params=pltpu.CompilerParams(collective_id=collective_id, has_side_effects=True),
    )(row)


def local(hidden, targets, row_count, norm_gain, head_weight, return_from, *, n_voc, n_grp):
    tok_rows = hidden.shape[0]
    positions = jnp.arange(tok_rows, dtype=jnp.int32)
    live_rows = positions < row_count[0]
    full_rows = lax.all_gather(hidden, "voc", axis=1, tiled=True)
    normed = normalize(full_rows, norm_gain)
    vocab_local = head_weight.shape[1]
    piece = lax.all_gather(head_weight, "grp", axis=0, tiled=True)
    logits = jnp.dot(normed, piece, preferred_element_type=jnp.float32)
    peak = jnp.max(logits, axis=1)
    shifted = jnp.exp(logits - peak[:, None])
    total = jnp.sum(shifted, axis=1)
    weighted = jnp.sum(shifted * logits, axis=1)
    global_columns = lax.axis_index("voc") * vocab_local + jnp.arange(vocab_local, dtype=jnp.int32)
    picked = jnp.sum(jnp.where(global_columns[None, :] == targets[:, None], logits, 0.0), axis=1)
    stats = jnp.concatenate([peak, total, weighted, picked])[None, :]
    parts = share(stats, "voc", "grp", n_voc, 0).reshape(n_voc, 4, tok_rows)
    peaks, totals, weights, picks = parts[:, 0], parts[:, 1], parts[:, 2], parts[:, 3]
    peak_all = jnp.max(peaks, axis=0)
    factor = jnp.exp(peaks - peak_all[None, :])
    total_all = jnp.sum(totals * factor, axis=0)
    weighted_all = jnp.sum(weights * factor, axis=0)
    picked_all = jnp.sum(picks, axis=0)
    log_total = peak_all + jnp.log(total_all)
    logp = jnp.where(live_rows, picked_all - log_total, 0.0)
    entropy = jnp.where(live_rows, log_total - weighted_all / total_all, 0.0)
    results = share(jnp.concatenate([logp, entropy])[None, :], "grp", "voc", n_grp, 1)
    results = results.reshape(n_grp, 2, tok_rows)
    every_logp = results[:, 0].reshape(n_grp * tok_rows)
    every_entropy = results[:, 1].reshape(n_grp * tok_rows)
    return (jnp.take(every_logp, return_from, axis=0), jnp.take(every_entropy, return_from, axis=0))


def solution(mesh):
    placed = (P("grp", "voc"), P("grp"), P("grp"), P(), P("grp", "voc"), P("grp"))
    body = functools.partial(local, n_voc=mesh.shape["voc"], n_grp=mesh.shape["grp"])
    return jax.shard_map(
        body, mesh=mesh, in_specs=placed, out_specs=(P("grp"), P("grp")), check_vma=False
    )
```

```python
import functools

import jax
import jax.numpy as jnp
from jax import lax
from jax.experimental import pallas as pl
from jax.experimental.pallas import tpu as pltpu
from jax.sharding import PartitionSpec as P

MESH = pl.DeviceIdType.MESH

EPSILON = 1e-05


def normalize(raw, norm_gain):
    values = raw.astype(jnp.float32)
    scale = lax.rsqrt(jnp.mean(values * values, axis=1, keepdims=True) + EPSILON)
    return (values * scale * norm_gain.astype(jnp.float32)[None, :]).astype(jnp.bfloat16)


def _share_kernel(axis, other, n, x_ref, o_ref, send_sem, recv_sem):
    me = lax.axis_index(axis)
    fixed = lax.axis_index(other)

    def dev(t):
        return (fixed, t) if axis == "voc" else (t, fixed)

    barrier = pltpu.get_barrier_semaphore()
    for k in range(1, n):
        pl.semaphore_signal(barrier, inc=1, device_id=dev(lax.rem(me + k, n)), device_id_type=MESH)
    pl.semaphore_wait(barrier, n - 1)
    copies = []
    for k in range(1, n):
        copy = pltpu.make_async_remote_copy(
            src_ref=x_ref,
            dst_ref=o_ref.at[pl.ds(me, 1)],
            send_sem=send_sem.at[k],
            recv_sem=recv_sem.at[k],
            device_id=dev(lax.rem(me + k, n)),
            device_id_type=MESH,
        )
        copy.start()
        copies.append(copy)
    o_ref[pl.ds(me, 1), :] = x_ref[...]
    for k in range(1, n):
        source = lax.rem(me + n - k, n)
        incoming = pltpu.make_async_remote_copy(
            src_ref=x_ref,
            dst_ref=o_ref.at[pl.ds(source, 1)],
            send_sem=send_sem.at[k],
            recv_sem=recv_sem.at[k],
            device_id=dev(source),
            device_id_type=MESH,
        )
        copies[k - 1].wait_send()
        incoming.wait_recv()


def _rows_kernel(n_y, x_ref, o_ref, s1, r1, s2, r2):
    me = lax.axis_index("voc")
    g = lax.axis_index("grp")
    width = x_ref.shape[1]
    y = me // 2
    c = me % 2
    partner = y * 2 + 1 - c

    def cols(v):
        return pl.ds(pl.multiple_of(v * width, width), width)

    def same_core(k):
        return lax.rem(y + k, n_y) * 2 + c

    def source(k):
        return lax.rem(y + n_y - k, n_y) * 2 + c

    barrier = pltpu.get_barrier_semaphore()
    for k in range(1, n_y):
        pl.semaphore_signal(barrier, inc=1, device_id=(g, same_core(k)), device_id_type=MESH)
    pl.semaphore_signal(barrier, inc=1, device_id=(g, partner), device_id_type=MESH)
    pl.semaphore_wait(barrier, n_y)

    def remote(src, dst, send, recv, target):
        return pltpu.make_async_remote_copy(
            src_ref=src, dst_ref=dst, send_sem=send, recv_sem=recv,
            device_id=(g, target), device_id_type=MESH,
        )

    sends = []
    for k in range(1, n_y):
        copy = remote(x_ref, o_ref.at[:, cols(me)], s1.at[k], r1.at[k], same_core(k))
        copy.start()
        sends.append(copy)
    copy = remote(x_ref, o_ref.at[:, cols(me)], s2.at[0], r2.at[0], partner)
    copy.start()
    sends.append(copy)
    o_ref[:, cols(me)] = x_ref[...]
    for k in range(1, n_y):
        block = o_ref.at[:, cols(source(k))]
        remote(x_ref, block, s1.at[k], r1.at[k], source(k)).wait_recv()
        copy = remote(block, block, s2.at[k], r2.at[k], partner)
        copy.start()
        sends.append(copy)
    for k in range(n_y):
        other = lax.rem(y + n_y - k, n_y) * 2 + 1 - c
        block = o_ref.at[:, cols(other)]
        remote(block, block, s2.at[k], r2.at[k], partner).wait_recv()
    for copy in sends:
        copy.wait_send()


def gather_rows(hidden, n_voc):
    rows, width = hidden.shape
    n_y = n_voc // 2
    return pl.pallas_call(
        functools.partial(_rows_kernel, n_y),
        out_shape=jax.ShapeDtypeStruct((rows, width * n_voc), hidden.dtype),
        in_specs=[pl.BlockSpec(memory_space=pltpu.VMEM)],
        out_specs=pl.BlockSpec(memory_space=pltpu.VMEM),
        scratch_shapes=[pltpu.SemaphoreType.DMA((n_y,))] * 4,
        compiler_params=pltpu.CompilerParams(collective_id=2, has_side_effects=True),
    )(hidden)


def share(row, axis, other, n, collective_id):
    width = row.shape[1]
    return pl.pallas_call(
        functools.partial(_share_kernel, axis, other, n),
        out_shape=jax.ShapeDtypeStruct((n, width), row.dtype),
        in_specs=[pl.BlockSpec(memory_space=pltpu.VMEM)],
        out_specs=pl.BlockSpec(memory_space=pltpu.VMEM),
        scratch_shapes=[pltpu.SemaphoreType.DMA((n,)), pltpu.SemaphoreType.DMA((n,))],
        compiler_params=pltpu.CompilerParams(collective_id=collective_id, has_side_effects=True),
    )(row)


def local(hidden, targets, row_count, norm_gain, head_weight, return_from, *, n_voc, n_grp):
    tok_rows = hidden.shape[0]
    positions = jnp.arange(tok_rows, dtype=jnp.int32)
    live_rows = positions < row_count[0]
    full_rows = gather_rows(hidden, n_voc)
    normed = normalize(full_rows, norm_gain)
    vocab_local = head_weight.shape[1]
    piece = lax.all_gather(head_weight, "grp", axis=0, tiled=True)
    logits = jnp.dot(normed, piece, preferred_element_type=jnp.float32)
    peak = jnp.max(logits, axis=1)
    shifted = jnp.exp(logits - peak[:, None])
    total = jnp.sum(shifted, axis=1)
    weighted = jnp.sum(shifted * logits, axis=1)
    global_columns = lax.axis_index("voc") * vocab_local + jnp.arange(vocab_local, dtype=jnp.int32)
    picked = jnp.sum(jnp.where(global_columns[None, :] == targets[:, None], logits, 0.0), axis=1)
    stats = jnp.concatenate([peak, total, weighted, picked])[None, :]
    parts = share(stats, "voc", "grp", n_voc, 0).reshape(n_voc, 4, tok_rows)
    peaks, totals, weights, picks = parts[:, 0], parts[:, 1], parts[:, 2], parts[:, 3]
    peak_all = jnp.max(peaks, axis=0)
    factor = jnp.exp(peaks - peak_all[None, :])
    total_all = jnp.sum(totals * factor, axis=0)
    weighted_all = jnp.sum(weights * factor, axis=0)
    picked_all = jnp.sum(picks, axis=0)
    log_total = peak_all + jnp.log(total_all)
    logp = jnp.where(live_rows, picked_all - log_total, 0.0)
    entropy = jnp.where(live_rows, log_total - weighted_all / total_all, 0.0)
    results = share(jnp.concatenate([logp, entropy])[None, :], "grp", "voc", n_grp, 1)
    results = results.reshape(n_grp, 2, tok_rows)
    every_logp = results[:, 0].reshape(n_grp * tok_rows)
    every_entropy = results[:, 1].reshape(n_grp * tok_rows)
    return (jnp.take(every_logp, return_from, axis=0), jnp.take(every_entropy, return_from, axis=0))


def solution(mesh):
    placed = (P("grp", "voc"), P("grp"), P("grp"), P(), P("grp", "voc"), P("grp"))
    body = functools.partial(local, n_voc=mesh.shape["voc"], n_grp=mesh.shape["grp"])
    return jax.shard_map(
        body, mesh=mesh, in_specs=placed, out_specs=(P("grp"), P("grp")), check_vma=False
    )
```

```python
import functools

import jax
import jax.numpy as jnp
from jax import lax
from jax.experimental import pallas as pl
from jax.experimental.pallas import tpu as pltpu
from jax.sharding import PartitionSpec as P

MESH = pl.DeviceIdType.MESH

EPSILON = 1e-05


def normalize(raw, norm_gain):
    values = raw.astype(jnp.float32)
    scale = lax.rsqrt(jnp.mean(values * values, axis=1, keepdims=True) + EPSILON)
    return (values * scale * norm_gain.astype(jnp.float32)[None, :]).astype(jnp.bfloat16)


def _share_kernel(axis, other, n, x_ref, o_ref, send_sem, recv_sem):
    me = lax.axis_index(axis)
    fixed = lax.axis_index(other)

    def dev(t):
        return (fixed, t) if axis == "voc" else (t, fixed)

    barrier = pltpu.get_barrier_semaphore()
    for k in range(1, n):
        pl.semaphore_signal(barrier, inc=1, device_id=dev(lax.rem(me + k, n)), device_id_type=MESH)
    pl.semaphore_wait(barrier, n - 1)
    copies = []
    for k in range(1, n):
        copy = pltpu.make_async_remote_copy(
            src_ref=x_ref,
            dst_ref=o_ref.at[pl.ds(me, 1)],
            send_sem=send_sem.at[k],
            recv_sem=recv_sem.at[k],
            device_id=dev(lax.rem(me + k, n)),
            device_id_type=MESH,
        )
        copy.start()
        copies.append(copy)
    o_ref[pl.ds(me, 1), :] = x_ref[...]
    for k in range(1, n):
        source = lax.rem(me + n - k, n)
        incoming = pltpu.make_async_remote_copy(
            src_ref=x_ref,
            dst_ref=o_ref.at[pl.ds(source, 1)],
            send_sem=send_sem.at[k],
            recv_sem=recv_sem.at[k],
            device_id=dev(source),
            device_id_type=MESH,
        )
        copies[k - 1].wait_send()
        incoming.wait_recv()


def _rows_kernel(n_y, x_ref, o_ref, s1, r1, s2, r2):
    me = lax.axis_index("voc")
    g = lax.axis_index("grp")
    width = x_ref.shape[1]
    y = me // 2
    c = me % 2
    partner = y * 2 + 1 - c

    def cols(v):
        return pl.ds(pl.multiple_of(v * width, width), width)

    def same_core(k):
        return lax.rem(y + k, n_y) * 2 + c

    def source(k):
        return lax.rem(y + n_y - k, n_y) * 2 + c

    barrier = pltpu.get_barrier_semaphore()
    for k in range(1, n_y):
        pl.semaphore_signal(barrier, inc=1, device_id=(g, same_core(k)), device_id_type=MESH)
    pl.semaphore_signal(barrier, inc=1, device_id=(g, partner), device_id_type=MESH)
    pl.semaphore_wait(barrier, n_y)

    def remote(src, dst, send, recv, target):
        return pltpu.make_async_remote_copy(
            src_ref=src, dst_ref=dst, send_sem=send, recv_sem=recv,
            device_id=(g, target), device_id_type=MESH,
        )

    sends = []
    for k in range(1, n_y):
        copy = remote(x_ref, o_ref.at[:, cols(me)], s1.at[k], r1.at[k], same_core(k))
        copy.start()
        sends.append(copy)
    copy = remote(x_ref, o_ref.at[:, cols(me)], s2.at[0], r2.at[0], partner)
    copy.start()
    sends.append(copy)
    o_ref[:, cols(me)] = x_ref[...]
    for k in range(1, n_y):
        block = o_ref.at[:, cols(source(k))]
        remote(x_ref, block, s1.at[k], r1.at[k], source(k)).wait_recv()
        copy = remote(block, block, s2.at[k], r2.at[k], partner)
        copy.start()
        sends.append(copy)
    for k in range(n_y):
        other = lax.rem(y + n_y - k, n_y) * 2 + 1 - c
        block = o_ref.at[:, cols(other)]
        remote(block, block, s2.at[k], r2.at[k], partner).wait_recv()
    for copy in sends:
        copy.wait_send()


def gather_rows(hidden, n_voc):
    rows, width = hidden.shape
    n_y = n_voc // 2
    return pl.pallas_call(
        functools.partial(_rows_kernel, n_y),
        out_shape=jax.ShapeDtypeStruct((rows, width * n_voc), hidden.dtype),
        in_specs=[pl.BlockSpec(memory_space=pltpu.VMEM)],
        out_specs=pl.BlockSpec(memory_space=pltpu.VMEM),
        scratch_shapes=[pltpu.SemaphoreType.DMA((n_y,))] * 4,
        compiler_params=pltpu.CompilerParams(collective_id=2, has_side_effects=True),
    )(hidden)


class _Ring:
    def __init__(self, pos, n, device, slot, own, sems):
        self.pos, self.n, self.device, self.slot, self.own = pos, n, device, slot, own
        self.sems = sems
        self.right = n // 2
        self.left = n - 1 - self.right
        self.copies = []

    def _copy(self, origin, kind, s, target):
        view = self.slot(origin)
        return pltpu.make_async_remote_copy(
            src_ref=view, dst_ref=view,
            send_sem=self.sems.at[kind, s], recv_sem=self.sems.at[kind + 1, s],
            device_id=self.device(target), device_id_type=MESH,
        )

    def _origin(self, step, sign):
        return lax.rem(self.pos + sign * step + 2 * self.n, self.n)

    def step(self, s):
        for count, kind, sign in ((self.right, 0, 1), (self.left, 2, -1)):
            if s > count:
                continue
            target = self._origin(1, sign)
            origin = self._origin(s - 1, -sign)
            if s == 1:
                src = self.own
            else:
                self._copy(origin, kind, s - 2, target).wait_recv()
                src = self.slot(origin)
            copy = pltpu.make_async_remote_copy(
                src_ref=src, dst_ref=self.slot(origin),
                send_sem=self.sems.at[kind, s - 1], recv_sem=self.sems.at[kind + 1, s - 1],
                device_id=self.device(target), device_id_type=MESH,
            )
            copy.start()
            self.copies.append(copy)

    def finish_recv(self):
        for count, kind, sign in ((self.right, 0, 1), (self.left, 2, -1)):
            if count:
                self._copy(self._origin(count, -sign), kind, count - 1, self._origin(1, sign)).wait_recv()

    def finish_send(self):
        for copy in self.copies:
            copy.wait_send()


def _head_kernel(n_x, n_z, x_ref, o_ref, local_sem, sems):
    me = lax.axis_index("grp")
    v = lax.axis_index("voc")
    x = me // n_z
    z = me % n_z
    half = x_ref.shape[0] // 2
    lo, hi = pl.ds(0, half), pl.ds(half, half)

    def along_x(t):
        return (t * n_z + z, v)

    def along_z(t):
        return (x * n_z + t, v)

    barrier = pltpu.get_barrier_semaphore()
    neighbours = [along_x(lax.rem(x + 1, n_x)), along_x(lax.rem(x + n_x - 1, n_x)),
                  along_z(lax.rem(z + 1, n_z)), along_z(lax.rem(z + n_z - 1, n_z))]
    for target in neighbours:
        pl.semaphore_signal(barrier, inc=1, device_id=target, device_id_type=MESH)
    pl.semaphore_wait(barrier, len(neighbours))

    own = pltpu.make_async_copy(x_ref, o_ref.at[x, z], local_sem.at[0])
    own.start()
    first_x = _Ring(x, n_x, along_x, lambda t: o_ref.at[t, z, lo], x_ref.at[lo], sems.at[0])
    first_z = _Ring(z, n_z, along_z, lambda t: o_ref.at[x, t, hi], x_ref.at[hi], sems.at[1])
    for s in range(1, max(n_x, n_z)):
        first_x.step(s)
        first_z.step(s)
    own.wait()
    first_x.finish_recv()
    first_z.finish_recv()
    second_z = _Ring(z, n_z, along_z, lambda t: o_ref.at[:, t, lo], o_ref.at[:, z, lo], sems.at[2])
    second_x = _Ring(x, n_x, along_x, lambda t: o_ref.at[t, :, hi], o_ref.at[x, :, hi], sems.at[3])
    for s in range(1, max(n_x, n_z)):
        second_z.step(s)
        second_x.step(s)
    second_z.finish_recv()
    second_x.finish_recv()
    for ring in (first_x, first_z, second_z, second_x):
        ring.finish_send()


def gather_head(piece, n_x, n_z):
    rows, width = piece.shape
    full = pl.pallas_call(
        functools.partial(_head_kernel, n_x, n_z),
        out_shape=jax.ShapeDtypeStruct((n_x, n_z, rows, width), piece.dtype),
        in_specs=[pl.BlockSpec(memory_space=pltpu.VMEM)],
        out_specs=pl.BlockSpec(memory_space=pltpu.VMEM),
        scratch_shapes=[pltpu.SemaphoreType.DMA((1,)), pltpu.SemaphoreType.DMA((4, 4, max(n_x, n_z)))],
        compiler_params=pltpu.CompilerParams(collective_id=3, has_side_effects=True),
    )(piece)
    return full.reshape(n_x * n_z * rows, width)


def share(row, axis, other, n, collective_id):
    width = row.shape[1]
    return pl.pallas_call(
        functools.partial(_share_kernel, axis, other, n),
        out_shape=jax.ShapeDtypeStruct((n, width), row.dtype),
        in_specs=[pl.BlockSpec(memory_space=pltpu.VMEM)],
        out_specs=pl.BlockSpec(memory_space=pltpu.VMEM),
        scratch_shapes=[pltpu.SemaphoreType.DMA((n,)), pltpu.SemaphoreType.DMA((n,))],
        compiler_params=pltpu.CompilerParams(collective_id=collective_id, has_side_effects=True),
    )(row)


def local(hidden, targets, row_count, norm_gain, head_weight, return_from, *, n_voc, n_grp, n_x, n_z):
    tok_rows = hidden.shape[0]
    positions = jnp.arange(tok_rows, dtype=jnp.int32)
    live_rows = positions < row_count[0]
    full_rows = lax.all_gather(hidden, "voc", axis=1, tiled=True)
    normed = normalize(full_rows, norm_gain)
    vocab_local = head_weight.shape[1]
    piece = gather_head(head_weight, n_x, n_z)
    logits = jnp.dot(normed, piece, preferred_element_type=jnp.float32)
    peak = jnp.max(logits, axis=1)
    shifted = jnp.exp(logits - peak[:, None])
    total = jnp.sum(shifted, axis=1)
    weighted = jnp.sum(shifted * logits, axis=1)
    global_columns = lax.axis_index("voc") * vocab_local + jnp.arange(vocab_local, dtype=jnp.int32)
    picked = jnp.sum(jnp.where(global_columns[None, :] == targets[:, None], logits, 0.0), axis=1)
    stats = jnp.concatenate([peak, total, weighted, picked])[None, :]
    parts = share(stats, "voc", "grp", n_voc, 0).reshape(n_voc, 4, tok_rows)
    peaks, totals, weights, picks = parts[:, 0], parts[:, 1], parts[:, 2], parts[:, 3]
    peak_all = jnp.max(peaks, axis=0)
    factor = jnp.exp(peaks - peak_all[None, :])
    total_all = jnp.sum(totals * factor, axis=0)
    weighted_all = jnp.sum(weights * factor, axis=0)
    picked_all = jnp.sum(picks, axis=0)
    log_total = peak_all + jnp.log(total_all)
    logp = jnp.where(live_rows, picked_all - log_total, 0.0)
    entropy = jnp.where(live_rows, log_total - weighted_all / total_all, 0.0)
    results = share(jnp.concatenate([logp, entropy])[None, :], "grp", "voc", n_grp, 1)
    results = results.reshape(n_grp, 2, tok_rows)
    every_logp = results[:, 0].reshape(n_grp * tok_rows)
    every_entropy = results[:, 1].reshape(n_grp * tok_rows)
    return (jnp.take(every_logp, return_from, axis=0), jnp.take(every_entropy, return_from, axis=0))


def solution(mesh):
    placed = (P("grp", "voc"), P("grp"), P("grp"), P(), P("grp", "voc"), P("grp"))
    n_grp = mesh.shape["grp"]
    n_z = len({device.coords[2] for device in mesh.devices[:, 0]})
    body = functools.partial(local, n_voc=mesh.shape["voc"], n_grp=n_grp, n_x=n_grp // n_z, n_z=n_z)
    return jax.shard_map(
        body, mesh=mesh, in_specs=placed, out_specs=(P("grp"), P("grp")), check_vma=False
    )
```

```python
import functools

import jax
import jax.numpy as jnp
from jax import lax
from jax.experimental import pallas as pl
from jax.experimental.pallas import tpu as pltpu
from jax.sharding import PartitionSpec as P

MESH = pl.DeviceIdType.MESH

EPSILON = 1e-05


def normalize(raw, norm_gain):
    values = raw.astype(jnp.float32)
    scale = lax.rsqrt(jnp.mean(values * values, axis=1, keepdims=True) + EPSILON)
    return (values * scale * norm_gain.astype(jnp.float32)[None, :]).astype(jnp.bfloat16)


def _share_kernel(axis, other, n, x_ref, o_ref, send_sem, recv_sem):
    me = lax.axis_index(axis)
    fixed = lax.axis_index(other)

    def dev(t):
        return (fixed, t) if axis == "voc" else (t, fixed)

    barrier = pltpu.get_barrier_semaphore()
    for k in range(1, n):
        pl.semaphore_signal(barrier, inc=1, device_id=dev(lax.rem(me + k, n)), device_id_type=MESH)
    pl.semaphore_wait(barrier, n - 1)
    copies = []
    for k in range(1, n):
        copy = pltpu.make_async_remote_copy(
            src_ref=x_ref,
            dst_ref=o_ref.at[pl.ds(me, 1)],
            send_sem=send_sem.at[k],
            recv_sem=recv_sem.at[k],
            device_id=dev(lax.rem(me + k, n)),
            device_id_type=MESH,
        )
        copy.start()
        copies.append(copy)
    o_ref[pl.ds(me, 1), :] = x_ref[...]
    for k in range(1, n):
        source = lax.rem(me + n - k, n)
        incoming = pltpu.make_async_remote_copy(
            src_ref=x_ref,
            dst_ref=o_ref.at[pl.ds(source, 1)],
            send_sem=send_sem.at[k],
            recv_sem=recv_sem.at[k],
            device_id=dev(source),
            device_id_type=MESH,
        )
        copies[k - 1].wait_send()
        incoming.wait_recv()


class _Ring:
    def __init__(self, pos, n, device, slot, own, sems, on_arrival=None):
        self.pos, self.n, self.device, self.slot, self.own = pos, n, device, slot, own
        self.sems = sems
        self.on_arrival = on_arrival
        self.right = n // 2
        self.left = n - 1 - self.right
        self.copies = []

    def _copy(self, origin, kind, s, target):
        view = self.slot(origin)
        return pltpu.make_async_remote_copy(
            src_ref=view, dst_ref=view,
            send_sem=self.sems.at[kind, s], recv_sem=self.sems.at[kind + 1, s],
            device_id=self.device(target), device_id_type=MESH,
        )

    def _origin(self, step, sign):
        return lax.rem(self.pos + sign * step + 2 * self.n, self.n)

    def step(self, s):
        for count, kind, sign in ((self.right, 0, 1), (self.left, 2, -1)):
            if s > count:
                continue
            target = self._origin(1, sign)
            origin = self._origin(s - 1, -sign)
            if s == 1:
                src = self.own
            else:
                self._copy(origin, kind, s - 2, target).wait_recv()
                if self.on_arrival is not None:
                    self.on_arrival(origin)
                src = self.slot(origin)
            copy = pltpu.make_async_remote_copy(
                src_ref=src, dst_ref=self.slot(origin),
                send_sem=self.sems.at[kind, s - 1], recv_sem=self.sems.at[kind + 1, s - 1],
                device_id=self.device(target), device_id_type=MESH,
            )
            copy.start()
            self.copies.append(copy)

    def finish_recv(self):
        for count, kind, sign in ((self.right, 0, 1), (self.left, 2, -1)):
            if count:
                origin = self._origin(count, -sign)
                self._copy(origin, kind, count - 1, self._origin(1, sign)).wait_recv()
                if self.on_arrival is not None:
                    self.on_arrival(origin)

    def finish_send(self):
        for copy in self.copies:
            copy.wait_send()


def _gather_kernel(n_x, n_z, n_y, rows_ref, head_ref, rows_out, head_out, local_sem, sems, pair_sems):
    me = lax.axis_index("grp")
    v = lax.axis_index("voc")
    x = me // n_z
    z = me % n_z
    y = v // 2
    c = v % 2
    partner = y * 2 + 1 - c
    half = head_ref.shape[0] // 2
    lo, hi = pl.ds(0, half), pl.ds(half, half)
    width = rows_ref.shape[1]

    def cols(t):
        return pl.ds(pl.multiple_of(t * width, width), width)

    def along_x(t):
        return (t * n_z + z, v)

    def along_z(t):
        return (x * n_z + t, v)

    def along_y(t):
        return (me, t * 2 + c)

    barrier = pltpu.get_barrier_semaphore()
    neighbours = [along_x(lax.rem(x + 1, n_x)), along_x(lax.rem(x + n_x - 1, n_x)),
                  along_z(lax.rem(z + 1, n_z)), along_z(lax.rem(z + n_z - 1, n_z)),
                  along_y(lax.rem(y + 1, n_y)), along_y(lax.rem(y + n_y - 1, n_y)),
                  (me, partner)]
    for target in neighbours:
        pl.semaphore_signal(barrier, inc=1, device_id=target, device_id_type=MESH)
    pl.semaphore_wait(barrier, len(neighbours))

    def to_partner(src, t):
        return pltpu.make_async_remote_copy(
            src_ref=src, dst_ref=rows_out.at[:, cols(t * 2 + c)],
            send_sem=pair_sems.at[0, t], recv_sem=pair_sems.at[1, t],
            device_id=(me, partner), device_id_type=MESH,
        )

    pair_copies = []

    def forward(t):
        copy = to_partner(rows_out.at[:, cols(t * 2 + c)], t)
        copy.start()
        pair_copies.append(copy)

    own = pltpu.make_async_copy(head_ref, head_out.at[x, z], local_sem.at[0])
    own.start()
    copy = to_partner(rows_ref, y)
    copy.start()
    pair_copies.append(copy)
    rows_out[:, cols(v)] = rows_ref[...]
    rows = _Ring(y, n_y, along_y, lambda t: rows_out.at[:, cols(t * 2 + c)], rows_ref, sems.at[4], forward)
    first_x = _Ring(x, n_x, along_x, lambda t: head_out.at[t, z, lo], head_ref.at[lo], sems.at[0])
    first_z = _Ring(z, n_z, along_z, lambda t: head_out.at[x, t, hi], head_ref.at[hi], sems.at[1])
    steps = max(n_x, n_z, n_y)
    rows.step(1)
    for s in range(1, steps):
        first_x.step(s)
        first_z.step(s)
    own.wait()
    first_x.finish_recv()
    first_z.finish_recv()
    second_z = _Ring(z, n_z, along_z, lambda t: head_out.at[:, t, lo], head_out.at[:, z, lo], sems.at[2])
    second_x = _Ring(x, n_x, along_x, lambda t: head_out.at[t, :, hi], head_out.at[x, :, hi], sems.at[3])
    for s in range(1, steps):
        second_z.step(s)
        second_x.step(s)
        rows.step(s + 1)
    rows.finish_recv()
    second_z.finish_recv()
    second_x.finish_recv()
    for t in range(n_y):
        other = t * 2 + 1 - c
        block = rows_out.at[:, cols(other)]
        pltpu.make_async_remote_copy(
            src_ref=block, dst_ref=block,
            send_sem=pair_sems.at[0, t], recv_sem=pair_sems.at[1, t],
            device_id=(me, partner), device_id_type=MESH,
        ).wait_recv()
    for ring in (first_x, first_z, second_z, second_x, rows):
        ring.finish_send()
    for copy in pair_copies:
        copy.wait_send()


def gather_both(hidden, piece, n_x, n_z, n_voc):
    rows, width = hidden.shape
    depth, vocab = piece.shape
    n_y = n_voc // 2
    steps = max(n_x, n_z, n_y)
    full_rows, full_head = pl.pallas_call(
        functools.partial(_gather_kernel, n_x, n_z, n_y),
        out_shape=(jax.ShapeDtypeStruct((rows, width * n_voc), hidden.dtype),
                   jax.ShapeDtypeStruct((n_x, n_z, depth, vocab), piece.dtype)),
        in_specs=[pl.BlockSpec(memory_space=pltpu.VMEM)] * 2,
        out_specs=(pl.BlockSpec(memory_space=pltpu.VMEM), pl.BlockSpec(memory_space=pltpu.VMEM)),
        scratch_shapes=[pltpu.SemaphoreType.DMA((1,)), pltpu.SemaphoreType.DMA((5, 4, steps)),
                        pltpu.SemaphoreType.DMA((2, n_y))],
        compiler_params=pltpu.CompilerParams(collective_id=3, has_side_effects=True),
    )(hidden, piece)
    return full_rows, full_head.reshape(n_x * n_z * depth, vocab)


def share(row, axis, other, n, collective_id):
    width = row.shape[1]
    return pl.pallas_call(
        functools.partial(_share_kernel, axis, other, n),
        out_shape=jax.ShapeDtypeStruct((n, width), row.dtype),
        in_specs=[pl.BlockSpec(memory_space=pltpu.VMEM)],
        out_specs=pl.BlockSpec(memory_space=pltpu.VMEM),
        scratch_shapes=[pltpu.SemaphoreType.DMA((n,)), pltpu.SemaphoreType.DMA((n,))],
        compiler_params=pltpu.CompilerParams(collective_id=collective_id, has_side_effects=True),
    )(row)


def local(hidden, targets, row_count, norm_gain, head_weight, return_from, *, n_voc, n_grp, n_x, n_z):
    tok_rows = hidden.shape[0]
    positions = jnp.arange(tok_rows, dtype=jnp.int32)
    live_rows = positions < row_count[0]
    full_rows, piece = gather_both(hidden, head_weight, n_x, n_z, n_voc)
    normed = normalize(full_rows, norm_gain)
    vocab_local = head_weight.shape[1]
    logits = jnp.dot(normed, piece, preferred_element_type=jnp.float32)
    peak = jnp.max(logits, axis=1)
    shifted = jnp.exp(logits - peak[:, None])
    total = jnp.sum(shifted, axis=1)
    weighted = jnp.sum(shifted * logits, axis=1)
    global_columns = lax.axis_index("voc") * vocab_local + jnp.arange(vocab_local, dtype=jnp.int32)
    picked = jnp.sum(jnp.where(global_columns[None, :] == targets[:, None], logits, 0.0), axis=1)
    stats = jnp.concatenate([peak, total, weighted, picked])[None, :]
    parts = share(stats, "voc", "grp", n_voc, 0).reshape(n_voc, 4, tok_rows)
    peaks, totals, weights, picks = parts[:, 0], parts[:, 1], parts[:, 2], parts[:, 3]
    peak_all = jnp.max(peaks, axis=0)
    factor = jnp.exp(peaks - peak_all[None, :])
    total_all = jnp.sum(totals * factor, axis=0)
    weighted_all = jnp.sum(weights * factor, axis=0)
    picked_all = jnp.sum(picks, axis=0)
    log_total = peak_all + jnp.log(total_all)
    logp = jnp.where(live_rows, picked_all - log_total, 0.0)
    entropy = jnp.where(live_rows, log_total - weighted_all / total_all, 0.0)
    results = share(jnp.concatenate([logp, entropy])[None, :], "grp", "voc", n_grp, 1)
    results = results.reshape(n_grp, 2, tok_rows)
    every_logp = results[:, 0].reshape(n_grp * tok_rows)
    every_entropy = results[:, 1].reshape(n_grp * tok_rows)
    return (jnp.take(every_logp, return_from, axis=0), jnp.take(every_entropy, return_from, axis=0))


def solution(mesh):
    placed = (P("grp", "voc"), P("grp"), P("grp"), P(), P("grp", "voc"), P("grp"))
    n_grp = mesh.shape["grp"]
    n_z = len({device.coords[2] for device in mesh.devices[:, 0]})
    body = functools.partial(local, n_voc=mesh.shape["voc"], n_grp=n_grp, n_x=n_grp // n_z, n_z=n_z)
    return jax.shard_map(
        body, mesh=mesh, in_specs=placed, out_specs=(P("grp"), P("grp")), check_vma=False
    )
```

```python
import functools

import jax
import jax.numpy as jnp
from jax import lax
from jax.experimental import pallas as pl
from jax.experimental.pallas import tpu as pltpu
from jax.sharding import PartitionSpec as P

MESH = pl.DeviceIdType.MESH

EPSILON = 1e-05


def normalize(raw, norm_gain):
    values = raw.astype(jnp.float32)
    scale = lax.rsqrt(jnp.mean(values * values, axis=1, keepdims=True) + EPSILON)
    return (values * scale * norm_gain.astype(jnp.float32)[None, :]).astype(jnp.bfloat16)


def _share_kernel(axis, other, n, x_ref, o_ref, send_sem, recv_sem):
    me = lax.axis_index(axis)
    fixed = lax.axis_index(other)

    def dev(t):
        return (fixed, t) if axis == "voc" else (t, fixed)

    barrier = pltpu.get_barrier_semaphore()
    for k in range(1, n):
        pl.semaphore_signal(barrier, inc=1, device_id=dev(lax.rem(me + k, n)), device_id_type=MESH)
    pl.semaphore_wait(barrier, n - 1)
    copies = []
    for k in range(1, n):
        copy = pltpu.make_async_remote_copy(
            src_ref=x_ref,
            dst_ref=o_ref.at[me],
            send_sem=send_sem.at[k],
            recv_sem=recv_sem.at[k],
            device_id=dev(lax.rem(me + k, n)),
            device_id_type=MESH,
        )
        copy.start()
        copies.append(copy)
    o_ref[me] = x_ref[...]
    for k in range(1, n):
        source = lax.rem(me + n - k, n)
        incoming = pltpu.make_async_remote_copy(
            src_ref=x_ref,
            dst_ref=o_ref.at[source],
            send_sem=send_sem.at[k],
            recv_sem=recv_sem.at[k],
            device_id=dev(source),
            device_id_type=MESH,
        )
        copies[k - 1].wait_send()
        incoming.wait_recv()


class _Ring:
    def __init__(self, pos, n, device, slot, own, sems, on_arrival=None):
        self.pos, self.n, self.device, self.slot, self.own = pos, n, device, slot, own
        self.sems = sems
        self.on_arrival = on_arrival
        self.right = n // 2
        self.left = n - 1 - self.right
        self.copies = []

    def _copy(self, origin, kind, s, target):
        view = self.slot(origin)
        return pltpu.make_async_remote_copy(
            src_ref=view, dst_ref=view,
            send_sem=self.sems.at[kind, s], recv_sem=self.sems.at[kind + 1, s],
            device_id=self.device(target), device_id_type=MESH,
        )

    def _origin(self, step, sign):
        return lax.rem(self.pos + sign * step + 2 * self.n, self.n)

    def step(self, s):
        for count, kind, sign in ((self.right, 0, 1), (self.left, 2, -1)):
            if s > count:
                continue
            target = self._origin(1, sign)
            origin = self._origin(s - 1, -sign)
            if s == 1:
                src = self.own
            else:
                self._copy(origin, kind, s - 2, target).wait_recv()
                if self.on_arrival is not None:
                    self.on_arrival(origin)
                src = self.slot(origin)
            copy = pltpu.make_async_remote_copy(
                src_ref=src, dst_ref=self.slot(origin),
                send_sem=self.sems.at[kind, s - 1], recv_sem=self.sems.at[kind + 1, s - 1],
                device_id=self.device(target), device_id_type=MESH,
            )
            copy.start()
            self.copies.append(copy)

    def finish_recv(self):
        for count, kind, sign in ((self.right, 0, 1), (self.left, 2, -1)):
            if count:
                origin = self._origin(count, -sign)
                self._copy(origin, kind, count - 1, self._origin(1, sign)).wait_recv()
                if self.on_arrival is not None:
                    self.on_arrival(origin)

    def finish_send(self):
        for copy in self.copies:
            copy.wait_send()


def _gather_kernel(n_x, n_z, n_y, rows_ref, head_ref, rows_out, head_out, local_sem, sems, pair_sems):
    me = lax.axis_index("grp")
    v = lax.axis_index("voc")
    x = me // n_z
    z = me % n_z
    y = v // 2
    c = v % 2
    partner = y * 2 + 1 - c
    half = head_ref.shape[0] // 2
    lo, hi = pl.ds(0, half), pl.ds(half, half)
    width = rows_ref.shape[1]

    def cols(t):
        return pl.ds(pl.multiple_of(t * width, width), width)

    def along_x(t):
        return (t * n_z + z, v)

    def along_z(t):
        return (x * n_z + t, v)

    def along_y(t):
        return (me, t * 2 + c)

    barrier = pltpu.get_barrier_semaphore()
    neighbours = [along_x(lax.rem(x + 1, n_x)), along_x(lax.rem(x + n_x - 1, n_x)),
                  along_z(lax.rem(z + 1, n_z)), along_z(lax.rem(z + n_z - 1, n_z)),
                  along_y(lax.rem(y + 1, n_y)), along_y(lax.rem(y + n_y - 1, n_y)),
                  (me, partner)]
    for target in neighbours:
        pl.semaphore_signal(barrier, inc=1, device_id=target, device_id_type=MESH)
    pl.semaphore_wait(barrier, len(neighbours))

    def to_partner(src, t):
        return pltpu.make_async_remote_copy(
            src_ref=src, dst_ref=rows_out.at[:, cols(t * 2 + c)],
            send_sem=pair_sems.at[0, t], recv_sem=pair_sems.at[1, t],
            device_id=(me, partner), device_id_type=MESH,
        )

    pair_copies = []

    def forward(t):
        copy = to_partner(rows_out.at[:, cols(t * 2 + c)], t)
        copy.start()
        pair_copies.append(copy)

    own = pltpu.make_async_copy(head_ref, head_out.at[x, z], local_sem.at[0])
    own.start()
    copy = to_partner(rows_ref, y)
    copy.start()
    pair_copies.append(copy)
    rows_out[:, cols(v)] = rows_ref[...]
    rows = _Ring(y, n_y, along_y, lambda t: rows_out.at[:, cols(t * 2 + c)], rows_ref, sems.at[4], forward)
    first_x = _Ring(x, n_x, along_x, lambda t: head_out.at[t, z, lo], head_ref.at[lo], sems.at[0])
    first_z = _Ring(z, n_z, along_z, lambda t: head_out.at[x, t, hi], head_ref.at[hi], sems.at[1])
    steps = max(n_x, n_z, n_y)
    rows.step(1)
    for s in range(1, steps):
        first_x.step(s)
        first_z.step(s)
    own.wait()
    first_x.finish_recv()
    first_z.finish_recv()
    second_z = _Ring(z, n_z, along_z, lambda t: head_out.at[:, t, lo], head_out.at[:, z, lo], sems.at[2])
    second_x = _Ring(x, n_x, along_x, lambda t: head_out.at[t, :, hi], head_out.at[x, :, hi], sems.at[3])
    for s in range(1, steps):
        second_z.step(s)
        second_x.step(s)
        rows.step(s + 1)
    rows.finish_recv()
    second_z.finish_recv()
    second_x.finish_recv()
    for t in range(n_y):
        other = t * 2 + 1 - c
        block = rows_out.at[:, cols(other)]
        pltpu.make_async_remote_copy(
            src_ref=block, dst_ref=block,
            send_sem=pair_sems.at[0, t], recv_sem=pair_sems.at[1, t],
            device_id=(me, partner), device_id_type=MESH,
        ).wait_recv()
    for ring in (first_x, first_z, second_z, second_x, rows):
        ring.finish_send()
    for copy in pair_copies:
        copy.wait_send()


def gather_both(hidden, piece, n_x, n_z, n_voc):
    rows, width = hidden.shape
    depth, vocab = piece.shape
    n_y = n_voc // 2
    steps = max(n_x, n_z, n_y)
    full_rows, full_head = pl.pallas_call(
        functools.partial(_gather_kernel, n_x, n_z, n_y),
        out_shape=(jax.ShapeDtypeStruct((rows, width * n_voc), hidden.dtype),
                   jax.ShapeDtypeStruct((n_x, n_z, depth, vocab), piece.dtype)),
        in_specs=[pl.BlockSpec(memory_space=pltpu.VMEM)] * 2,
        out_specs=(pl.BlockSpec(memory_space=pltpu.VMEM), pl.BlockSpec(memory_space=pltpu.VMEM)),
        scratch_shapes=[pltpu.SemaphoreType.DMA((1,)), pltpu.SemaphoreType.DMA((5, 4, steps)),
                        pltpu.SemaphoreType.DMA((2, n_y))],
        compiler_params=pltpu.CompilerParams(collective_id=3, has_side_effects=True),
    )(hidden, piece)
    return full_rows, full_head.reshape(n_x * n_z * depth, vocab)


def share(block, axis, other, n, collective_id):
    return pl.pallas_call(
        functools.partial(_share_kernel, axis, other, n),
        out_shape=jax.ShapeDtypeStruct((n,) + block.shape, block.dtype),
        in_specs=[pl.BlockSpec(memory_space=pltpu.VMEM)],
        out_specs=pl.BlockSpec(memory_space=pltpu.VMEM),
        scratch_shapes=[pltpu.SemaphoreType.DMA((n,)), pltpu.SemaphoreType.DMA((n,))],
        compiler_params=pltpu.CompilerParams(collective_id=collective_id, has_side_effects=True),
    )(block)


def local(hidden, targets, row_count, norm_gain, head_weight, return_from, *, n_voc, n_grp, n_x, n_z):
    tok_rows = hidden.shape[0]
    positions = jnp.arange(tok_rows, dtype=jnp.int32)
    live_rows = positions < row_count[0]
    full_rows, piece = gather_both(hidden, head_weight, n_x, n_z, n_voc)
    normed = normalize(full_rows, norm_gain)
    vocab_local = head_weight.shape[1]
    logits = jnp.dot(normed, piece, preferred_element_type=jnp.float32)
    peak = jnp.max(logits, axis=1)
    shifted = jnp.exp(logits - peak[:, None])
    total = jnp.sum(shifted, axis=1)
    weighted = jnp.sum(shifted * logits, axis=1)
    global_columns = lax.axis_index("voc") * vocab_local + jnp.arange(vocab_local, dtype=jnp.int32)
    picked = jnp.sum(jnp.where(global_columns[None, :] == targets[:, None], logits, 0.0), axis=1)
    stats = jnp.concatenate([peak, total, weighted, picked]).reshape(8, -1)
    parts = share(stats, "voc", "grp", n_voc, 0).reshape(n_voc, 4, tok_rows)
    peaks, totals, weights, picks = parts[:, 0], parts[:, 1], parts[:, 2], parts[:, 3]
    peak_all = jnp.max(peaks, axis=0)
    factor = jnp.exp(peaks - peak_all[None, :])
    total_all = jnp.sum(totals * factor, axis=0)
    weighted_all = jnp.sum(weights * factor, axis=0)
    picked_all = jnp.sum(picks, axis=0)
    log_total = peak_all + jnp.log(total_all)
    logp = jnp.where(live_rows, picked_all - log_total, 0.0)
    entropy = jnp.where(live_rows, log_total - weighted_all / total_all, 0.0)
    both = jnp.concatenate([logp, entropy]).reshape(-1, 128)
    results = share(both, "grp", "voc", n_grp, 1).reshape(n_grp, 2, tok_rows)
    every = jnp.transpose(results, (0, 2, 1)).reshape(n_grp * tok_rows, 2)
    picked_rows = jnp.take(every, return_from, axis=0)
    return (picked_rows[:, 0], picked_rows[:, 1])


def solution(mesh):
    placed = (P("grp", "voc"), P("grp"), P("grp"), P(), P("grp", "voc"), P("grp"))
    n_grp = mesh.shape["grp"]
    n_z = len({device.coords[2] for device in mesh.devices[:, 0]})
    body = functools.partial(local, n_voc=mesh.shape["voc"], n_grp=n_grp, n_x=n_grp // n_z, n_z=n_z)
    return jax.shard_map(
        body, mesh=mesh, in_specs=placed, out_specs=(P("grp"), P("grp")), check_vma=False
    )
```

```python
import functools

import jax
import jax.numpy as jnp
from jax import lax
from jax.experimental import pallas as pl
from jax.experimental.pallas import tpu as pltpu
from jax.sharding import PartitionSpec as P

MESH = pl.DeviceIdType.MESH

EPSILON = 1e-05


def normalize(raw, norm_gain):
    values = raw.astype(jnp.float32)
    scale = lax.rsqrt(jnp.mean(values * values, axis=1, keepdims=True) + EPSILON)
    return (values * scale * norm_gain.astype(jnp.float32)[None, :]).astype(jnp.bfloat16)


def _share_kernel(axis, other, n, x_ref, o_ref, send_sem, recv_sem):
    me = lax.axis_index(axis)
    fixed = lax.axis_index(other)

    def dev(t):
        return (fixed, t) if axis == "voc" else (t, fixed)

    barrier = pltpu.get_barrier_semaphore()
    for k in range(1, n):
        pl.semaphore_signal(barrier, inc=1, device_id=dev(lax.rem(me + k, n)), device_id_type=MESH)
    pl.semaphore_wait(barrier, n - 1)
    copies = []
    for k in range(1, n):
        copy = pltpu.make_async_remote_copy(
            src_ref=x_ref,
            dst_ref=o_ref.at[me],
            send_sem=send_sem.at[k],
            recv_sem=recv_sem.at[k],
            device_id=dev(lax.rem(me + k, n)),
            device_id_type=MESH,
        )
        copy.start()
        copies.append(copy)
    o_ref[me] = x_ref[...]
    for k in range(1, n):
        source = lax.rem(me + n - k, n)
        incoming = pltpu.make_async_remote_copy(
            src_ref=x_ref,
            dst_ref=o_ref.at[source],
            send_sem=send_sem.at[k],
            recv_sem=recv_sem.at[k],
            device_id=dev(source),
            device_id_type=MESH,
        )
        copies[k - 1].wait_send()
        incoming.wait_recv()


class _Ring:
    def __init__(self, pos, n, device, slot, own, sems, on_arrival=None):
        self.pos, self.n, self.device, self.slot, self.own = pos, n, device, slot, own
        self.sems = sems
        self.on_arrival = on_arrival
        self.steps = n // 2
        self.split = n % 2 == 0
        self.copies = []

    def _part(self, s, kind):
        return kind // 2 if self.split and s == self.steps else None

    def _origin(self, step, sign):
        return lax.rem(self.pos + sign * step + 2 * self.n, self.n)

    def _desc(self, src, origin, kind, s, target):
        return pltpu.make_async_remote_copy(
            src_ref=src, dst_ref=self.slot(origin, self._part(s, kind)),
            send_sem=self.sems.at[kind, s - 1], recv_sem=self.sems.at[kind + 1, s - 1],
            device_id=self.device(target), device_id_type=MESH,
        )

    def step(self, s):
        if s > self.steps:
            return
        for kind, sign in ((0, 1), (2, -1)):
            target = self._origin(1, sign)
            origin = self._origin(s - 1, -sign)
            part = self._part(s, kind)
            if s == 1:
                src = self.own(part)
            else:
                self._desc(self.slot(origin), origin, kind, s - 1, target).wait_recv()
                if self.on_arrival is not None:
                    self.on_arrival(origin)
                src = self.slot(origin, part)
            copy = self._desc(src, origin, kind, s, target)
            copy.start()
            self.copies.append(copy)

    def finish_recv(self):
        if not self.steps:
            return
        last = []
        for kind, sign in ((0, 1), (2, -1)):
            origin = self._origin(self.steps, -sign)
            view = self.slot(origin, self._part(self.steps, kind))
            self._desc(view, origin, kind, self.steps, self._origin(1, sign)).wait_recv()
            last.append(origin)
        if self.on_arrival is not None:
            for origin in last[:1] if self.split else last:
                self.on_arrival(origin)

    def finish_send(self):
        for copy in self.copies:
            copy.wait_send()


def _gather_kernel(n_x, n_z, n_y, rows_ref, head_ref, rows_out, head_out, local_sem, sems, pair_sems):
    me = lax.axis_index("grp")
    v = lax.axis_index("voc")
    x = me // n_z
    z = me % n_z
    y = v // 2
    c = v % 2
    partner = y * 2 + 1 - c
    half = head_ref.shape[0] // 2
    lo, hi = pl.ds(0, half), pl.ds(half, half)
    width = rows_ref.shape[1]

    def cols(t):
        return pl.ds(pl.multiple_of(t * width, width), width)

    def along_x(t):
        return (t * n_z + z, v)

    def along_z(t):
        return (x * n_z + t, v)

    def along_y(t):
        return (me, t * 2 + c)

    barrier = pltpu.get_barrier_semaphore()
    neighbours = [along_x(lax.rem(x + 1, n_x)), along_x(lax.rem(x + n_x - 1, n_x)),
                  along_z(lax.rem(z + 1, n_z)), along_z(lax.rem(z + n_z - 1, n_z)),
                  along_y(lax.rem(y + 1, n_y)), along_y(lax.rem(y + n_y - 1, n_y)),
                  (me, partner)]
    for target in neighbours:
        pl.semaphore_signal(barrier, inc=1, device_id=target, device_id_type=MESH)
    pl.semaphore_wait(barrier, len(neighbours))

    def to_partner(src, t):
        return pltpu.make_async_remote_copy(
            src_ref=src, dst_ref=rows_out.at[:, cols(t * 2 + c)],
            send_sem=pair_sems.at[0, t], recv_sem=pair_sems.at[1, t],
            device_id=(me, partner), device_id_type=MESH,
        )

    pair_copies = []

    def forward(t):
        copy = to_partner(rows_out.at[:, cols(t * 2 + c)], t)
        copy.start()
        pair_copies.append(copy)

    own = pltpu.make_async_copy(head_ref, head_out.at[x, z], local_sem.at[0])
    own.start()
    copy = to_partner(rows_ref, y)
    copy.start()
    pair_copies.append(copy)
    rows_out[:, cols(v)] = rows_ref[...]
    def halves(size, start=0):
        return lambda part: pl.ds(start, size) if part is None else pl.ds(start + part * (size // 2), size // 2)

    rows_part = halves(rows_ref.shape[0])
    lo_part, hi_part = halves(half), halves(half, half)
    x_part, z_part = halves(n_x), halves(n_z)
    rows = _Ring(y, n_y, along_y, lambda t, p=None: rows_out.at[rows_part(p), cols(t * 2 + c)],
                 lambda p: rows_ref.at[rows_part(p)], sems.at[4], forward)
    first_x = _Ring(x, n_x, along_x, lambda t, p=None: head_out.at[t, z, lo_part(p)],
                    lambda p: head_ref.at[lo_part(p)], sems.at[0])
    first_z = _Ring(z, n_z, along_z, lambda t, p=None: head_out.at[x, t, hi_part(p)],
                    lambda p: head_ref.at[hi_part(p)], sems.at[1])
    steps = max(n_x, n_z, n_y)
    rows.step(1)
    for s in range(1, steps):
        first_x.step(s)
        first_z.step(s)
    own.wait()
    first_x.finish_recv()
    first_z.finish_recv()
    second_z = _Ring(z, n_z, along_z, lambda t, p=None: head_out.at[x_part(p), t, lo],
                     lambda p: head_out.at[x_part(p), z, lo], sems.at[2])
    second_x = _Ring(x, n_x, along_x, lambda t, p=None: head_out.at[t, z_part(p), hi],
                     lambda p: head_out.at[x, z_part(p), hi], sems.at[3])
    for s in range(1, steps):
        second_z.step(s)
        second_x.step(s)
        rows.step(s + 1)
    rows.finish_recv()
    second_z.finish_recv()
    second_x.finish_recv()
    for t in range(n_y):
        other = t * 2 + 1 - c
        block = rows_out.at[:, cols(other)]
        pltpu.make_async_remote_copy(
            src_ref=block, dst_ref=block,
            send_sem=pair_sems.at[0, t], recv_sem=pair_sems.at[1, t],
            device_id=(me, partner), device_id_type=MESH,
        ).wait_recv()
    for ring in (first_x, first_z, second_z, second_x, rows):
        ring.finish_send()
    for copy in pair_copies:
        copy.wait_send()


def gather_both(hidden, piece, n_x, n_z, n_voc):
    rows, width = hidden.shape
    depth, vocab = piece.shape
    n_y = n_voc // 2
    steps = max(n_x, n_z, n_y)
    full_rows, full_head = pl.pallas_call(
        functools.partial(_gather_kernel, n_x, n_z, n_y),
        out_shape=(jax.ShapeDtypeStruct((rows, width * n_voc), hidden.dtype),
                   jax.ShapeDtypeStruct((n_x, n_z, depth, vocab), piece.dtype)),
        in_specs=[pl.BlockSpec(memory_space=pltpu.VMEM)] * 2,
        out_specs=(pl.BlockSpec(memory_space=pltpu.VMEM), pl.BlockSpec(memory_space=pltpu.VMEM)),
        scratch_shapes=[pltpu.SemaphoreType.DMA((1,)), pltpu.SemaphoreType.DMA((5, 4, steps)),
                        pltpu.SemaphoreType.DMA((2, n_y))],
        compiler_params=pltpu.CompilerParams(collective_id=3, has_side_effects=True),
    )(hidden, piece)
    return full_rows, full_head.reshape(n_x * n_z * depth, vocab)


def share(block, axis, other, n, collective_id):
    return pl.pallas_call(
        functools.partial(_share_kernel, axis, other, n),
        out_shape=jax.ShapeDtypeStruct((n,) + block.shape, block.dtype),
        in_specs=[pl.BlockSpec(memory_space=pltpu.VMEM)],
        out_specs=pl.BlockSpec(memory_space=pltpu.VMEM),
        scratch_shapes=[pltpu.SemaphoreType.DMA((n,)), pltpu.SemaphoreType.DMA((n,))],
        compiler_params=pltpu.CompilerParams(collective_id=collective_id, has_side_effects=True),
    )(block)


def local(hidden, targets, row_count, norm_gain, head_weight, return_from, *, n_voc, n_grp, n_x, n_z):
    tok_rows = hidden.shape[0]
    positions = jnp.arange(tok_rows, dtype=jnp.int32)
    live_rows = positions < row_count[0]
    full_rows, piece = gather_both(hidden, head_weight, n_x, n_z, n_voc)
    normed = normalize(full_rows, norm_gain)
    vocab_local = head_weight.shape[1]
    logits = jnp.dot(normed, piece, preferred_element_type=jnp.float32)
    peak = jnp.max(logits, axis=1)
    shifted = jnp.exp(logits - peak[:, None])
    total = jnp.sum(shifted, axis=1)
    weighted = jnp.sum(shifted * logits, axis=1)
    global_columns = lax.axis_index("voc") * vocab_local + jnp.arange(vocab_local, dtype=jnp.int32)
    picked = jnp.sum(jnp.where(global_columns[None, :] == targets[:, None], logits, 0.0), axis=1)
    stats = jnp.concatenate([peak, total, weighted, picked]).reshape(8, -1)
    parts = share(stats, "voc", "grp", n_voc, 0).reshape(n_voc, 4, tok_rows)
    peaks, totals, weights, picks = parts[:, 0], parts[:, 1], parts[:, 2], parts[:, 3]
    peak_all = jnp.max(peaks, axis=0)
    factor = jnp.exp(peaks - peak_all[None, :])
    total_all = jnp.sum(totals * factor, axis=0)
    weighted_all = jnp.sum(weights * factor, axis=0)
    picked_all = jnp.sum(picks, axis=0)
    log_total = peak_all + jnp.log(total_all)
    logp = jnp.where(live_rows, picked_all - log_total, 0.0)
    entropy = jnp.where(live_rows, log_total - weighted_all / total_all, 0.0)
    both = jnp.concatenate([logp, entropy]).reshape(-1, 128)
    results = share(both, "grp", "voc", n_grp, 1).reshape(n_grp, 2, tok_rows)
    every_logp = results[:, 0].reshape(n_grp * tok_rows)
    every_entropy = results[:, 1].reshape(n_grp * tok_rows)
    return (jnp.take(every_logp, return_from, axis=0), jnp.take(every_entropy, return_from, axis=0))


def solution(mesh):
    placed = (P("grp", "voc"), P("grp"), P("grp"), P(), P("grp", "voc"), P("grp"))
    n_grp = mesh.shape["grp"]
    n_z = len({device.coords[2] for device in mesh.devices[:, 0]})
    body = functools.partial(local, n_voc=mesh.shape["voc"], n_grp=n_grp, n_x=n_grp // n_z, n_z=n_z)
    return jax.shard_map(
        body, mesh=mesh, in_specs=placed, out_specs=(P("grp"), P("grp")), check_vma=False
    )
```

```python
import functools

import jax
import jax.numpy as jnp
from jax import lax
from jax.experimental import pallas as pl
from jax.experimental.pallas import tpu as pltpu
from jax.sharding import PartitionSpec as P

MESH = pl.DeviceIdType.MESH

EPSILON = 1e-05


def normalize(raw, norm_gain):
    values = raw.astype(jnp.float32)
    scale = lax.rsqrt(jnp.mean(values * values, axis=1, keepdims=True) + EPSILON)
    return (values * scale * norm_gain.astype(jnp.float32)[None, :]).astype(jnp.bfloat16)


def _share_kernel(axis, other, n, x_ref, o_ref, send_sem, recv_sem):
    me = lax.axis_index(axis)
    fixed = lax.axis_index(other)

    def dev(t):
        return (fixed, t) if axis == "voc" else (t, fixed)

    barrier = pltpu.get_barrier_semaphore()
    for k in range(1, n):
        pl.semaphore_signal(barrier, inc=1, device_id=dev(lax.rem(me + k, n)), device_id_type=MESH)
    pl.semaphore_wait(barrier, n - 1)
    copies = []
    for k in range(1, n):
        copy = pltpu.make_async_remote_copy(
            src_ref=x_ref,
            dst_ref=o_ref.at[me],
            send_sem=send_sem.at[k],
            recv_sem=recv_sem.at[k],
            device_id=dev(lax.rem(me + k, n)),
            device_id_type=MESH,
        )
        copy.start()
        copies.append(copy)
    o_ref[me] = x_ref[...]
    for k in range(1, n):
        source = lax.rem(me + n - k, n)
        incoming = pltpu.make_async_remote_copy(
            src_ref=x_ref,
            dst_ref=o_ref.at[source],
            send_sem=send_sem.at[k],
            recv_sem=recv_sem.at[k],
            device_id=dev(source),
            device_id_type=MESH,
        )
        copies[k - 1].wait_send()
        incoming.wait_recv()


class _Ring:
    def __init__(self, pos, n, device, slot, own, sems, on_arrival=None):
        self.pos, self.n, self.device, self.slot, self.own = pos, n, device, slot, own
        self.sems = sems
        self.on_arrival = on_arrival
        self.steps = n // 2
        self.split = n % 2 == 0
        self.copies = []

    def _part(self, s, kind):
        return kind // 2 if self.split and s == self.steps else None

    def _origin(self, step, sign):
        return lax.rem(self.pos + sign * step + 2 * self.n, self.n)

    def _desc(self, src, origin, kind, s, target):
        return pltpu.make_async_remote_copy(
            src_ref=src, dst_ref=self.slot(origin, self._part(s, kind)),
            send_sem=self.sems.at[kind, s - 1], recv_sem=self.sems.at[kind + 1, s - 1],
            device_id=self.device(target), device_id_type=MESH,
        )

    def step(self, s):
        if s > self.steps:
            return
        for kind, sign in ((0, 1), (2, -1)):
            target = self._origin(1, sign)
            origin = self._origin(s - 1, -sign)
            part = self._part(s, kind)
            if s == 1:
                src = self.own(part)
            else:
                self._desc(self.slot(origin), origin, kind, s - 1, target).wait_recv()
                if self.on_arrival is not None:
                    self.on_arrival(origin)
                src = self.slot(origin, part)
            copy = self._desc(src, origin, kind, s, target)
            copy.start()
            self.copies.append(copy)

    def finish_recv(self):
        if not self.steps:
            return
        last = []
        for kind, sign in ((0, 1), (2, -1)):
            origin = self._origin(self.steps, -sign)
            view = self.slot(origin, self._part(self.steps, kind))
            self._desc(view, origin, kind, self.steps, self._origin(1, sign)).wait_recv()
            last.append(origin)
        if self.on_arrival is not None:
            for origin in last[:1] if self.split else last:
                self.on_arrival(origin)

    def finish_send(self):
        for copy in self.copies:
            copy.wait_send()


def _gather_kernel(n_x, n_z, n_y, rows_ref, head_ref, rows_out, head_out, local_sem, sems, pair_sems):
    me = lax.axis_index("grp")
    v = lax.axis_index("voc")
    x = me // n_z
    z = me % n_z
    y = v // 2
    c = v % 2
    partner = y * 2 + 1 - c
    half = head_ref.shape[0] // 2
    lo, hi = pl.ds(0, half), pl.ds(half, half)
    width = rows_ref.shape[1]

    def cols(t):
        return pl.ds(pl.multiple_of(t * width, width), width)

    def along_x(t):
        return (t * n_z + z, v)

    def along_z(t):
        return (x * n_z + t, v)

    def along_y(t):
        return (me, t * 2 + c)

    barrier = pltpu.get_barrier_semaphore()
    neighbours = [along_x(lax.rem(x + 1, n_x)), along_x(lax.rem(x + n_x - 1, n_x)),
                  along_z(lax.rem(z + 1, n_z)), along_z(lax.rem(z + n_z - 1, n_z)),
                  along_y(lax.rem(y + 1, n_y)), along_y(lax.rem(y + n_y - 1, n_y)),
                  (me, partner)]
    for target in neighbours:
        pl.semaphore_signal(barrier, inc=1, device_id=target, device_id_type=MESH)
    pl.semaphore_wait(barrier, len(neighbours))

    def to_partner(src, t):
        return pltpu.make_async_remote_copy(
            src_ref=src, dst_ref=rows_out.at[:, cols(t * 2 + c)],
            send_sem=pair_sems.at[0, t], recv_sem=pair_sems.at[1, t],
            device_id=(me, partner), device_id_type=MESH,
        )

    pair_copies = []

    def forward(t):
        copy = to_partner(rows_out.at[:, cols(t * 2 + c)], t)
        copy.start()
        pair_copies.append(copy)

    own = pltpu.make_async_copy(head_ref, head_out.at[x, z], local_sem.at[0])
    own.start()
    copy = to_partner(rows_ref, y)
    copy.start()
    pair_copies.append(copy)
    rows_out[:, cols(v)] = rows_ref[...]
    def halves(size, start=0):
        return lambda part: pl.ds(start, size) if part is None else pl.ds(start + part * (size // 2), size // 2)

    rows_part = halves(rows_ref.shape[0])
    lo_part, hi_part = halves(half), halves(half, half)
    x_part, z_part = halves(n_x), halves(n_z)
    rows = _Ring(y, n_y, along_y, lambda t, p=None: rows_out.at[rows_part(p), cols(t * 2 + c)],
                 lambda p: rows_ref.at[rows_part(p)], sems.at[4], forward)
    first_x = _Ring(x, n_x, along_x, lambda t, p=None: head_out.at[t, z, lo_part(p)],
                    lambda p: head_ref.at[lo_part(p)], sems.at[0])
    first_z = _Ring(z, n_z, along_z, lambda t, p=None: head_out.at[x, t, hi_part(p)],
                    lambda p: head_ref.at[hi_part(p)], sems.at[1])
    steps = max(n_x, n_z, n_y)
    rows.step(1)
    for s in range(1, steps):
        first_x.step(s)
        first_z.step(s)
    own.wait()
    first_x.finish_recv()
    first_z.finish_recv()
    second_z = _Ring(z, n_z, along_z, lambda t, p=None: head_out.at[x_part(p), t, lo],
                     lambda p: head_out.at[x_part(p), z, lo], sems.at[2])
    second_x = _Ring(x, n_x, along_x, lambda t, p=None: head_out.at[t, z_part(p), hi],
                     lambda p: head_out.at[x, z_part(p), hi], sems.at[3])
    for s in range(1, steps):
        second_z.step(s)
        second_x.step(s)
        rows.step(s + 1)
    rows.finish_recv()
    second_z.finish_recv()
    second_x.finish_recv()
    for t in range(n_y):
        other = t * 2 + 1 - c
        block = rows_out.at[:, cols(other)]
        pltpu.make_async_remote_copy(
            src_ref=block, dst_ref=block,
            send_sem=pair_sems.at[0, t], recv_sem=pair_sems.at[1, t],
            device_id=(me, partner), device_id_type=MESH,
        ).wait_recv()
    for ring in (first_x, first_z, second_z, second_x, rows):
        ring.finish_send()
    for copy in pair_copies:
        copy.wait_send()


def gather_both(hidden, piece, n_x, n_z, n_voc):
    rows, width = hidden.shape
    depth, vocab = piece.shape
    n_y = n_voc // 2
    steps = max(n_x, n_z, n_y)
    full_rows, full_head = pl.pallas_call(
        functools.partial(_gather_kernel, n_x, n_z, n_y),
        out_shape=(jax.ShapeDtypeStruct((rows, width * n_voc), hidden.dtype),
                   jax.ShapeDtypeStruct((n_x, n_z, depth, vocab), piece.dtype)),
        in_specs=[pl.BlockSpec(memory_space=pltpu.VMEM)] * 2,
        out_specs=(pl.BlockSpec(memory_space=pltpu.VMEM), pl.BlockSpec(memory_space=pltpu.VMEM)),
        scratch_shapes=[pltpu.SemaphoreType.DMA((1,)), pltpu.SemaphoreType.DMA((5, 4, steps)),
                        pltpu.SemaphoreType.DMA((2, n_y))],
        compiler_params=pltpu.CompilerParams(collective_id=3, has_side_effects=True),
    )(hidden, piece)
    return full_rows, full_head.reshape(n_x * n_z * depth, vocab)


def share(block, axis, other, n, collective_id):
    return pl.pallas_call(
        functools.partial(_share_kernel, axis, other, n),
        out_shape=jax.ShapeDtypeStruct((n,) + block.shape, block.dtype),
        in_specs=[pl.BlockSpec(memory_space=pltpu.VMEM)],
        out_specs=pl.BlockSpec(memory_space=pltpu.VMEM),
        scratch_shapes=[pltpu.SemaphoreType.DMA((n,)), pltpu.SemaphoreType.DMA((n,))],
        compiler_params=pltpu.CompilerParams(collective_id=collective_id, has_side_effects=True),
    )(block)


def local(hidden, targets, row_count, norm_gain, head_weight, return_from, *, n_voc, n_grp, n_x, n_z):
    tok_rows = hidden.shape[0]
    positions = jnp.arange(tok_rows, dtype=jnp.int32)
    live_rows = positions < row_count[0]
    full_rows, piece = gather_both(hidden, head_weight, n_x, n_z, n_voc)
    normed = normalize(full_rows, norm_gain)
    vocab_local = head_weight.shape[1]
    logits = jnp.dot(normed, piece, preferred_element_type=jnp.float32)
    peak = jnp.max(logits, axis=1)
    shifted = jnp.exp(logits - peak[:, None])
    total = jnp.sum(shifted, axis=1)
    weighted = jnp.sum(shifted * logits, axis=1)
    global_columns = lax.axis_index("voc") * vocab_local + jnp.arange(vocab_local, dtype=jnp.int32)
    picked = jnp.sum(jnp.where(global_columns[None, :] == targets[:, None], logits, 0.0), axis=1)
    stats = jnp.concatenate([peak, total, weighted, picked]).reshape(8, -1)
    parts = share(stats, "voc", "grp", n_voc, 0).reshape(n_voc, 4, tok_rows)
    peaks, totals, weights, picks = parts[:, 0], parts[:, 1], parts[:, 2], parts[:, 3]
    peak_all = jnp.max(peaks, axis=0)
    factor = jnp.exp(peaks - peak_all[None, :])
    total_all = jnp.sum(totals * factor, axis=0)
    weighted_all = jnp.sum(weights * factor, axis=0)
    picked_all = jnp.sum(picks, axis=0)
    log_total = peak_all + jnp.log(total_all)
    logp = jnp.where(live_rows, picked_all - log_total, 0.0)
    entropy = jnp.where(live_rows, log_total - weighted_all / total_all, 0.0)
    both = jnp.concatenate([logp, entropy]).reshape(-1, 128)
    results = share(both, "grp", "voc", n_grp, 1).reshape(n_grp, 2, tok_rows)
    lanes = 128
    every = jnp.concatenate(
        [results[:, 0].reshape(-1, lanes), results[:, 1].reshape(-1, lanes)], axis=1)
    high = return_from // lanes
    low = return_from % lanes
    pick_row = (high[:, None] == jnp.arange(every.shape[0], dtype=jnp.int32)[None, :]).astype(jnp.float32)
    rows_picked = jnp.dot(pick_row, every, precision=lax.Precision.HIGHEST)
    pick_lane = low[:, None] == jnp.arange(lanes, dtype=jnp.int32)[None, :]
    token_logp = jnp.sum(jnp.where(pick_lane, rows_picked[:, :lanes], 0.0), axis=1)
    token_entropy = jnp.sum(jnp.where(pick_lane, rows_picked[:, lanes:], 0.0), axis=1)
    return (token_logp, token_entropy)


def solution(mesh):
    placed = (P("grp", "voc"), P("grp"), P("grp"), P(), P("grp", "voc"), P("grp"))
    n_grp = mesh.shape["grp"]
    n_z = len({device.coords[2] for device in mesh.devices[:, 0]})
    body = functools.partial(local, n_voc=mesh.shape["voc"], n_grp=n_grp, n_x=n_grp // n_z, n_z=n_z)
    return jax.shard_map(
        body, mesh=mesh, in_specs=placed, out_specs=(P("grp"), P("grp")), check_vma=False
    )
```

```python
import functools

import jax
import jax.numpy as jnp
from jax import lax
from jax.experimental import pallas as pl
from jax.experimental.pallas import tpu as pltpu
from jax.sharding import PartitionSpec as P

MESH = pl.DeviceIdType.MESH

EPSILON = 1e-05


def normalize(raw, norm_gain):
    values = raw.astype(jnp.float32)
    scale = lax.rsqrt(jnp.mean(values * values, axis=1, keepdims=True) + EPSILON)
    return (values * scale * norm_gain.astype(jnp.float32)[None, :]).astype(jnp.bfloat16)


def _share_kernel(axis, other, n, x_ref, o_ref, send_sem, recv_sem):
    me = lax.axis_index(axis)
    fixed = lax.axis_index(other)

    def dev(t):
        return (fixed, t) if axis == "voc" else (t, fixed)

    barrier = pltpu.get_barrier_semaphore()
    for k in range(1, n):
        pl.semaphore_signal(barrier, inc=1, device_id=dev(lax.rem(me + k, n)), device_id_type=MESH)
    pl.semaphore_wait(barrier, n - 1)
    copies = []
    for k in range(1, n):
        copy = pltpu.make_async_remote_copy(
            src_ref=x_ref,
            dst_ref=o_ref.at[me],
            send_sem=send_sem.at[k],
            recv_sem=recv_sem.at[k],
            device_id=dev(lax.rem(me + k, n)),
            device_id_type=MESH,
        )
        copy.start()
        copies.append(copy)
    o_ref[me] = x_ref[...]
    for k in range(1, n):
        source = lax.rem(me + n - k, n)
        incoming = pltpu.make_async_remote_copy(
            src_ref=x_ref,
            dst_ref=o_ref.at[source],
            send_sem=send_sem.at[k],
            recv_sem=recv_sem.at[k],
            device_id=dev(source),
            device_id_type=MESH,
        )
        copies[k - 1].wait_send()
        incoming.wait_recv()


class _Ring:
    def __init__(self, pos, n, device, slot, own, sems, on_arrival=None):
        self.pos, self.n, self.device, self.slot, self.own = pos, n, device, slot, own
        self.sems = sems
        self.on_arrival = on_arrival
        self.steps = n // 2
        self.split = n % 2 == 0
        self.copies = []
        self.next = 1

    def advance(self):
        if self.next <= self.steps:
            self.step(self.next)
            self.next += 1

    def _part(self, s, kind):
        return kind // 2 if self.split and s == self.steps else None

    def _origin(self, step, sign):
        return lax.rem(self.pos + sign * step + 2 * self.n, self.n)

    def _desc(self, src, origin, kind, s, target):
        return pltpu.make_async_remote_copy(
            src_ref=src, dst_ref=self.slot(origin, self._part(s, kind)),
            send_sem=self.sems.at[kind, s - 1], recv_sem=self.sems.at[kind + 1, s - 1],
            device_id=self.device(target), device_id_type=MESH,
        )

    def step(self, s):
        if s > self.steps:
            return
        for kind, sign in ((0, 1), (2, -1)):
            target = self._origin(1, sign)
            origin = self._origin(s - 1, -sign)
            part = self._part(s, kind)
            if s == 1:
                src = self.own(part)
            else:
                self._desc(self.slot(origin), origin, kind, s - 1, target).wait_recv()
                if self.on_arrival is not None:
                    self.on_arrival(origin)
                src = self.slot(origin, part)
            copy = self._desc(src, origin, kind, s, target)
            copy.start()
            self.copies.append(copy)

    def finish_recv(self):
        while self.next <= self.steps:
            self.advance()
        if not self.steps:
            return
        last = []
        for kind, sign in ((0, 1), (2, -1)):
            origin = self._origin(self.steps, -sign)
            view = self.slot(origin, self._part(self.steps, kind))
            self._desc(view, origin, kind, self.steps, self._origin(1, sign)).wait_recv()
            last.append(origin)
        if self.on_arrival is not None:
            for origin in last[:1] if self.split else last:
                self.on_arrival(origin)

    def finish_send(self):
        for copy in self.copies:
            copy.wait_send()


def _gather_kernel(n_x, n_z, n_y, rows_ref, head_ref, rows_out, head_out, local_sem, sems, pair_sems):
    me = lax.axis_index("grp")
    v = lax.axis_index("voc")
    x = me // n_z
    z = me % n_z
    y = v // 2
    c = v % 2
    partner = y * 2 + 1 - c
    half = head_ref.shape[0] // 2
    lo, hi = pl.ds(0, half), pl.ds(half, half)
    width = rows_ref.shape[1]

    def cols(t):
        return pl.ds(pl.multiple_of(t * width, width), width)

    def along_x(t):
        return (t * n_z + z, v)

    def along_z(t):
        return (x * n_z + t, v)

    def along_y(t):
        return (me, t * 2 + c)

    barrier = pltpu.get_barrier_semaphore()
    neighbours = [along_x(lax.rem(x + 1, n_x)), along_x(lax.rem(x + n_x - 1, n_x)),
                  along_z(lax.rem(z + 1, n_z)), along_z(lax.rem(z + n_z - 1, n_z)),
                  along_y(lax.rem(y + 1, n_y)), along_y(lax.rem(y + n_y - 1, n_y)),
                  (me, partner)]
    for target in neighbours:
        pl.semaphore_signal(barrier, inc=1, device_id=target, device_id_type=MESH)
    pl.semaphore_wait(barrier, len(neighbours))

    def to_partner(src, t):
        return pltpu.make_async_remote_copy(
            src_ref=src, dst_ref=rows_out.at[:, cols(t * 2 + c)],
            send_sem=pair_sems.at[0, t], recv_sem=pair_sems.at[1, t],
            device_id=(me, partner), device_id_type=MESH,
        )

    pair_copies = []

    def forward(t):
        copy = to_partner(rows_out.at[:, cols(t * 2 + c)], t)
        copy.start()
        pair_copies.append(copy)

    own = pltpu.make_async_copy(head_ref, head_out.at[x, z], local_sem.at[0])
    own.start()
    copy = to_partner(rows_ref, y)
    copy.start()
    pair_copies.append(copy)
    rows_out[:, cols(v)] = rows_ref[...]
    def halves(size, start=0):
        return lambda part: pl.ds(start, size) if part is None else pl.ds(start + part * (size // 2), size // 2)

    rows_part = halves(rows_ref.shape[0])
    lo_part, hi_part = halves(half), halves(half, half)
    x_part, z_part = halves(n_x), halves(n_z)
    rows = _Ring(y, n_y, along_y, lambda t, p=None: rows_out.at[rows_part(p), cols(t * 2 + c)],
                 lambda p: rows_ref.at[rows_part(p)], sems.at[4], forward)
    first_x = _Ring(x, n_x, along_x, lambda t, p=None: head_out.at[t, z, lo_part(p)],
                    lambda p: head_ref.at[lo_part(p)], sems.at[0])
    first_z = _Ring(z, n_z, along_z, lambda t, p=None: head_out.at[x, t, hi_part(p)],
                    lambda p: head_ref.at[hi_part(p)], sems.at[1])
    rows.advance()
    first_x.advance()
    first_z.advance()
    first_x.advance()
    first_z.advance()
    own.wait()
    first_x.finish_recv()
    second_z = _Ring(z, n_z, along_z, lambda t, p=None: head_out.at[x_part(p), t, lo],
                     lambda p: head_out.at[x_part(p), z, lo], sems.at[2])
    second_x = _Ring(x, n_x, along_x, lambda t, p=None: head_out.at[t, z_part(p), hi],
                     lambda p: head_out.at[x, z_part(p), hi], sems.at[3])
    second_z.advance()
    first_z.advance()
    rows.advance()
    first_z.advance()
    first_z.finish_recv()
    second_x.advance()
    rows.advance()
    second_z.advance()
    rows.advance()
    second_z.advance()
    rows.finish_recv()
    second_x.advance()
    second_z.advance()
    second_z.finish_recv()
    second_x.finish_recv()
    for t in range(n_y):
        other = t * 2 + 1 - c
        block = rows_out.at[:, cols(other)]
        pltpu.make_async_remote_copy(
            src_ref=block, dst_ref=block,
            send_sem=pair_sems.at[0, t], recv_sem=pair_sems.at[1, t],
            device_id=(me, partner), device_id_type=MESH,
        ).wait_recv()
    for ring in (first_x, first_z, second_z, second_x, rows):
        ring.finish_send()
    for copy in pair_copies:
        copy.wait_send()


def gather_both(hidden, piece, n_x, n_z, n_voc):
    rows, width = hidden.shape
    depth, vocab = piece.shape
    n_y = n_voc // 2
    steps = max(n_x, n_z, n_y)
    full_rows, full_head = pl.pallas_call(
        functools.partial(_gather_kernel, n_x, n_z, n_y),
        out_shape=(jax.ShapeDtypeStruct((rows, width * n_voc), hidden.dtype),
                   jax.ShapeDtypeStruct((n_x, n_z, depth, vocab), piece.dtype)),
        in_specs=[pl.BlockSpec(memory_space=pltpu.VMEM)] * 2,
        out_specs=(pl.BlockSpec(memory_space=pltpu.VMEM), pl.BlockSpec(memory_space=pltpu.VMEM)),
        scratch_shapes=[pltpu.SemaphoreType.DMA((1,)), pltpu.SemaphoreType.DMA((5, 4, steps)),
                        pltpu.SemaphoreType.DMA((2, n_y))],
        compiler_params=pltpu.CompilerParams(collective_id=3, has_side_effects=True),
    )(hidden, piece)
    return full_rows, full_head.reshape(n_x * n_z * depth, vocab)


def share(block, axis, other, n, collective_id):
    return pl.pallas_call(
        functools.partial(_share_kernel, axis, other, n),
        out_shape=jax.ShapeDtypeStruct((n,) + block.shape, block.dtype),
        in_specs=[pl.BlockSpec(memory_space=pltpu.VMEM)],
        out_specs=pl.BlockSpec(memory_space=pltpu.VMEM),
        scratch_shapes=[pltpu.SemaphoreType.DMA((n,)), pltpu.SemaphoreType.DMA((n,))],
        compiler_params=pltpu.CompilerParams(collective_id=collective_id, has_side_effects=True),
    )(block)


def local(hidden, targets, row_count, norm_gain, head_weight, return_from, *, n_voc, n_grp, n_x, n_z):
    tok_rows = hidden.shape[0]
    positions = jnp.arange(tok_rows, dtype=jnp.int32)
    live_rows = positions < row_count[0]
    full_rows, piece = gather_both(hidden, head_weight, n_x, n_z, n_voc)
    normed = normalize(full_rows, norm_gain)
    vocab_local = head_weight.shape[1]
    logits = jnp.dot(normed, piece, preferred_element_type=jnp.float32)
    peak = jnp.max(logits, axis=1)
    shifted = jnp.exp(logits - peak[:, None])
    total = jnp.sum(shifted, axis=1)
    weighted = jnp.sum(shifted * logits, axis=1)
    global_columns = lax.axis_index("voc") * vocab_local + jnp.arange(vocab_local, dtype=jnp.int32)
    picked = jnp.sum(jnp.where(global_columns[None, :] == targets[:, None], logits, 0.0), axis=1)
    stats = jnp.concatenate([peak, total, weighted, picked]).reshape(8, -1)
    parts = share(stats, "voc", "grp", n_voc, 0).reshape(n_voc, 4, tok_rows)
    peaks, totals, weights, picks = parts[:, 0], parts[:, 1], parts[:, 2], parts[:, 3]
    peak_all = jnp.max(peaks, axis=0)
    factor = jnp.exp(peaks - peak_all[None, :])
    total_all = jnp.sum(totals * factor, axis=0)
    weighted_all = jnp.sum(weights * factor, axis=0)
    picked_all = jnp.sum(picks, axis=0)
    log_total = peak_all + jnp.log(total_all)
    logp = jnp.where(live_rows, picked_all - log_total, 0.0)
    entropy = jnp.where(live_rows, log_total - weighted_all / total_all, 0.0)
    both = jnp.concatenate([logp, entropy]).reshape(-1, 128)
    results = share(both, "grp", "voc", n_grp, 1).reshape(n_grp, 2, tok_rows)
    lanes = 128
    every = jnp.concatenate(
        [results[:, 0].reshape(-1, lanes), results[:, 1].reshape(-1, lanes)], axis=1)
    high = return_from // lanes
    low = return_from % lanes
    pick_row = (high[:, None] == jnp.arange(every.shape[0], dtype=jnp.int32)[None, :]).astype(jnp.float32)
    rows_picked = jnp.dot(pick_row, every, precision=lax.Precision.HIGHEST)
    pick_lane = low[:, None] == jnp.arange(lanes, dtype=jnp.int32)[None, :]
    token_logp = jnp.sum(jnp.where(pick_lane, rows_picked[:, :lanes], 0.0), axis=1)
    token_entropy = jnp.sum(jnp.where(pick_lane, rows_picked[:, lanes:], 0.0), axis=1)
    return (token_logp, token_entropy)


def solution(mesh):
    placed = (P("grp", "voc"), P("grp"), P("grp"), P(), P("grp", "voc"), P("grp"))
    n_grp = mesh.shape["grp"]
    n_z = len({device.coords[2] for device in mesh.devices[:, 0]})
    body = functools.partial(local, n_voc=mesh.shape["voc"], n_grp=n_grp, n_x=n_grp // n_z, n_z=n_z)
    return jax.shard_map(
        body, mesh=mesh, in_specs=placed, out_specs=(P("grp"), P("grp")), check_vma=False
    )
```

```python
import functools

import jax
import jax.numpy as jnp
from jax import lax
from jax.experimental import pallas as pl
from jax.experimental.pallas import tpu as pltpu
from jax.sharding import PartitionSpec as P

MESH = pl.DeviceIdType.MESH

EPSILON = 1e-05


def normalize(raw, norm_gain):
    values = raw.astype(jnp.float32)
    scale = lax.rsqrt(jnp.mean(values * values, axis=1, keepdims=True) + EPSILON)
    return (values * scale * norm_gain.astype(jnp.float32)[None, :]).astype(jnp.bfloat16)


def _exchange_kernel(n_voc, n_grp, stats_ref, live_ref, out_ref, parts, voc_sems, grp_sems):
    g = lax.axis_index("grp")
    v = lax.axis_index("voc")

    def along_voc(t):
        return (g, t)

    def along_grp(t):
        return (t, v)

    barrier = pltpu.get_barrier_semaphore()
    for k in range(1, n_voc):
        pl.semaphore_signal(barrier, inc=1, device_id=along_voc(lax.rem(v + k, n_voc)), device_id_type=MESH)
    for k in range(1, n_grp):
        pl.semaphore_signal(barrier, inc=1, device_id=along_grp(lax.rem(g + k, n_grp)), device_id_type=MESH)
    pl.semaphore_wait(barrier, n_voc + n_grp - 2)

    def send_all(src, buffer, me, n, sems, device, fill):
        copies = []
        for k in range(1, n):
            copy = pltpu.make_async_remote_copy(
                src_ref=src, dst_ref=buffer.at[me],
                send_sem=sems.at[0, k], recv_sem=sems.at[1, k],
                device_id=device(lax.rem(me + k, n)), device_id_type=MESH,
            )
            copy.start()
            copies.append(copy)
        fill()
        for k in range(1, n):
            source = lax.rem(me + n - k, n)
            pltpu.make_async_remote_copy(
                src_ref=src, dst_ref=buffer.at[source],
                send_sem=sems.at[0, k], recv_sem=sems.at[1, k],
                device_id=device(source), device_id_type=MESH,
            ).wait_recv()
        for copy in copies:
            copy.wait_send()

    def keep_stats():
        parts[v] = stats_ref[...]

    send_all(stats_ref, parts, v, n_voc, voc_sems, along_voc, keep_stats)
    every = parts[...]
    quarter = every.shape[1] // 4
    peaks = every[:, :quarter]
    peak = jnp.max(peaks, axis=0)
    factor = jnp.exp(peaks - peak[None])
    total = jnp.sum(every[:, quarter:2 * quarter] * factor, axis=0)
    weighted = jnp.sum(every[:, 2 * quarter:3 * quarter] * factor, axis=0)
    picked = jnp.sum(every[:, 3 * quarter:], axis=0)
    log_total = peak + jnp.log(total)
    live = live_ref[...] > 0.0
    out_ref[g, :quarter] = jnp.where(live, picked - log_total, 0.0)
    out_ref[g, quarter:] = jnp.where(live, log_total - weighted / total, 0.0)
    send_all(out_ref.at[g], out_ref, g, n_grp, grp_sems, along_grp, lambda: None)


def exchange(stats, live, n_voc, n_grp):
    rows, lanes = stats.shape
    return pl.pallas_call(
        functools.partial(_exchange_kernel, n_voc, n_grp),
        out_shape=jax.ShapeDtypeStruct((n_grp, rows // 2, lanes), stats.dtype),
        in_specs=[pl.BlockSpec(memory_space=pltpu.VMEM)] * 2,
        out_specs=pl.BlockSpec(memory_space=pltpu.VMEM),
        scratch_shapes=[pltpu.VMEM((n_voc, rows, lanes), stats.dtype),
                        pltpu.SemaphoreType.DMA((2, n_voc)), pltpu.SemaphoreType.DMA((2, n_grp))],
        compiler_params=pltpu.CompilerParams(collective_id=0, has_side_effects=True),
    )(stats, live)


class _Ring:
    def __init__(self, pos, n, device, slot, own, sems, on_arrival=None):
        self.pos, self.n, self.device, self.slot, self.own = pos, n, device, slot, own
        self.sems = sems
        self.on_arrival = on_arrival
        self.steps = n // 2
        self.split = n % 2 == 0
        self.copies = []
        self.next = 1

    def advance(self):
        if self.next <= self.steps:
            self.step(self.next)
            self.next += 1

    def _part(self, s, kind):
        return kind // 2 if self.split and s == self.steps else None

    def _origin(self, step, sign):
        return lax.rem(self.pos + sign * step + 2 * self.n, self.n)

    def _desc(self, src, origin, kind, s, target):
        return pltpu.make_async_remote_copy(
            src_ref=src, dst_ref=self.slot(origin, self._part(s, kind)),
            send_sem=self.sems.at[kind, s - 1], recv_sem=self.sems.at[kind + 1, s - 1],
            device_id=self.device(target), device_id_type=MESH,
        )

    def step(self, s):
        if s > self.steps:
            return
        for kind, sign in ((0, 1), (2, -1)):
            target = self._origin(1, sign)
            origin = self._origin(s - 1, -sign)
            part = self._part(s, kind)
            if s == 1:
                src = self.own(part)
            else:
                self._desc(self.slot(origin), origin, kind, s - 1, target).wait_recv()
                if self.on_arrival is not None:
                    self.on_arrival(origin)
                src = self.slot(origin, part)
            copy = self._desc(src, origin, kind, s, target)
            copy.start()
            self.copies.append(copy)

    def finish_recv(self):
        while self.next <= self.steps:
            self.advance()
        if not self.steps:
            return
        last = []
        for kind, sign in ((0, 1), (2, -1)):
            origin = self._origin(self.steps, -sign)
            view = self.slot(origin, self._part(self.steps, kind))
            self._desc(view, origin, kind, self.steps, self._origin(1, sign)).wait_recv()
            last.append(origin)
        if self.on_arrival is not None:
            for origin in last[:1] if self.split else last:
                self.on_arrival(origin)

    def finish_send(self):
        for copy in self.copies:
            copy.wait_send()


def _gather_kernel(n_x, n_z, n_y, rows_ref, head_ref, rows_out, head_out, local_sem, sems, pair_sems):
    me = lax.axis_index("grp")
    v = lax.axis_index("voc")
    x = me // n_z
    z = me % n_z
    y = v // 2
    c = v % 2
    partner = y * 2 + 1 - c
    half = head_ref.shape[0] // 2
    lo, hi = pl.ds(0, half), pl.ds(half, half)
    width = rows_ref.shape[1]

    def cols(t):
        return pl.ds(pl.multiple_of(t * width, width), width)

    def along_x(t):
        return (t * n_z + z, v)

    def along_z(t):
        return (x * n_z + t, v)

    def along_y(t):
        return (me, t * 2 + c)

    barrier = pltpu.get_barrier_semaphore()
    neighbours = [along_x(lax.rem(x + 1, n_x)), along_x(lax.rem(x + n_x - 1, n_x)),
                  along_z(lax.rem(z + 1, n_z)), along_z(lax.rem(z + n_z - 1, n_z)),
                  along_y(lax.rem(y + 1, n_y)), along_y(lax.rem(y + n_y - 1, n_y)),
                  (me, partner)]
    for target in neighbours:
        pl.semaphore_signal(barrier, inc=1, device_id=target, device_id_type=MESH)
    pl.semaphore_wait(barrier, len(neighbours))

    def to_partner(src, t):
        return pltpu.make_async_remote_copy(
            src_ref=src, dst_ref=rows_out.at[:, cols(t * 2 + c)],
            send_sem=pair_sems.at[0, t], recv_sem=pair_sems.at[1, t],
            device_id=(me, partner), device_id_type=MESH,
        )

    pair_copies = []

    def forward(t):
        copy = to_partner(rows_out.at[:, cols(t * 2 + c)], t)
        copy.start()
        pair_copies.append(copy)

    own = pltpu.make_async_copy(head_ref, head_out.at[x, z], local_sem.at[0])
    own.start()
    copy = to_partner(rows_ref, y)
    copy.start()
    pair_copies.append(copy)
    rows_out[:, cols(v)] = rows_ref[...]
    def halves(size, start=0):
        return lambda part: pl.ds(start, size) if part is None else pl.ds(start + part * (size // 2), size // 2)

    rows_part = halves(rows_ref.shape[0])
    lo_part, hi_part = halves(half), halves(half, half)
    x_part, z_part = halves(n_x), halves(n_z)
    rows = _Ring(y, n_y, along_y, lambda t, p=None: rows_out.at[rows_part(p), cols(t * 2 + c)],
                 lambda p: rows_ref.at[rows_part(p)], sems.at[4], forward)
    first_x = _Ring(x, n_x, along_x, lambda t, p=None: head_out.at[t, z, lo_part(p)],
                    lambda p: head_ref.at[lo_part(p)], sems.at[0])
    first_z = _Ring(z, n_z, along_z, lambda t, p=None: head_out.at[x, t, hi_part(p)],
                    lambda p: head_ref.at[hi_part(p)], sems.at[1])
    rows.advance()
    first_x.advance()
    first_z.advance()
    first_x.advance()
    first_z.advance()
    own.wait()
    first_x.finish_recv()
    second_z = _Ring(z, n_z, along_z, lambda t, p=None: head_out.at[x_part(p), t, lo],
                     lambda p: head_out.at[x_part(p), z, lo], sems.at[2])
    second_x = _Ring(x, n_x, along_x, lambda t, p=None: head_out.at[t, z_part(p), hi],
                     lambda p: head_out.at[x, z_part(p), hi], sems.at[3])
    second_z.advance()
    first_z.advance()
    rows.advance()
    first_z.advance()
    first_z.finish_recv()
    second_x.advance()
    rows.advance()
    second_z.advance()
    rows.advance()
    second_z.advance()
    rows.finish_recv()
    second_x.advance()
    second_z.advance()
    second_z.finish_recv()
    second_x.finish_recv()
    for t in range(n_y):
        other = t * 2 + 1 - c
        block = rows_out.at[:, cols(other)]
        pltpu.make_async_remote_copy(
            src_ref=block, dst_ref=block,
            send_sem=pair_sems.at[0, t], recv_sem=pair_sems.at[1, t],
            device_id=(me, partner), device_id_type=MESH,
        ).wait_recv()
    for ring in (first_x, first_z, second_z, second_x, rows):
        ring.finish_send()
    for copy in pair_copies:
        copy.wait_send()


def gather_both(hidden, piece, n_x, n_z, n_voc):
    rows, width = hidden.shape
    depth, vocab = piece.shape
    n_y = n_voc // 2
    steps = max(n_x, n_z, n_y)
    full_rows, full_head = pl.pallas_call(
        functools.partial(_gather_kernel, n_x, n_z, n_y),
        out_shape=(jax.ShapeDtypeStruct((rows, width * n_voc), hidden.dtype),
                   jax.ShapeDtypeStruct((n_x, n_z, depth, vocab), piece.dtype)),
        in_specs=[pl.BlockSpec(memory_space=pltpu.VMEM)] * 2,
        out_specs=(pl.BlockSpec(memory_space=pltpu.VMEM), pl.BlockSpec(memory_space=pltpu.VMEM)),
        scratch_shapes=[pltpu.SemaphoreType.DMA((1,)), pltpu.SemaphoreType.DMA((5, 4, steps)),
                        pltpu.SemaphoreType.DMA((2, n_y))],
        compiler_params=pltpu.CompilerParams(collective_id=3, has_side_effects=True),
    )(hidden, piece)
    return full_rows, full_head.reshape(n_x * n_z * depth, vocab)


def local(hidden, targets, row_count, norm_gain, head_weight, return_from, *, n_voc, n_grp, n_x, n_z):
    tok_rows = hidden.shape[0]
    positions = jnp.arange(tok_rows, dtype=jnp.int32)
    live_rows = positions < row_count[0]
    full_rows, piece = gather_both(hidden, head_weight, n_x, n_z, n_voc)
    normed = normalize(full_rows, norm_gain)
    vocab_local = head_weight.shape[1]
    logits = jnp.dot(normed, piece, preferred_element_type=jnp.float32)
    peak = jnp.max(logits, axis=1)
    shifted = jnp.exp(logits - peak[:, None])
    total = jnp.sum(shifted, axis=1)
    weighted = jnp.sum(shifted * logits, axis=1)
    global_columns = lax.axis_index("voc") * vocab_local + jnp.arange(vocab_local, dtype=jnp.int32)
    picked = jnp.sum(jnp.where(global_columns[None, :] == targets[:, None], logits, 0.0), axis=1)
    stats = jnp.concatenate([peak, total, weighted, picked]).reshape(8, -1)
    live = live_rows.astype(jnp.float32).reshape(2, -1)
    results = exchange(stats, live, n_voc, n_grp).reshape(n_grp, 2, tok_rows)
    lanes = 128
    every = jnp.concatenate(
        [results[:, 0].reshape(-1, lanes), results[:, 1].reshape(-1, lanes)], axis=1)
    high = return_from // lanes
    low = return_from % lanes
    pick_row = (high[:, None] == jnp.arange(every.shape[0], dtype=jnp.int32)[None, :]).astype(jnp.float32)
    rows_picked = jnp.dot(pick_row, every, precision=lax.Precision.HIGHEST)
    pick_lane = low[:, None] == jnp.arange(lanes, dtype=jnp.int32)[None, :]
    token_logp = jnp.sum(jnp.where(pick_lane, rows_picked[:, :lanes], 0.0), axis=1)
    token_entropy = jnp.sum(jnp.where(pick_lane, rows_picked[:, lanes:], 0.0), axis=1)
    return (token_logp, token_entropy)


def solution(mesh):
    placed = (P("grp", "voc"), P("grp"), P("grp"), P(), P("grp", "voc"), P("grp"))
    n_grp = mesh.shape["grp"]
    n_z = len({device.coords[2] for device in mesh.devices[:, 0]})
    body = functools.partial(local, n_voc=mesh.shape["voc"], n_grp=n_grp, n_x=n_grp // n_z, n_z=n_z)
    return jax.shard_map(
        body, mesh=mesh, in_specs=placed, out_specs=(P("grp"), P("grp")), check_vma=False
    )
```

```python
import functools

import jax
import jax.numpy as jnp
from jax import lax
from jax.experimental import pallas as pl
from jax.experimental.pallas import tpu as pltpu
from jax.sharding import PartitionSpec as P

MESH = pl.DeviceIdType.MESH

EPSILON = 1e-05


def _exchange_kernel(n_voc, n_grp, stats_ref, live_ref, out_ref, parts, voc_sems, grp_sems):
    g = lax.axis_index("grp")
    v = lax.axis_index("voc")

    def along_voc(t):
        return (g, t)

    def along_grp(t):
        return (t, v)

    barrier = pltpu.get_barrier_semaphore()
    for k in range(1, n_voc):
        pl.semaphore_signal(barrier, inc=1, device_id=along_voc(lax.rem(v + k, n_voc)), device_id_type=MESH)
    for k in range(1, n_grp):
        pl.semaphore_signal(barrier, inc=1, device_id=along_grp(lax.rem(g + k, n_grp)), device_id_type=MESH)
    pl.semaphore_wait(barrier, n_voc + n_grp - 2)

    def send_all(src, buffer, me, n, sems, device, fill):
        copies = []
        for k in range(1, n):
            copy = pltpu.make_async_remote_copy(
                src_ref=src, dst_ref=buffer.at[me],
                send_sem=sems.at[0, k], recv_sem=sems.at[1, k],
                device_id=device(lax.rem(me + k, n)), device_id_type=MESH,
            )
            copy.start()
            copies.append(copy)
        fill()
        for k in range(1, n):
            source = lax.rem(me + n - k, n)
            pltpu.make_async_remote_copy(
                src_ref=src, dst_ref=buffer.at[source],
                send_sem=sems.at[0, k], recv_sem=sems.at[1, k],
                device_id=device(source), device_id_type=MESH,
            ).wait_recv()
        for copy in copies:
            copy.wait_send()

    def keep_stats():
        parts[v] = stats_ref[...]

    send_all(stats_ref, parts, v, n_voc, voc_sems, along_voc, keep_stats)
    every = parts[...]
    quarter = every.shape[1] // 4
    peaks = every[:, :quarter]
    peak = jnp.max(peaks, axis=0)
    factor = jnp.exp(peaks - peak[None])
    total = jnp.sum(every[:, quarter:2 * quarter] * factor, axis=0)
    weighted = jnp.sum(every[:, 2 * quarter:3 * quarter] * factor, axis=0)
    picked = jnp.sum(every[:, 3 * quarter:], axis=0)
    log_total = peak + jnp.log(total)
    live = live_ref[...] > 0.0
    out_ref[g, :quarter] = jnp.where(live, picked - log_total, 0.0)
    out_ref[g, quarter:] = jnp.where(live, log_total - weighted / total, 0.0)
    send_all(out_ref.at[g], out_ref, g, n_grp, grp_sems, along_grp, lambda: None)


def exchange(stats, live, n_voc, n_grp):
    rows, lanes = stats.shape
    return pl.pallas_call(
        functools.partial(_exchange_kernel, n_voc, n_grp),
        out_shape=jax.ShapeDtypeStruct((n_grp, rows // 2, lanes), stats.dtype),
        in_specs=[pl.BlockSpec(memory_space=pltpu.VMEM)] * 2,
        out_specs=pl.BlockSpec(memory_space=pltpu.VMEM),
        scratch_shapes=[pltpu.VMEM((n_voc, rows, lanes), stats.dtype),
                        pltpu.SemaphoreType.DMA((2, n_voc)), pltpu.SemaphoreType.DMA((2, n_grp))],
        compiler_params=pltpu.CompilerParams(collective_id=0, has_side_effects=True),
    )(stats, live)


class _Ring:
    def __init__(self, pos, n, device, slot, own, sems, on_arrival=None):
        self.pos, self.n, self.device, self.slot, self.own = pos, n, device, slot, own
        self.sems = sems
        self.on_arrival = on_arrival
        self.steps = n // 2
        self.split = n % 2 == 0
        self.copies = []
        self.next = 1

    def advance(self):
        if self.next <= self.steps:
            self.step(self.next)
            self.next += 1

    def _part(self, s, kind):
        return kind // 2 if self.split and s == self.steps else None

    def _origin(self, step, sign):
        return lax.rem(self.pos + sign * step + 2 * self.n, self.n)

    def _desc(self, src, origin, kind, s, target):
        return pltpu.make_async_remote_copy(
            src_ref=src, dst_ref=self.slot(origin, self._part(s, kind)),
            send_sem=self.sems.at[kind, s - 1], recv_sem=self.sems.at[kind + 1, s - 1],
            device_id=self.device(target), device_id_type=MESH,
        )

    def step(self, s):
        if s > self.steps:
            return
        for kind, sign in ((0, 1), (2, -1)):
            target = self._origin(1, sign)
            origin = self._origin(s - 1, -sign)
            part = self._part(s, kind)
            if s == 1:
                src = self.own(part)
            else:
                self._desc(self.slot(origin), origin, kind, s - 1, target).wait_recv()
                if self.on_arrival is not None:
                    self.on_arrival(origin)
                src = self.slot(origin, part)
            copy = self._desc(src, origin, kind, s, target)
            copy.start()
            self.copies.append(copy)

    def finish_recv(self):
        while self.next <= self.steps:
            self.advance()
        if not self.steps:
            return
        last = []
        for kind, sign in ((0, 1), (2, -1)):
            origin = self._origin(self.steps, -sign)
            view = self.slot(origin, self._part(self.steps, kind))
            self._desc(view, origin, kind, self.steps, self._origin(1, sign)).wait_recv()
            last.append(origin)
        if self.on_arrival is not None:
            for origin in last[:1] if self.split else last:
                self.on_arrival(origin)

    def finish_send(self):
        for copy in self.copies:
            copy.wait_send()


def _gather_kernel(n_x, n_z, n_y, rows_ref, head_ref, gain_ref, normed_out, head_out, rows_out,
                   local_sem, sems, pair_sems):
    me = lax.axis_index("grp")
    v = lax.axis_index("voc")
    x = me // n_z
    z = me % n_z
    y = v // 2
    c = v % 2
    partner = y * 2 + 1 - c
    half = head_ref.shape[0] // 2
    lo, hi = pl.ds(0, half), pl.ds(half, half)
    width = rows_ref.shape[1]

    def cols(t):
        return pl.ds(pl.multiple_of(t * width, width), width)

    def along_x(t):
        return (t * n_z + z, v)

    def along_z(t):
        return (x * n_z + t, v)

    def along_y(t):
        return (me, t * 2 + c)

    barrier = pltpu.get_barrier_semaphore()
    neighbours = [along_x(lax.rem(x + 1, n_x)), along_x(lax.rem(x + n_x - 1, n_x)),
                  along_z(lax.rem(z + 1, n_z)), along_z(lax.rem(z + n_z - 1, n_z)),
                  along_y(lax.rem(y + 1, n_y)), along_y(lax.rem(y + n_y - 1, n_y)),
                  (me, partner)]
    for target in neighbours:
        pl.semaphore_signal(barrier, inc=1, device_id=target, device_id_type=MESH)
    pl.semaphore_wait(barrier, len(neighbours))

    def to_partner(src, t):
        return pltpu.make_async_remote_copy(
            src_ref=src, dst_ref=rows_out.at[:, cols(t * 2 + c)],
            send_sem=pair_sems.at[0, t], recv_sem=pair_sems.at[1, t],
            device_id=(me, partner), device_id_type=MESH,
        )

    pair_copies = []

    def forward(t):
        copy = to_partner(rows_out.at[:, cols(t * 2 + c)], t)
        copy.start()
        pair_copies.append(copy)

    own = pltpu.make_async_copy(head_ref, head_out.at[x, z], local_sem.at[0])
    own.start()
    copy = to_partner(rows_ref, y)
    copy.start()
    pair_copies.append(copy)
    rows_out[:, cols(v)] = rows_ref[...]
    def halves(size, start=0):
        return lambda part: pl.ds(start, size) if part is None else pl.ds(start + part * (size // 2), size // 2)

    rows_part = halves(rows_ref.shape[0])
    lo_part, hi_part = halves(half), halves(half, half)
    x_part, z_part = halves(n_x), halves(n_z)
    rows = _Ring(y, n_y, along_y, lambda t, p=None: rows_out.at[rows_part(p), cols(t * 2 + c)],
                 lambda p: rows_ref.at[rows_part(p)], sems.at[4], forward)
    first_x = _Ring(x, n_x, along_x, lambda t, p=None: head_out.at[t, z, lo_part(p)],
                    lambda p: head_ref.at[lo_part(p)], sems.at[0])
    first_z = _Ring(z, n_z, along_z, lambda t, p=None: head_out.at[x, t, hi_part(p)],
                    lambda p: head_ref.at[hi_part(p)], sems.at[1])
    rows.advance()
    first_x.advance()
    first_z.advance()
    first_x.advance()
    first_z.advance()
    own.wait()
    first_x.finish_recv()
    second_z = _Ring(z, n_z, along_z, lambda t, p=None: head_out.at[x_part(p), t, lo],
                     lambda p: head_out.at[x_part(p), z, lo], sems.at[2])
    second_x = _Ring(x, n_x, along_x, lambda t, p=None: head_out.at[t, z_part(p), hi],
                     lambda p: head_out.at[x, z_part(p), hi], sems.at[3])
    second_z.advance()
    first_z.advance()
    rows.advance()
    first_z.advance()
    first_z.finish_recv()
    second_x.advance()
    rows.advance()
    second_z.advance()
    rows.advance()
    second_z.advance()
    rows.finish_recv()
    second_x.advance()
    second_z.advance()
    for t in range(n_y):
        other = t * 2 + 1 - c
        block = rows_out.at[:, cols(other)]
        pltpu.make_async_remote_copy(
            src_ref=block, dst_ref=block,
            send_sem=pair_sems.at[0, t], recv_sem=pair_sems.at[1, t],
            device_id=(me, partner), device_id_type=MESH,
        ).wait_recv()
    chunk = 64

    def norm_chunk(i, carry):
        start = pl.multiple_of(i * chunk, chunk)
        values = rows_out[pl.ds(start, chunk), :].astype(jnp.float32)
        scale = lax.rsqrt(jnp.mean(values * values, axis=1, keepdims=True) + EPSILON)
        normed_out[pl.ds(start, chunk), :] = (values * scale * gain_ref[...]).astype(normed_out.dtype)
        return carry

    lax.fori_loop(0, rows_out.shape[0] // chunk, norm_chunk, 0)
    second_z.finish_recv()
    second_x.finish_recv()
    for ring in (first_x, first_z, second_z, second_x, rows):
        ring.finish_send()
    for copy in pair_copies:
        copy.wait_send()


def gather_both(hidden, piece, norm_gain, n_x, n_z, n_voc):
    rows, width = hidden.shape
    depth, vocab = piece.shape
    n_y = n_voc // 2
    steps = max(n_x, n_z, n_y)
    gain = norm_gain.astype(jnp.float32)[None, :]
    full_rows, full_head = pl.pallas_call(
        functools.partial(_gather_kernel, n_x, n_z, n_y),
        out_shape=(jax.ShapeDtypeStruct((rows, width * n_voc), hidden.dtype),
                   jax.ShapeDtypeStruct((n_x, n_z, depth, vocab), piece.dtype)),
        in_specs=[pl.BlockSpec(memory_space=pltpu.VMEM)] * 3,
        out_specs=(pl.BlockSpec(memory_space=pltpu.VMEM), pl.BlockSpec(memory_space=pltpu.VMEM)),
        scratch_shapes=[pltpu.VMEM((rows, width * n_voc), hidden.dtype),
                        pltpu.SemaphoreType.DMA((1,)), pltpu.SemaphoreType.DMA((5, 4, steps)),
                        pltpu.SemaphoreType.DMA((2, n_y))],
        compiler_params=pltpu.CompilerParams(collective_id=3, has_side_effects=True),
    )(hidden, piece, gain)
    return full_rows, full_head.reshape(n_x * n_z * depth, vocab)


def local(hidden, targets, row_count, norm_gain, head_weight, return_from, *, n_voc, n_grp, n_x, n_z):
    tok_rows = hidden.shape[0]
    positions = jnp.arange(tok_rows, dtype=jnp.int32)
    live_rows = positions < row_count[0]
    normed, piece = gather_both(hidden, head_weight, norm_gain, n_x, n_z, n_voc)
    vocab_local = head_weight.shape[1]
    logits = jnp.dot(normed, piece, preferred_element_type=jnp.float32)
    peak = jnp.max(logits, axis=1)
    shifted = jnp.exp(logits - peak[:, None])
    total = jnp.sum(shifted, axis=1)
    weighted = jnp.sum(shifted * logits, axis=1)
    global_columns = lax.axis_index("voc") * vocab_local + jnp.arange(vocab_local, dtype=jnp.int32)
    picked = jnp.sum(jnp.where(global_columns[None, :] == targets[:, None], logits, 0.0), axis=1)
    stats = jnp.concatenate([peak, total, weighted, picked]).reshape(8, -1)
    live = live_rows.astype(jnp.float32).reshape(2, -1)
    results = exchange(stats, live, n_voc, n_grp).reshape(n_grp, 2, tok_rows)
    lanes = 128
    every = jnp.concatenate(
        [results[:, 0].reshape(-1, lanes), results[:, 1].reshape(-1, lanes)], axis=1)
    high = return_from // lanes
    low = return_from % lanes
    pick_row = (high[:, None] == jnp.arange(every.shape[0], dtype=jnp.int32)[None, :]).astype(jnp.float32)
    rows_picked = jnp.dot(pick_row, every, precision=lax.Precision.HIGHEST)
    pick_lane = low[:, None] == jnp.arange(lanes, dtype=jnp.int32)[None, :]
    token_logp = jnp.sum(jnp.where(pick_lane, rows_picked[:, :lanes], 0.0), axis=1)
    token_entropy = jnp.sum(jnp.where(pick_lane, rows_picked[:, lanes:], 0.0), axis=1)
    return (token_logp, token_entropy)


def solution(mesh):
    placed = (P("grp", "voc"), P("grp"), P("grp"), P(), P("grp", "voc"), P("grp"))
    n_grp = mesh.shape["grp"]
    n_z = len({device.coords[2] for device in mesh.devices[:, 0]})
    body = functools.partial(local, n_voc=mesh.shape["voc"], n_grp=n_grp, n_x=n_grp // n_z, n_z=n_z)
    return jax.shard_map(
        body, mesh=mesh, in_specs=placed, out_specs=(P("grp"), P("grp")), check_vma=False
    )
```

```python
import functools

import jax
import jax.numpy as jnp
from jax import lax
from jax.experimental import pallas as pl
from jax.experimental.pallas import tpu as pltpu
from jax.sharding import PartitionSpec as P

MESH = pl.DeviceIdType.MESH

EPSILON = 1e-05


def _exchange_kernel(n_voc, n_grp, stats_ref, live_ref, out_ref, parts, voc_sems, grp_sems):
    g = lax.axis_index("grp")
    v = lax.axis_index("voc")

    def along_voc(t):
        return (g, t)

    def along_grp(t):
        return (t, v)

    barrier = pltpu.get_barrier_semaphore()
    for k in range(1, n_voc):
        pl.semaphore_signal(barrier, inc=1, device_id=along_voc(lax.rem(v + k, n_voc)), device_id_type=MESH)
    for k in range(1, n_grp):
        pl.semaphore_signal(barrier, inc=1, device_id=along_grp(lax.rem(g + k, n_grp)), device_id_type=MESH)
    pl.semaphore_wait(barrier, n_voc + n_grp - 2)

    def send_all(src, buffer, me, n, sems, device, fill):
        copies = []
        for k in range(1, n):
            copy = pltpu.make_async_remote_copy(
                src_ref=src, dst_ref=buffer.at[me],
                send_sem=sems.at[0, k], recv_sem=sems.at[1, k],
                device_id=device(lax.rem(me + k, n)), device_id_type=MESH,
            )
            copy.start()
            copies.append(copy)
        fill()
        for k in range(1, n):
            source = lax.rem(me + n - k, n)
            pltpu.make_async_remote_copy(
                src_ref=src, dst_ref=buffer.at[source],
                send_sem=sems.at[0, k], recv_sem=sems.at[1, k],
                device_id=device(source), device_id_type=MESH,
            ).wait_recv()
        for copy in copies:
            copy.wait_send()

    def keep_stats():
        parts[v] = stats_ref[...]

    send_all(stats_ref, parts, v, n_voc, voc_sems, along_voc, keep_stats)
    every = parts[...]
    quarter = every.shape[1] // 4
    peaks = every[:, :quarter]
    peak = jnp.max(peaks, axis=0)
    factor = jnp.exp(peaks - peak[None])
    total = jnp.sum(every[:, quarter:2 * quarter] * factor, axis=0)
    weighted = jnp.sum(every[:, 2 * quarter:3 * quarter] * factor, axis=0)
    picked = jnp.sum(every[:, 3 * quarter:], axis=0)
    log_total = peak + jnp.log(total)
    live = live_ref[...] > 0.0
    out_ref[g, :quarter] = jnp.where(live, picked - log_total, 0.0)
    out_ref[g, quarter:] = jnp.where(live, log_total - weighted / total, 0.0)
    send_all(out_ref.at[g], out_ref, g, n_grp, grp_sems, along_grp, lambda: None)


def exchange(stats, live, n_voc, n_grp):
    rows, lanes = stats.shape
    return pl.pallas_call(
        functools.partial(_exchange_kernel, n_voc, n_grp),
        out_shape=jax.ShapeDtypeStruct((n_grp, rows // 2, lanes), stats.dtype),
        in_specs=[pl.BlockSpec(memory_space=pltpu.VMEM)] * 2,
        out_specs=pl.BlockSpec(memory_space=pltpu.VMEM),
        scratch_shapes=[pltpu.VMEM((n_voc, rows, lanes), stats.dtype),
                        pltpu.SemaphoreType.DMA((2, n_voc)), pltpu.SemaphoreType.DMA((2, n_grp))],
        compiler_params=pltpu.CompilerParams(collective_id=0, has_side_effects=True),
    )(stats, live)


class _Ring:
    def __init__(self, pos, n, device, slot, own, sems, on_arrival=None):
        self.pos, self.n, self.device, self.slot, self.own = pos, n, device, slot, own
        self.sems = sems
        self.on_arrival = on_arrival
        self.steps = n // 2
        self.split = n % 2 == 0
        self.copies = []
        self.next = 1

    def advance(self):
        if self.next <= self.steps:
            self.step(self.next)
            self.next += 1

    def _part(self, s, kind):
        return kind // 2 if self.split and s == self.steps else None

    def _origin(self, step, sign):
        return lax.rem(self.pos + sign * step + 2 * self.n, self.n)

    def _desc(self, src, origin, kind, s, target):
        return pltpu.make_async_remote_copy(
            src_ref=src, dst_ref=self.slot(origin, self._part(s, kind)),
            send_sem=self.sems.at[kind, s - 1], recv_sem=self.sems.at[kind + 1, s - 1],
            device_id=self.device(target), device_id_type=MESH,
        )

    def step(self, s):
        if s > self.steps:
            return
        for kind, sign in ((0, 1), (2, -1)):
            target = self._origin(1, sign)
            origin = self._origin(s - 1, -sign)
            part = self._part(s, kind)
            if s == 1:
                src = self.own(part)
            else:
                self._desc(self.slot(origin), origin, kind, s - 1, target).wait_recv()
                if self.on_arrival is not None:
                    self.on_arrival(origin)
                src = self.slot(origin, part)
            copy = self._desc(src, origin, kind, s, target)
            copy.start()
            self.copies.append(copy)

    def finish_recv(self):
        while self.next <= self.steps:
            self.advance()
        if not self.steps:
            return
        last = []
        for kind, sign in ((0, 1), (2, -1)):
            origin = self._origin(self.steps, -sign)
            view = self.slot(origin, self._part(self.steps, kind))
            self._desc(view, origin, kind, self.steps, self._origin(1, sign)).wait_recv()
            last.append(origin)
        if self.on_arrival is not None:
            for origin in last[:1] if self.split else last:
                self.on_arrival(origin)

    def finish_send(self):
        for copy in self.copies:
            copy.wait_send()


def _gather_kernel(n_x, n_z, n_y, rows_ref, head_ref, gain_ref, normed_out, head_out, rows_out,
                   local_sem, sems, pair_sems):
    me = lax.axis_index("grp")
    v = lax.axis_index("voc")
    x = me // n_z
    z = me % n_z
    y = v // 2
    c = v % 2
    partner = y * 2 + 1 - c
    half = head_ref.shape[0] // 2
    lo, hi = pl.ds(0, half), pl.ds(half, half)
    width = rows_ref.shape[1]

    def cols(t):
        return pl.ds(pl.multiple_of(t * width, width), width)

    def along_x(t):
        return (t * n_z + z, v)

    def along_z(t):
        return (x * n_z + t, v)

    def along_y(t):
        return (me, t * 2 + c)

    barrier = pltpu.get_barrier_semaphore()
    neighbours = [along_x(lax.rem(x + 1, n_x)), along_x(lax.rem(x + n_x - 1, n_x)),
                  along_z(lax.rem(z + 1, n_z)), along_z(lax.rem(z + n_z - 1, n_z)),
                  along_y(lax.rem(y + 1, n_y)), along_y(lax.rem(y + n_y - 1, n_y)),
                  (me, partner)]
    for target in neighbours:
        pl.semaphore_signal(barrier, inc=1, device_id=target, device_id_type=MESH)
    pl.semaphore_wait(barrier, len(neighbours))

    def to_partner(src, t):
        return pltpu.make_async_remote_copy(
            src_ref=src, dst_ref=rows_out.at[:, cols(t * 2 + c)],
            send_sem=pair_sems.at[0, t], recv_sem=pair_sems.at[1, t],
            device_id=(me, partner), device_id_type=MESH,
        )

    pair_copies = []

    def forward(t):
        copy = to_partner(rows_out.at[:, cols(t * 2 + c)], t)
        copy.start()
        pair_copies.append(copy)

    own = pltpu.make_async_copy(head_ref, head_out.at[x, z], local_sem.at[0])
    own.start()
    copy = to_partner(rows_ref, y)
    copy.start()
    pair_copies.append(copy)
    rows_out[:, cols(v)] = rows_ref[...]
    def halves(size, start=0):
        return lambda part: pl.ds(start, size) if part is None else pl.ds(start + part * (size // 2), size // 2)

    rows_part = halves(rows_ref.shape[0])
    lo_part, hi_part = halves(half), halves(half, half)
    x_part, z_part = halves(n_x), halves(n_z)
    rows = _Ring(y, n_y, along_y, lambda t, p=None: rows_out.at[rows_part(p), cols(t * 2 + c)],
                 lambda p: rows_ref.at[rows_part(p)], sems.at[4], forward)
    first_x = _Ring(x, n_x, along_x, lambda t, p=None: head_out.at[t, z, lo_part(p)],
                    lambda p: head_ref.at[lo_part(p)], sems.at[0])
    first_z = _Ring(z, n_z, along_z, lambda t, p=None: head_out.at[x, t, hi_part(p)],
                    lambda p: head_ref.at[hi_part(p)], sems.at[1])
    rows.advance()
    first_x.advance()
    first_z.advance()
    first_x.advance()
    first_z.advance()
    own.wait()
    first_x.finish_recv()
    second_z = _Ring(z, n_z, along_z, lambda t, p=None: head_out.at[x_part(p), t, lo],
                     lambda p: head_out.at[x_part(p), z, lo], sems.at[2])
    second_x = _Ring(x, n_x, along_x, lambda t, p=None: head_out.at[t, z_part(p), hi],
                     lambda p: head_out.at[x, z_part(p), hi], sems.at[3])
    second_z.advance()
    first_z.advance()
    rows.advance()
    first_z.advance()
    first_z.finish_recv()
    second_x.advance()
    rows.advance()
    second_z.advance()
    rows.advance()
    second_z.advance()
    rows.finish_recv()
    second_x.advance()
    second_z.advance()
    for t in range(n_y):
        other = t * 2 + 1 - c
        block = rows_out.at[:, cols(other)]
        pltpu.make_async_remote_copy(
            src_ref=block, dst_ref=block,
            send_sem=pair_sems.at[0, t], recv_sem=pair_sems.at[1, t],
            device_id=(me, partner), device_id_type=MESH,
        ).wait_recv()
    chunk = 64

    def norm_chunk(i, carry):
        start = pl.multiple_of(i * chunk, chunk)
        values = rows_out[pl.ds(start, chunk), :].astype(jnp.float32)
        scale = lax.rsqrt(jnp.mean(values * values, axis=1, keepdims=True) + EPSILON)
        gain = gain_ref[...].astype(jnp.float32)
        normed_out[pl.ds(start, chunk), :] = (values * scale * gain).astype(normed_out.dtype)
        return carry

    lax.fori_loop(0, rows_out.shape[0] // chunk, norm_chunk, 0)
    second_z.finish_recv()
    second_x.finish_recv()
    for ring in (first_x, first_z, second_z, second_x, rows):
        ring.finish_send()
    for copy in pair_copies:
        copy.wait_send()


def gather_both(hidden, piece, norm_gain, n_x, n_z, n_voc):
    rows, width = hidden.shape
    depth, vocab = piece.shape
    n_y = n_voc // 2
    steps = max(n_x, n_z, n_y)
    gain = norm_gain.reshape(1, -1)
    full_rows, full_head = pl.pallas_call(
        functools.partial(_gather_kernel, n_x, n_z, n_y),
        out_shape=(jax.ShapeDtypeStruct((rows, width * n_voc), hidden.dtype),
                   jax.ShapeDtypeStruct((n_x, n_z, depth, vocab), piece.dtype)),
        in_specs=[pl.BlockSpec(memory_space=pltpu.VMEM)] * 3,
        out_specs=(pl.BlockSpec(memory_space=pltpu.VMEM), pl.BlockSpec(memory_space=pltpu.VMEM)),
        scratch_shapes=[pltpu.VMEM((rows, width * n_voc), hidden.dtype),
                        pltpu.SemaphoreType.DMA((1,)), pltpu.SemaphoreType.DMA((5, 4, steps)),
                        pltpu.SemaphoreType.DMA((2, n_y))],
        compiler_params=pltpu.CompilerParams(collective_id=3, has_side_effects=True),
    )(hidden, piece, gain)
    return full_rows, full_head.reshape(n_x * n_z * depth, vocab)


def local(hidden, targets, row_count, norm_gain, head_weight, return_from, *, n_voc, n_grp, n_x, n_z):
    tok_rows = hidden.shape[0]
    positions = jnp.arange(tok_rows, dtype=jnp.int32)
    live_rows = positions < row_count[0]
    normed, piece = gather_both(hidden, head_weight, norm_gain, n_x, n_z, n_voc)
    vocab_local = head_weight.shape[1]
    logits = jnp.dot(normed, piece, preferred_element_type=jnp.float32)
    peak = jnp.max(logits, axis=1)
    shifted = jnp.exp(logits - peak[:, None])
    total = jnp.sum(shifted, axis=1)
    weighted = jnp.sum(shifted * logits, axis=1)
    global_columns = lax.axis_index("voc") * vocab_local + jnp.arange(vocab_local, dtype=jnp.int32)
    picked = jnp.sum(jnp.where(global_columns[None, :] == targets[:, None], logits, 0.0), axis=1)
    stats = jnp.concatenate([peak, total, weighted, picked]).reshape(8, -1)
    live = live_rows.astype(jnp.float32).reshape(2, -1)
    results = exchange(stats, live, n_voc, n_grp).reshape(n_grp, 2, tok_rows)
    lanes = 128
    every = jnp.concatenate(
        [results[:, 0].reshape(-1, lanes), results[:, 1].reshape(-1, lanes)], axis=1)
    high = return_from // lanes
    low = return_from % lanes
    pick_row = (high[:, None] == jnp.arange(every.shape[0], dtype=jnp.int32)[None, :]).astype(jnp.float32)
    rows_picked = jnp.dot(pick_row, every, precision=lax.Precision.HIGHEST)
    pick_lane = low[:, None] == jnp.arange(lanes, dtype=jnp.int32)[None, :]
    token_logp = jnp.sum(jnp.where(pick_lane, rows_picked[:, :lanes], 0.0), axis=1)
    token_entropy = jnp.sum(jnp.where(pick_lane, rows_picked[:, lanes:], 0.0), axis=1)
    return (token_logp, token_entropy)


def solution(mesh):
    placed = (P("grp", "voc"), P("grp"), P("grp"), P(), P("grp", "voc"), P("grp"))
    n_grp = mesh.shape["grp"]
    n_z = len({device.coords[2] for device in mesh.devices[:, 0]})
    body = functools.partial(local, n_voc=mesh.shape["voc"], n_grp=n_grp, n_x=n_grp // n_z, n_z=n_z)
    return jax.shard_map(
        body, mesh=mesh, in_specs=placed, out_specs=(P("grp"), P("grp")), check_vma=False
    )
```

```python
import functools

import jax
import jax.numpy as jnp
from jax import lax
from jax.experimental import pallas as pl
from jax.experimental.pallas import tpu as pltpu
from jax.sharding import PartitionSpec as P

MESH = pl.DeviceIdType.MESH

EPSILON = 1e-05


def _exchange_kernel(n_voc, n_grp, stats_ref, live_ref, out_ref, parts, voc_sems, grp_sems):
    g = lax.axis_index("grp")
    v = lax.axis_index("voc")

    def along_voc(t):
        return (g, t)

    def along_grp(t):
        return (t, v)

    barrier = pltpu.get_barrier_semaphore()
    for k in range(1, n_voc):
        pl.semaphore_signal(barrier, inc=1, device_id=along_voc(lax.rem(v + k, n_voc)), device_id_type=MESH)
    for k in range(1, n_grp):
        pl.semaphore_signal(barrier, inc=1, device_id=along_grp(lax.rem(g + k, n_grp)), device_id_type=MESH)
    pl.semaphore_wait(barrier, n_voc + n_grp - 2)

    def send_all(src, buffer, me, n, sems, device, fill):
        copies = []
        for k in range(1, n):
            copy = pltpu.make_async_remote_copy(
                src_ref=src, dst_ref=buffer.at[me],
                send_sem=sems.at[0, k], recv_sem=sems.at[1, k],
                device_id=device(lax.rem(me + k, n)), device_id_type=MESH,
            )
            copy.start()
            copies.append(copy)
        fill()
        for k in range(1, n):
            source = lax.rem(me + n - k, n)
            pltpu.make_async_remote_copy(
                src_ref=src, dst_ref=buffer.at[source],
                send_sem=sems.at[0, k], recv_sem=sems.at[1, k],
                device_id=device(source), device_id_type=MESH,
            ).wait_recv()
        for copy in copies:
            copy.wait_send()

    def keep_stats():
        parts[v] = stats_ref[...]

    send_all(stats_ref, parts, v, n_voc, voc_sems, along_voc, keep_stats)
    every = parts[...]
    quarter = every.shape[1] // 4
    peaks = every[:, :quarter]
    peak = jnp.max(peaks, axis=0)
    factor = jnp.exp(peaks - peak[None])
    total = jnp.sum(every[:, quarter:2 * quarter] * factor, axis=0)
    weighted = jnp.sum(every[:, 2 * quarter:3 * quarter] * factor, axis=0)
    picked = jnp.sum(every[:, 3 * quarter:], axis=0)
    log_total = peak + jnp.log(total)
    live = live_ref[...] > 0.0
    out_ref[g, :quarter] = jnp.where(live, picked - log_total, 0.0)
    out_ref[g, quarter:] = jnp.where(live, log_total - weighted / total, 0.0)
    send_all(out_ref.at[g], out_ref, g, n_grp, grp_sems, along_grp, lambda: None)


def exchange(stats, live, n_voc, n_grp):
    rows, lanes = stats.shape
    return pl.pallas_call(
        functools.partial(_exchange_kernel, n_voc, n_grp),
        out_shape=jax.ShapeDtypeStruct((n_grp, rows // 2, lanes), stats.dtype),
        in_specs=[pl.BlockSpec(memory_space=pltpu.VMEM)] * 2,
        out_specs=pl.BlockSpec(memory_space=pltpu.VMEM),
        scratch_shapes=[pltpu.VMEM((n_voc, rows, lanes), stats.dtype),
                        pltpu.SemaphoreType.DMA((2, n_voc)), pltpu.SemaphoreType.DMA((2, n_grp))],
        compiler_params=pltpu.CompilerParams(collective_id=0, has_side_effects=True),
    )(stats, live)


class _Ring:
    def __init__(self, pos, n, device, slot, own, sems, on_arrival=None, split=True):
        self.pos, self.n, self.device, self.slot, self.own = pos, n, device, slot, own
        self.sems = sems
        self.on_arrival = on_arrival
        self.split = split and n % 2 == 0
        self.counts = (n // 2, n // 2) if self.split else (n // 2, n - 1 - n // 2)
        self.steps = max(self.counts)
        self.copies = []
        self.next = 1

    def advance(self):
        if self.next <= self.steps:
            self.step(self.next)
            self.next += 1

    def _part(self, s, kind):
        return kind // 2 if self.split and s == self.steps else None

    def _origin(self, step, sign):
        return lax.rem(self.pos + sign * step + 2 * self.n, self.n)

    def _desc(self, src, origin, kind, s, target):
        return pltpu.make_async_remote_copy(
            src_ref=src, dst_ref=self.slot(origin, self._part(s, kind)),
            send_sem=self.sems.at[kind, s - 1], recv_sem=self.sems.at[kind + 1, s - 1],
            device_id=self.device(target), device_id_type=MESH,
        )

    def step(self, s):
        if s > self.steps:
            return
        for (kind, sign), count in zip(((0, 1), (2, -1)), self.counts):
            if s > count:
                continue
            target = self._origin(1, sign)
            origin = self._origin(s - 1, -sign)
            part = self._part(s, kind)
            if s == 1:
                src = self.own(part)
            else:
                self._desc(self.slot(origin), origin, kind, s - 1, target).wait_recv()
                if self.on_arrival is not None:
                    self.on_arrival(origin)
                src = self.slot(origin, part)
            copy = self._desc(src, origin, kind, s, target)
            copy.start()
            self.copies.append(copy)

    def finish_recv(self):
        while self.next <= self.steps:
            self.advance()
        if not self.steps:
            return
        last = []
        for (kind, sign), count in zip(((0, 1), (2, -1)), self.counts):
            if not count:
                continue
            origin = self._origin(count, -sign)
            view = self.slot(origin, self._part(count, kind))
            self._desc(view, origin, kind, count, self._origin(1, sign)).wait_recv()
            last.append(origin)
        if self.on_arrival is not None:
            for origin in last[:1] if self.split else last:
                self.on_arrival(origin)

    def finish_send(self):
        for copy in self.copies:
            copy.wait_send()


def _gather_kernel(n_x, n_z, n_y, rows_ref, head_ref, gain_ref, normed_out, head_out, rows_out,
                   local_sem, sems, pair_sems):
    me = lax.axis_index("grp")
    v = lax.axis_index("voc")
    x = me // n_z
    z = me % n_z
    y = v // 2
    c = v % 2
    partner = y * 2 + 1 - c
    half = head_ref.shape[0] * 3 // 8
    lo, hi = pl.ds(0, half), pl.ds(half, head_ref.shape[0] - half)
    width = rows_ref.shape[1]

    def cols(t):
        return pl.ds(pl.multiple_of(t * width, width), width)

    def along_x(t):
        return (t * n_z + z, v)

    def along_z(t):
        return (x * n_z + t, v)

    def along_y(t):
        return (me, t * 2 + c)

    barrier = pltpu.get_barrier_semaphore()
    neighbours = [along_x(lax.rem(x + 1, n_x)), along_x(lax.rem(x + n_x - 1, n_x)),
                  along_z(lax.rem(z + 1, n_z)), along_z(lax.rem(z + n_z - 1, n_z)),
                  along_y(lax.rem(y + 1, n_y)), along_y(lax.rem(y + n_y - 1, n_y)),
                  (me, partner)]
    for target in neighbours:
        pl.semaphore_signal(barrier, inc=1, device_id=target, device_id_type=MESH)
    pl.semaphore_wait(barrier, len(neighbours))

    def to_partner(src, t):
        return pltpu.make_async_remote_copy(
            src_ref=src, dst_ref=rows_out.at[:, cols(t * 2 + c)],
            send_sem=pair_sems.at[0, t], recv_sem=pair_sems.at[1, t],
            device_id=(me, partner), device_id_type=MESH,
        )

    pair_copies = []

    def forward(t):
        copy = to_partner(rows_out.at[:, cols(t * 2 + c)], t)
        copy.start()
        pair_copies.append(copy)

    own = pltpu.make_async_copy(head_ref, head_out.at[x, z], local_sem.at[0])
    own.start()
    copy = to_partner(rows_ref, y)
    copy.start()
    pair_copies.append(copy)
    rows_out[:, cols(v)] = rows_ref[...]
    def halves(size, start=0):
        return lambda part: pl.ds(start, size) if part is None else pl.ds(start + part * (size // 2), size // 2)

    rows_part = halves(rows_ref.shape[0])
    lo_part, hi_part = halves(half), halves(head_ref.shape[0] - half, half)
    x_part, z_part = halves(n_x), halves(n_z)
    rows = _Ring(y, n_y, along_y, lambda t, p=None: rows_out.at[rows_part(p), cols(t * 2 + c)],
                 lambda p: rows_ref.at[rows_part(p)], sems.at[4], forward)
    first_x = _Ring(x, n_x, along_x, lambda t, p=None: head_out.at[t, z, lo_part(p)],
                    lambda p: head_ref.at[lo_part(p)], sems.at[0], split=False)
    first_z = _Ring(z, n_z, along_z, lambda t, p=None: head_out.at[x, t, hi_part(p)],
                    lambda p: head_ref.at[hi_part(p)], sems.at[1], split=False)
    rows.advance()
    first_x.advance()
    first_z.advance()
    first_x.advance()
    first_z.advance()
    own.wait()
    first_x.finish_recv()
    second_z = _Ring(z, n_z, along_z, lambda t, p=None: head_out.at[x_part(p), t, lo],
                     lambda p: head_out.at[x_part(p), z, lo], sems.at[2])
    second_x = _Ring(x, n_x, along_x, lambda t, p=None: head_out.at[t, z_part(p), hi],
                     lambda p: head_out.at[x, z_part(p), hi], sems.at[3])
    second_z.advance()
    first_z.advance()
    rows.advance()
    first_z.advance()
    first_z.finish_recv()
    second_x.advance()
    rows.advance()
    second_z.advance()
    rows.advance()
    second_z.advance()
    rows.finish_recv()
    second_x.advance()
    second_z.advance()
    for t in range(n_y):
        other = t * 2 + 1 - c
        block = rows_out.at[:, cols(other)]
        pltpu.make_async_remote_copy(
            src_ref=block, dst_ref=block,
            send_sem=pair_sems.at[0, t], recv_sem=pair_sems.at[1, t],
            device_id=(me, partner), device_id_type=MESH,
        ).wait_recv()
    chunk = 64

    def norm_chunk(i, carry):
        start = pl.multiple_of(i * chunk, chunk)
        values = rows_out[pl.ds(start, chunk), :].astype(jnp.float32)
        scale = lax.rsqrt(jnp.mean(values * values, axis=1, keepdims=True) + EPSILON)
        normed_out[pl.ds(start, chunk), :] = (values * scale * gain_ref[...]).astype(normed_out.dtype)
        return carry

    lax.fori_loop(0, rows_out.shape[0] // chunk, norm_chunk, 0)
    second_z.finish_recv()
    second_x.finish_recv()
    for ring in (first_x, first_z, second_z, second_x, rows):
        ring.finish_send()
    for copy in pair_copies:
        copy.wait_send()


def gather_both(hidden, piece, norm_gain, n_x, n_z, n_voc):
    rows, width = hidden.shape
    depth, vocab = piece.shape
    n_y = n_voc // 2
    steps = max(n_x, n_z, n_y)
    gain = norm_gain.astype(jnp.float32)[None, :]
    full_rows, full_head = pl.pallas_call(
        functools.partial(_gather_kernel, n_x, n_z, n_y),
        out_shape=(jax.ShapeDtypeStruct((rows, width * n_voc), hidden.dtype),
                   jax.ShapeDtypeStruct((n_x, n_z, depth, vocab), piece.dtype)),
        in_specs=[pl.BlockSpec(memory_space=pltpu.VMEM)] * 3,
        out_specs=(pl.BlockSpec(memory_space=pltpu.VMEM), pl.BlockSpec(memory_space=pltpu.VMEM)),
        scratch_shapes=[pltpu.VMEM((rows, width * n_voc), hidden.dtype),
                        pltpu.SemaphoreType.DMA((1,)), pltpu.SemaphoreType.DMA((5, 4, steps)),
                        pltpu.SemaphoreType.DMA((2, n_y))],
        compiler_params=pltpu.CompilerParams(collective_id=3, has_side_effects=True),
    )(hidden, piece, gain)
    return full_rows, full_head.reshape(n_x * n_z * depth, vocab)


def local(hidden, targets, row_count, norm_gain, head_weight, return_from, *, n_voc, n_grp, n_x, n_z):
    tok_rows = hidden.shape[0]
    positions = jnp.arange(tok_rows, dtype=jnp.int32)
    live_rows = positions < row_count[0]
    normed, piece = gather_both(hidden, head_weight, norm_gain, n_x, n_z, n_voc)
    vocab_local = head_weight.shape[1]
    logits = jnp.dot(normed, piece, preferred_element_type=jnp.float32)
    peak = jnp.max(logits, axis=1)
    shifted = jnp.exp(logits - peak[:, None])
    total = jnp.sum(shifted, axis=1)
    weighted = jnp.sum(shifted * logits, axis=1)
    global_columns = lax.axis_index("voc") * vocab_local + jnp.arange(vocab_local, dtype=jnp.int32)
    picked = jnp.sum(jnp.where(global_columns[None, :] == targets[:, None], logits, 0.0), axis=1)
    stats = jnp.concatenate([peak, total, weighted, picked]).reshape(8, -1)
    live = live_rows.astype(jnp.float32).reshape(2, -1)
    results = exchange(stats, live, n_voc, n_grp).reshape(n_grp, 2, tok_rows)
    lanes = 128
    every = jnp.concatenate(
        [results[:, 0].reshape(-1, lanes), results[:, 1].reshape(-1, lanes)], axis=1)
    high = return_from // lanes
    low = return_from % lanes
    pick_row = (high[:, None] == jnp.arange(every.shape[0], dtype=jnp.int32)[None, :]).astype(jnp.float32)
    rows_picked = jnp.dot(pick_row, every, precision=lax.Precision.HIGHEST)
    pick_lane = low[:, None] == jnp.arange(lanes, dtype=jnp.int32)[None, :]
    token_logp = jnp.sum(jnp.where(pick_lane, rows_picked[:, :lanes], 0.0), axis=1)
    token_entropy = jnp.sum(jnp.where(pick_lane, rows_picked[:, lanes:], 0.0), axis=1)
    return (token_logp, token_entropy)


def solution(mesh):
    placed = (P("grp", "voc"), P("grp"), P("grp"), P(), P("grp", "voc"), P("grp"))
    n_grp = mesh.shape["grp"]
    n_z = len({device.coords[2] for device in mesh.devices[:, 0]})
    body = functools.partial(local, n_voc=mesh.shape["voc"], n_grp=n_grp, n_x=n_grp // n_z, n_z=n_z)
    return jax.shard_map(
        body, mesh=mesh, in_specs=placed, out_specs=(P("grp"), P("grp")), check_vma=False
    )
```

```python
import functools

import jax
import jax.numpy as jnp
from jax import lax
from jax.experimental import pallas as pl
from jax.experimental.pallas import tpu as pltpu
from jax.sharding import PartitionSpec as P

MESH = pl.DeviceIdType.MESH

EPSILON = 1e-05


def _exchange_kernel(n_voc, n_grp, stats_ref, count_ref, out_ref, parts, voc_sems, grp_sems):
    g = lax.axis_index("grp")
    v = lax.axis_index("voc")

    def along_voc(t):
        return (g, t)

    def along_grp(t):
        return (t, v)

    barrier = pltpu.get_barrier_semaphore()
    for k in range(1, n_voc):
        pl.semaphore_signal(barrier, inc=1, device_id=along_voc(lax.rem(v + k, n_voc)), device_id_type=MESH)
    for k in range(1, n_grp):
        pl.semaphore_signal(barrier, inc=1, device_id=along_grp(lax.rem(g + k, n_grp)), device_id_type=MESH)
    pl.semaphore_wait(barrier, n_voc + n_grp - 2)

    def send_all(src, buffer, me, n, sems, device, fill):
        copies = []
        for k in range(1, n):
            copy = pltpu.make_async_remote_copy(
                src_ref=src, dst_ref=buffer.at[me],
                send_sem=sems.at[0, k], recv_sem=sems.at[1, k],
                device_id=device(lax.rem(me + k, n)), device_id_type=MESH,
            )
            copy.start()
            copies.append(copy)
        fill()
        for k in range(1, n):
            source = lax.rem(me + n - k, n)
            pltpu.make_async_remote_copy(
                src_ref=src, dst_ref=buffer.at[source],
                send_sem=sems.at[0, k], recv_sem=sems.at[1, k],
                device_id=device(source), device_id_type=MESH,
            ).wait_recv()
        for copy in copies:
            copy.wait_send()

    def keep_stats():
        parts[v] = stats_ref[...]

    send_all(stats_ref, parts, v, n_voc, voc_sems, along_voc, keep_stats)
    every = parts[...]
    quarter = every.shape[1] // 4
    peaks = every[:, :quarter]
    peak = jnp.max(peaks, axis=0)
    factor = jnp.exp(peaks - peak[None])
    total = jnp.sum(every[:, quarter:2 * quarter] * factor, axis=0)
    weighted = jnp.sum(every[:, 2 * quarter:3 * quarter] * factor, axis=0)
    picked = jnp.sum(every[:, 3 * quarter:], axis=0)
    log_total = peak + jnp.log(total)
    shape = peak.shape
    row = lax.broadcasted_iota(jnp.int32, shape, 0) * shape[1] + lax.broadcasted_iota(jnp.int32, shape, 1)
    live = row < count_ref[...]
    out_ref[g, :quarter] = jnp.where(live, picked - log_total, 0.0)
    out_ref[g, quarter:] = jnp.where(live, log_total - weighted / total, 0.0)
    send_all(out_ref.at[g], out_ref, g, n_grp, grp_sems, along_grp, lambda: None)


def exchange(stats, count, n_voc, n_grp):
    rows, lanes = stats.shape
    return pl.pallas_call(
        functools.partial(_exchange_kernel, n_voc, n_grp),
        out_shape=jax.ShapeDtypeStruct((n_grp, rows // 2, lanes), stats.dtype),
        in_specs=[pl.BlockSpec(memory_space=pltpu.VMEM)] * 2,
        out_specs=pl.BlockSpec(memory_space=pltpu.VMEM),
        scratch_shapes=[pltpu.VMEM((n_voc, rows, lanes), stats.dtype),
                        pltpu.SemaphoreType.DMA((2, n_voc)), pltpu.SemaphoreType.DMA((2, n_grp))],
        compiler_params=pltpu.CompilerParams(collective_id=0, has_side_effects=True),
    )(stats, count)


class _Ring:
    def __init__(self, pos, n, device, slot, own, sems, on_arrival=None):
        self.pos, self.n, self.device, self.slot, self.own = pos, n, device, slot, own
        self.sems = sems
        self.on_arrival = on_arrival
        self.steps = n // 2
        self.split = n % 2 == 0
        self.copies = []
        self.next = 1

    def advance(self):
        if self.next <= self.steps:
            self.step(self.next)
            self.next += 1

    def _part(self, s, kind):
        return kind // 2 if self.split and s == self.steps else None

    def _origin(self, step, sign):
        return lax.rem(self.pos + sign * step + 2 * self.n, self.n)

    def _desc(self, src, origin, kind, s, target):
        return pltpu.make_async_remote_copy(
            src_ref=src, dst_ref=self.slot(origin, self._part(s, kind)),
            send_sem=self.sems.at[kind, s - 1], recv_sem=self.sems.at[kind + 1, s - 1],
            device_id=self.device(target), device_id_type=MESH,
        )

    def step(self, s):
        if s > self.steps:
            return
        for kind, sign in ((0, 1), (2, -1)):
            target = self._origin(1, sign)
            origin = self._origin(s - 1, -sign)
            part = self._part(s, kind)
            if s == 1:
                src = self.own(part)
            else:
                self._desc(self.slot(origin), origin, kind, s - 1, target).wait_recv()
                if self.on_arrival is not None:
                    self.on_arrival(origin)
                src = self.slot(origin, part)
            copy = self._desc(src, origin, kind, s, target)
            copy.start()
            self.copies.append(copy)

    def finish_recv(self):
        while self.next <= self.steps:
            self.advance()
        if not self.steps:
            return
        last = []
        for kind, sign in ((0, 1), (2, -1)):
            origin = self._origin(self.steps, -sign)
            view = self.slot(origin, self._part(self.steps, kind))
            self._desc(view, origin, kind, self.steps, self._origin(1, sign)).wait_recv()
            last.append(origin)
        if self.on_arrival is not None:
            for origin in last[:1] if self.split else last:
                self.on_arrival(origin)

    def finish_send(self):
        for copy in self.copies:
            copy.wait_send()


def _gather_kernel(n_x, n_z, n_y, rows_ref, head_ref, gain_ref, normed_out, head_out, rows_out,
                   local_sem, sems, pair_sems):
    me = lax.axis_index("grp")
    v = lax.axis_index("voc")
    x = me // n_z
    z = me % n_z
    y = v // 2
    c = v % 2
    partner = y * 2 + 1 - c
    half = head_ref.shape[0] // 2
    lo, hi = pl.ds(0, half), pl.ds(half, half)
    width = rows_ref.shape[1]

    def cols(t):
        return pl.ds(pl.multiple_of(t * width, width), width)

    def along_x(t):
        return (t * n_z + z, v)

    def along_z(t):
        return (x * n_z + t, v)

    def along_y(t):
        return (me, t * 2 + c)

    barrier = pltpu.get_barrier_semaphore()
    neighbours = [along_x(lax.rem(x + 1, n_x)), along_x(lax.rem(x + n_x - 1, n_x)),
                  along_z(lax.rem(z + 1, n_z)), along_z(lax.rem(z + n_z - 1, n_z)),
                  along_y(lax.rem(y + 1, n_y)), along_y(lax.rem(y + n_y - 1, n_y)),
                  (me, partner)]
    for target in neighbours:
        pl.semaphore_signal(barrier, inc=1, device_id=target, device_id_type=MESH)
    pl.semaphore_wait(barrier, len(neighbours))

    def to_partner(src, t):
        return pltpu.make_async_remote_copy(
            src_ref=src, dst_ref=rows_out.at[:, cols(t * 2 + c)],
            send_sem=pair_sems.at[0, t], recv_sem=pair_sems.at[1, t],
            device_id=(me, partner), device_id_type=MESH,
        )

    pair_copies = []

    def forward(t):
        copy = to_partner(rows_out.at[:, cols(t * 2 + c)], t)
        copy.start()
        pair_copies.append(copy)

    own = pltpu.make_async_copy(head_ref, head_out.at[x, z], local_sem.at[0])
    own.start()
    copy = to_partner(rows_ref, y)
    copy.start()
    pair_copies.append(copy)
    rows_out[:, cols(v)] = rows_ref[...]
    def halves(size, start=0):
        return lambda part: pl.ds(start, size) if part is None else pl.ds(start + part * (size // 2), size // 2)

    rows_part = halves(rows_ref.shape[0])
    lo_part, hi_part = halves(half), halves(half, half)
    x_part, z_part = halves(n_x), halves(n_z)
    rows = _Ring(y, n_y, along_y, lambda t, p=None: rows_out.at[rows_part(p), cols(t * 2 + c)],
                 lambda p: rows_ref.at[rows_part(p)], sems.at[4], forward)
    first_x = _Ring(x, n_x, along_x, lambda t, p=None: head_out.at[t, z, lo_part(p)],
                    lambda p: head_ref.at[lo_part(p)], sems.at[0])
    first_z = _Ring(z, n_z, along_z, lambda t, p=None: head_out.at[x, t, hi_part(p)],
                    lambda p: head_ref.at[hi_part(p)], sems.at[1])
    rows.advance()
    first_x.advance()
    first_z.advance()
    first_x.advance()
    first_z.advance()
    own.wait()
    first_x.finish_recv()
    second_z = _Ring(z, n_z, along_z, lambda t, p=None: head_out.at[x_part(p), t, lo],
                     lambda p: head_out.at[x_part(p), z, lo], sems.at[2])
    second_x = _Ring(x, n_x, along_x, lambda t, p=None: head_out.at[t, z_part(p), hi],
                     lambda p: head_out.at[x, z_part(p), hi], sems.at[3])
    second_z.advance()
    first_z.advance()
    rows.advance()
    first_z.advance()
    first_z.finish_recv()
    second_x.advance()
    rows.advance()
    second_z.advance()
    rows.advance()
    second_z.advance()
    rows.finish_recv()
    second_x.advance()
    second_z.advance()
    for t in range(n_y):
        other = t * 2 + 1 - c
        block = rows_out.at[:, cols(other)]
        pltpu.make_async_remote_copy(
            src_ref=block, dst_ref=block,
            send_sem=pair_sems.at[0, t], recv_sem=pair_sems.at[1, t],
            device_id=(me, partner), device_id_type=MESH,
        ).wait_recv()
    chunk = 64

    def norm_chunk(i, carry):
        start = pl.multiple_of(i * chunk, chunk)
        values = rows_out[pl.ds(start, chunk), :].astype(jnp.float32)
        scale = lax.rsqrt(jnp.mean(values * values, axis=1, keepdims=True) + EPSILON)
        normed_out[pl.ds(start, chunk), :] = (values * scale * gain_ref[...]).astype(normed_out.dtype)
        return carry

    lax.fori_loop(0, rows_out.shape[0] // chunk, norm_chunk, 0)
    second_z.finish_recv()
    second_x.finish_recv()
    for ring in (first_x, first_z, second_z, second_x, rows):
        ring.finish_send()
    for copy in pair_copies:
        copy.wait_send()


def gather_both(hidden, piece, norm_gain, n_x, n_z, n_voc):
    rows, width = hidden.shape
    depth, vocab = piece.shape
    n_y = n_voc // 2
    steps = max(n_x, n_z, n_y)
    gain = norm_gain.astype(jnp.float32)[None, :]
    full_rows, full_head = pl.pallas_call(
        functools.partial(_gather_kernel, n_x, n_z, n_y),
        out_shape=(jax.ShapeDtypeStruct((rows, width * n_voc), hidden.dtype),
                   jax.ShapeDtypeStruct((n_x, n_z, depth, vocab), piece.dtype)),
        in_specs=[pl.BlockSpec(memory_space=pltpu.VMEM)] * 3,
        out_specs=(pl.BlockSpec(memory_space=pltpu.VMEM), pl.BlockSpec(memory_space=pltpu.VMEM)),
        scratch_shapes=[pltpu.VMEM((rows, width * n_voc), hidden.dtype),
                        pltpu.SemaphoreType.DMA((1,)), pltpu.SemaphoreType.DMA((5, 4, steps)),
                        pltpu.SemaphoreType.DMA((2, n_y))],
        compiler_params=pltpu.CompilerParams(collective_id=3, has_side_effects=True),
    )(hidden, piece, gain)
    return full_rows, full_head.reshape(n_x * n_z * depth, vocab)


def local(hidden, targets, row_count, norm_gain, head_weight, return_from, *, n_voc, n_grp, n_x, n_z):
    tok_rows = hidden.shape[0]
    normed, piece = gather_both(hidden, head_weight, norm_gain, n_x, n_z, n_voc)
    vocab_local = head_weight.shape[1]
    logits = jnp.dot(normed, piece, preferred_element_type=jnp.float32)
    peak = jnp.max(logits, axis=1)
    shifted = jnp.exp(logits - peak[:, None])
    total = jnp.sum(shifted, axis=1)
    weighted = jnp.sum(shifted * logits, axis=1)
    global_columns = lax.axis_index("voc") * vocab_local + jnp.arange(vocab_local, dtype=jnp.int32)
    picked = jnp.sum(jnp.where(global_columns[None, :] == targets[:, None], logits, 0.0), axis=1)
    stats = jnp.concatenate([peak, total, weighted, picked]).reshape(8, -1)
    results = exchange(stats, row_count.reshape(1, 1), n_voc, n_grp).reshape(n_grp, 2, tok_rows)
    lanes = 128
    every = jnp.concatenate(
        [results[:, 0].reshape(-1, lanes), results[:, 1].reshape(-1, lanes)], axis=1)
    high = return_from // lanes
    low = return_from % lanes
    pick_row = (high[:, None] == jnp.arange(every.shape[0], dtype=jnp.int32)[None, :]).astype(jnp.float32)
    rows_picked = jnp.dot(pick_row, every, precision=lax.Precision.HIGHEST)
    pick_lane = low[:, None] == jnp.arange(lanes, dtype=jnp.int32)[None, :]
    token_logp = jnp.sum(jnp.where(pick_lane, rows_picked[:, :lanes], 0.0), axis=1)
    token_entropy = jnp.sum(jnp.where(pick_lane, rows_picked[:, lanes:], 0.0), axis=1)
    return (token_logp, token_entropy)


def solution(mesh):
    placed = (P("grp", "voc"), P("grp"), P("grp"), P(), P("grp", "voc"), P("grp"))
    n_grp = mesh.shape["grp"]
    n_z = len({device.coords[2] for device in mesh.devices[:, 0]})
    body = functools.partial(local, n_voc=mesh.shape["voc"], n_grp=n_grp, n_x=n_grp // n_z, n_z=n_z)
    return jax.shard_map(
        body, mesh=mesh, in_specs=placed, out_specs=(P("grp"), P("grp")), check_vma=False
    )
```

```python
import functools

import jax
import jax.numpy as jnp
from jax import lax
from jax.experimental import pallas as pl
from jax.experimental.pallas import tpu as pltpu
from jax.sharding import PartitionSpec as P

MESH = pl.DeviceIdType.MESH

EPSILON = 1e-05


def _exchange_kernel(n_voc, n_grp, stats_ref, count_ref, out_ref, parts, voc_sems, grp_sems):
    g = lax.axis_index("grp")
    v = lax.axis_index("voc")

    def along_voc(t):
        return (g, t)

    def along_grp(t):
        return (t, v)

    barrier = pltpu.get_barrier_semaphore()
    for k in range(1, n_voc):
        pl.semaphore_signal(barrier, inc=1, device_id=along_voc(lax.rem(v + k, n_voc)), device_id_type=MESH)
    for k in range(1, n_grp):
        pl.semaphore_signal(barrier, inc=1, device_id=along_grp(lax.rem(g + k, n_grp)), device_id_type=MESH)
    pl.semaphore_wait(barrier, n_voc + n_grp - 2)

    def send_all(src, buffer, me, n, sems, device, fill):
        copies = []
        for k in range(1, n):
            copy = pltpu.make_async_remote_copy(
                src_ref=src, dst_ref=buffer.at[me],
                send_sem=sems.at[0, k], recv_sem=sems.at[1, k],
                device_id=device(lax.rem(me + k, n)), device_id_type=MESH,
            )
            copy.start()
            copies.append(copy)
        fill()
        for k in range(1, n):
            source = lax.rem(me + n - k, n)
            pltpu.make_async_remote_copy(
                src_ref=src, dst_ref=buffer.at[source],
                send_sem=sems.at[0, k], recv_sem=sems.at[1, k],
                device_id=device(source), device_id_type=MESH,
            ).wait_recv()
        for copy in copies:
            copy.wait_send()

    def keep_stats():
        parts[v] = stats_ref[...]

    send_all(stats_ref, parts, v, n_voc, voc_sems, along_voc, keep_stats)
    every = parts[...]
    quarter = every.shape[1] // 4
    peaks = every[:, :quarter]
    peak = jnp.max(peaks, axis=0)
    factor = jnp.exp(peaks - peak[None])
    total = jnp.sum(every[:, quarter:2 * quarter] * factor, axis=0)
    weighted = jnp.sum(every[:, 2 * quarter:3 * quarter] * factor, axis=0)
    picked = jnp.sum(every[:, 3 * quarter:], axis=0)
    log_total = peak + jnp.log(total)
    shape = peak.shape
    row = lax.broadcasted_iota(jnp.int32, shape, 0) * shape[1] + lax.broadcasted_iota(jnp.int32, shape, 1)
    live = row < count_ref[...]
    out_ref[g, :quarter] = jnp.where(live, picked - log_total, 0.0)
    out_ref[g, quarter:] = jnp.where(live, log_total - weighted / total, 0.0)
    send_all(out_ref.at[g], out_ref, g, n_grp, grp_sems, along_grp, lambda: None)


def exchange(stats, count, n_voc, n_grp):
    rows, lanes = stats.shape
    return pl.pallas_call(
        functools.partial(_exchange_kernel, n_voc, n_grp),
        out_shape=jax.ShapeDtypeStruct((n_grp, rows // 2, lanes), stats.dtype),
        in_specs=[pl.BlockSpec(memory_space=pltpu.VMEM)] * 2,
        out_specs=pl.BlockSpec(memory_space=pltpu.VMEM),
        scratch_shapes=[pltpu.VMEM((n_voc, rows, lanes), stats.dtype),
                        pltpu.SemaphoreType.DMA((2, n_voc)), pltpu.SemaphoreType.DMA((2, n_grp))],
        compiler_params=pltpu.CompilerParams(collective_id=0, has_side_effects=True),
    )(stats, count)


class _Ring:
    def __init__(self, pos, n, device, slot, own, sems, on_arrival=None):
        self.pos, self.n, self.device, self.slot, self.own = pos, n, device, slot, own
        self.sems = sems
        self.on_arrival = on_arrival
        self.steps = n // 2
        self.split = n % 2 == 0
        self.copies = []
        self.next = 1

    def advance(self):
        if self.next <= self.steps:
            self.step(self.next)
            self.next += 1

    def _part(self, s, kind):
        return kind // 2 if self.split and s == self.steps else None

    def _origin(self, step, sign):
        return lax.rem(self.pos + sign * step + 2 * self.n, self.n)

    def _desc(self, src, origin, kind, s, target):
        return pltpu.make_async_remote_copy(
            src_ref=src, dst_ref=self.slot(origin, self._part(s, kind)),
            send_sem=self.sems.at[kind, s - 1], recv_sem=self.sems.at[kind + 1, s - 1],
            device_id=self.device(target), device_id_type=MESH,
        )

    def step(self, s):
        if s > self.steps:
            return
        for kind, sign in ((0, 1), (2, -1)):
            target = self._origin(1, sign)
            origin = self._origin(s - 1, -sign)
            part = self._part(s, kind)
            if s == 1:
                src = self.own(part)
            else:
                self._desc(self.slot(origin), origin, kind, s - 1, target).wait_recv()
                if self.on_arrival is not None:
                    self.on_arrival(origin)
                src = self.slot(origin, part)
            copy = self._desc(src, origin, kind, s, target)
            copy.start()
            self.copies.append(copy)

    def finish_recv(self):
        while self.next <= self.steps:
            self.advance()
        if not self.steps:
            return
        last = []
        for kind, sign in ((0, 1), (2, -1)):
            origin = self._origin(self.steps, -sign)
            view = self.slot(origin, self._part(self.steps, kind))
            self._desc(view, origin, kind, self.steps, self._origin(1, sign)).wait_recv()
            last.append(origin)
        if self.on_arrival is not None:
            for origin in last[:1] if self.split else last:
                self.on_arrival(origin)

    def finish_send(self):
        for copy in self.copies:
            copy.wait_send()


def _gather_kernel(n_x, n_z, n_y, rows_ref, head_ref, gain_ref, normed_out, head_out, rows_out,
                   local_sem, sems, pair_sems):
    me = lax.axis_index("grp")
    v = lax.axis_index("voc")
    x = me // n_z
    z = me % n_z
    y = v // 2
    c = v % 2
    partner = y * 2 + 1 - c
    half = head_ref.shape[0] // 2
    lo, hi = pl.ds(0, half), pl.ds(half, half)
    width = rows_ref.shape[1]

    def cols(t):
        return pl.ds(pl.multiple_of(t * width, width), width)

    def along_x(t):
        return (t * n_z + z, v)

    def along_z(t):
        return (x * n_z + t, v)

    def along_y(t):
        return (me, t * 2 + c)

    barrier = pltpu.get_barrier_semaphore()
    neighbours = [along_x(lax.rem(x + 1, n_x)), along_x(lax.rem(x + n_x - 1, n_x)),
                  along_z(lax.rem(z + 1, n_z)), along_z(lax.rem(z + n_z - 1, n_z)),
                  along_y(lax.rem(y + 1, n_y)), along_y(lax.rem(y + n_y - 1, n_y)),
                  (me, partner)]
    for target in neighbours:
        pl.semaphore_signal(barrier, inc=1, device_id=target, device_id_type=MESH)
    pl.semaphore_wait(barrier, len(neighbours))

    def to_partner(src, t):
        return pltpu.make_async_remote_copy(
            src_ref=src, dst_ref=rows_out.at[:, cols(t * 2 + c)],
            send_sem=pair_sems.at[0, t], recv_sem=pair_sems.at[1, t],
            device_id=(me, partner), device_id_type=MESH,
        )

    pair_copies = []

    def forward(t):
        copy = to_partner(rows_out.at[:, cols(t * 2 + c)], t)
        copy.start()
        pair_copies.append(copy)

    own = pltpu.make_async_copy(head_ref, head_out.at[x, z], local_sem.at[0])
    own.start()
    copy = to_partner(rows_ref, y)
    copy.start()
    pair_copies.append(copy)
    rows_out[:, cols(v)] = rows_ref[...]
    def halves(size, start=0):
        return lambda part: pl.ds(start, size) if part is None else pl.ds(start + part * (size // 2), size // 2)

    rows_part = halves(rows_ref.shape[0])
    lo_part, hi_part = halves(half), halves(half, half)
    x_part, z_part = halves(n_x), halves(n_z)
    rows = _Ring(y, n_y, along_y, lambda t, p=None: rows_out.at[rows_part(p), cols(t * 2 + c)],
                 lambda p: rows_ref.at[rows_part(p)], sems.at[4], forward)
    first_x = _Ring(x, n_x, along_x, lambda t, p=None: head_out.at[t, z, lo_part(p)],
                    lambda p: head_ref.at[lo_part(p)], sems.at[0])
    first_z = _Ring(z, n_z, along_z, lambda t, p=None: head_out.at[x, t, hi_part(p)],
                    lambda p: head_ref.at[hi_part(p)], sems.at[1])
    rows.advance()
    first_x.advance()
    first_z.advance()
    first_x.advance()
    first_z.advance()
    own.wait()
    first_x.finish_recv()
    second_z = _Ring(z, n_z, along_z, lambda t, p=None: head_out.at[x_part(p), t, lo],
                     lambda p: head_out.at[x_part(p), z, lo], sems.at[2])
    second_x = _Ring(x, n_x, along_x, lambda t, p=None: head_out.at[t, z_part(p), hi],
                     lambda p: head_out.at[x, z_part(p), hi], sems.at[3])
    second_z.advance()
    first_z.advance()
    rows.advance()
    first_z.advance()
    first_z.finish_recv()
    second_x.advance()
    rows.advance()
    second_z.advance()
    rows.advance()
    second_z.advance()
    rows.finish_recv()
    second_x.advance()
    second_z.advance()
    for t in range(n_y):
        other = t * 2 + 1 - c
        block = rows_out.at[:, cols(other)]
        pltpu.make_async_remote_copy(
            src_ref=block, dst_ref=block,
            send_sem=pair_sems.at[0, t], recv_sem=pair_sems.at[1, t],
            device_id=(me, partner), device_id_type=MESH,
        ).wait_recv()
    chunk = 64

    def norm_chunk(i, carry):
        start = pl.multiple_of(i * chunk, chunk)
        values = rows_out[pl.ds(start, chunk), :].astype(jnp.float32)
        scale = lax.rsqrt(jnp.mean(values * values, axis=1, keepdims=True) + EPSILON)
        normed_out[pl.ds(start, chunk), :] = (values * scale * gain_ref[...]).astype(normed_out.dtype)
        return carry

    lax.fori_loop(0, rows_out.shape[0] // chunk, norm_chunk, 0)
    second_z.finish_recv()
    second_x.finish_recv()
    for ring in (first_x, first_z, second_z, second_x, rows):
        ring.finish_send()
    for copy in pair_copies:
        copy.wait_send()


def gather_both(hidden, piece, norm_gain, n_x, n_z, n_voc):
    rows, width = hidden.shape
    depth, vocab = piece.shape
    n_y = n_voc // 2
    steps = max(n_x, n_z, n_y)
    gain = norm_gain.astype(jnp.float32)[None, :]
    full_rows, full_head = pl.pallas_call(
        functools.partial(_gather_kernel, n_x, n_z, n_y),
        out_shape=(jax.ShapeDtypeStruct((rows, width * n_voc), hidden.dtype),
                   jax.ShapeDtypeStruct((n_x, n_z, depth, vocab), piece.dtype)),
        in_specs=[pl.BlockSpec(memory_space=pltpu.VMEM)] * 3,
        out_specs=(pl.BlockSpec(memory_space=pltpu.VMEM), pl.BlockSpec(memory_space=pltpu.VMEM)),
        scratch_shapes=[pltpu.VMEM((rows, width * n_voc), hidden.dtype),
                        pltpu.SemaphoreType.DMA((1,)), pltpu.SemaphoreType.DMA((5, 4, steps)),
                        pltpu.SemaphoreType.DMA((2, n_y))],
        compiler_params=pltpu.CompilerParams(collective_id=3, has_side_effects=True),
    )(hidden, piece, gain)
    return full_rows, full_head.reshape(n_x * n_z * depth, vocab)


def local(hidden, targets, row_count, norm_gain, head_weight, return_from, *, n_voc, n_grp, n_x, n_z):
    tok_rows = hidden.shape[0]
    normed, piece = gather_both(hidden, head_weight, norm_gain, n_x, n_z, n_voc)
    vocab_local = head_weight.shape[1]
    logits = jnp.dot(normed, piece, preferred_element_type=jnp.float32)
    peak = jnp.max(logits, axis=1)
    shifted = jnp.exp(logits - peak[:, None])
    total = jnp.sum(shifted, axis=1)
    weighted = jnp.sum(shifted * logits, axis=1)
    global_columns = lax.axis_index("voc") * vocab_local + jnp.arange(vocab_local, dtype=jnp.int32)
    picked = jnp.sum(jnp.where(global_columns[None, :] == targets[:, None], logits, 0.0), axis=1)
    stats = jnp.stack([peak, total, weighted, picked])
    results = exchange(stats, row_count.reshape(1, 1), n_voc, n_grp).reshape(n_grp, 2, tok_rows)
    lanes = 128
    every = jnp.concatenate(
        [results[:, 0].reshape(-1, lanes), results[:, 1].reshape(-1, lanes)], axis=1)
    high = return_from // lanes
    low = return_from % lanes
    pick_row = (high[:, None] == jnp.arange(every.shape[0], dtype=jnp.int32)[None, :]).astype(jnp.float32)
    rows_picked = jnp.dot(pick_row, every, precision=lax.Precision.HIGHEST)
    pick_lane = low[:, None] == jnp.arange(lanes, dtype=jnp.int32)[None, :]
    token_logp = jnp.sum(jnp.where(pick_lane, rows_picked[:, :lanes], 0.0), axis=1)
    token_entropy = jnp.sum(jnp.where(pick_lane, rows_picked[:, lanes:], 0.0), axis=1)
    return (token_logp, token_entropy)


def solution(mesh):
    placed = (P("grp", "voc"), P("grp"), P("grp"), P(), P("grp", "voc"), P("grp"))
    n_grp = mesh.shape["grp"]
    n_z = len({device.coords[2] for device in mesh.devices[:, 0]})
    body = functools.partial(local, n_voc=mesh.shape["voc"], n_grp=n_grp, n_x=n_grp // n_z, n_z=n_z)
    return jax.shard_map(
        body, mesh=mesh, in_specs=placed, out_specs=(P("grp"), P("grp")), check_vma=False
    )
```

```python
import functools

import jax
import jax.numpy as jnp
from jax import lax
from jax.experimental import pallas as pl
from jax.experimental.pallas import tpu as pltpu
from jax.sharding import PartitionSpec as P

MESH = pl.DeviceIdType.MESH

EPSILON = 1e-05


def _exchange_kernel(n_voc, n_grp, stats_ref, count_ref, out_ref, parts, voc_sems, grp_sems):
    g = lax.axis_index("grp")
    v = lax.axis_index("voc")

    def along_voc(t):
        return (g, t)

    def along_grp(t):
        return (t, v)

    barrier = pltpu.get_barrier_semaphore()
    for k in range(1, n_voc):
        pl.semaphore_signal(barrier, inc=1, device_id=along_voc(lax.rem(v + k, n_voc)), device_id_type=MESH)
    for k in range(1, n_grp):
        pl.semaphore_signal(barrier, inc=1, device_id=along_grp(lax.rem(g + k, n_grp)), device_id_type=MESH)
    pl.semaphore_wait(barrier, n_voc + n_grp - 2)

    def send_all(src, buffer, me, n, sems, device, fill):
        copies = []
        for k in range(1, n):
            copy = pltpu.make_async_remote_copy(
                src_ref=src, dst_ref=buffer.at[me],
                send_sem=sems.at[0, k], recv_sem=sems.at[1, k],
                device_id=device(lax.rem(me + k, n)), device_id_type=MESH,
            )
            copy.start()
            copies.append(copy)
        fill()
        for k in range(1, n):
            source = lax.rem(me + n - k, n)
            pltpu.make_async_remote_copy(
                src_ref=src, dst_ref=buffer.at[source],
                send_sem=sems.at[0, k], recv_sem=sems.at[1, k],
                device_id=device(source), device_id_type=MESH,
            ).wait_recv()
        for copy in copies:
            copy.wait_send()

    def keep_stats():
        parts[v] = stats_ref[...]

    send_all(stats_ref, parts, v, n_voc, voc_sems, along_voc, keep_stats)
    every = parts[...]
    quarter = every.shape[1] // 4
    peaks = every[:, :quarter]
    peak = jnp.max(peaks, axis=0)
    factor = jnp.exp(peaks - peak[None])
    total = jnp.sum(every[:, quarter:2 * quarter] * factor, axis=0)
    weighted = jnp.sum(every[:, 2 * quarter:3 * quarter] * factor, axis=0)
    picked = jnp.sum(every[:, 3 * quarter:], axis=0)
    log_total = peak + jnp.log(total)
    shape = peak.shape
    row = lax.broadcasted_iota(jnp.int32, shape, 0) * shape[1] + lax.broadcasted_iota(jnp.int32, shape, 1)
    live = row < count_ref[...]
    out_ref[g, :quarter] = jnp.where(live, picked - log_total, 0.0)
    out_ref[g, quarter:] = jnp.where(live, log_total - weighted / total, 0.0)
    send_all(out_ref.at[g], out_ref, g, n_grp, grp_sems, along_grp, lambda: None)


def exchange(stats, count, n_voc, n_grp):
    rows, lanes = stats.shape
    return pl.pallas_call(
        functools.partial(_exchange_kernel, n_voc, n_grp),
        out_shape=jax.ShapeDtypeStruct((n_grp, rows // 2, lanes), stats.dtype),
        in_specs=[pl.BlockSpec(memory_space=pltpu.VMEM)] * 2,
        out_specs=pl.BlockSpec(memory_space=pltpu.VMEM),
        scratch_shapes=[pltpu.VMEM((n_voc, rows, lanes), stats.dtype),
                        pltpu.SemaphoreType.DMA((2, n_voc)), pltpu.SemaphoreType.DMA((2, n_grp))],
        compiler_params=pltpu.CompilerParams(collective_id=0, has_side_effects=True),
    )(stats, count)


class _Ring:
    def __init__(self, pos, n, device, slot, own, sems, on_arrival=None, split=True):
        self.pos, self.n, self.device, self.slot, self.own = pos, n, device, slot, own
        self.sems = sems
        self.on_arrival = on_arrival
        self.split = split and n % 2 == 0
        self.counts = (n // 2, n // 2) if self.split else (n // 2, n - 1 - n // 2)
        self.steps = max(self.counts)
        self.copies = []
        self.next = 1

    def advance(self):
        if self.next <= self.steps:
            self.step(self.next)
            self.next += 1

    def _part(self, s, kind):
        return kind // 2 if self.split and s == self.steps else None

    def _origin(self, step, sign):
        return lax.rem(self.pos + sign * step + 2 * self.n, self.n)

    def _desc(self, src, origin, kind, s, target):
        return pltpu.make_async_remote_copy(
            src_ref=src, dst_ref=self.slot(origin, self._part(s, kind)),
            send_sem=self.sems.at[kind, s - 1], recv_sem=self.sems.at[kind + 1, s - 1],
            device_id=self.device(target), device_id_type=MESH,
        )

    def step(self, s):
        if s > self.steps:
            return
        for (kind, sign), count in zip(((0, 1), (2, -1)), self.counts):
            if s > count:
                continue
            target = self._origin(1, sign)
            origin = self._origin(s - 1, -sign)
            part = self._part(s, kind)
            if s == 1:
                src = self.own(part)
            else:
                self._desc(self.slot(origin), origin, kind, s - 1, target).wait_recv()
                if self.on_arrival is not None:
                    self.on_arrival(origin)
                src = self.slot(origin, part)
            copy = self._desc(src, origin, kind, s, target)
            copy.start()
            self.copies.append(copy)

    def finish_recv(self):
        while self.next <= self.steps:
            self.advance()
        if not self.steps:
            return
        last = []
        for (kind, sign), count in zip(((0, 1), (2, -1)), self.counts):
            if not count:
                continue
            origin = self._origin(count, -sign)
            view = self.slot(origin, self._part(count, kind))
            self._desc(view, origin, kind, count, self._origin(1, sign)).wait_recv()
            last.append(origin)
        if self.on_arrival is not None:
            for origin in last[:1] if self.split else last:
                self.on_arrival(origin)

    def finish_send(self):
        for copy in self.copies:
            copy.wait_send()


def _gather_kernel(n_x, n_z, n_y, rows_ref, head_ref, gain_ref, normed_out, head_out, rows_out,
                   local_sem, sems, pair_sems):
    me = lax.axis_index("grp")
    v = lax.axis_index("voc")
    x = me // n_z
    z = me % n_z
    y = v // 2
    c = v % 2
    partner = y * 2 + 1 - c
    half = head_ref.shape[0] * 5 // 8
    lo, hi = pl.ds(0, half), pl.ds(half, head_ref.shape[0] - half)
    width = rows_ref.shape[1]

    def cols(t):
        return pl.ds(pl.multiple_of(t * width, width), width)

    def along_x(t):
        return (t * n_z + z, v)

    def along_z(t):
        return (x * n_z + t, v)

    def along_y(t):
        return (me, t * 2 + c)

    barrier = pltpu.get_barrier_semaphore()
    neighbours = [along_x(lax.rem(x + 1, n_x)), along_x(lax.rem(x + n_x - 1, n_x)),
                  along_z(lax.rem(z + 1, n_z)), along_z(lax.rem(z + n_z - 1, n_z)),
                  along_y(lax.rem(y + 1, n_y)), along_y(lax.rem(y + n_y - 1, n_y)),
                  (me, partner)]
    for target in neighbours:
        pl.semaphore_signal(barrier, inc=1, device_id=target, device_id_type=MESH)
    pl.semaphore_wait(barrier, len(neighbours))

    def to_partner(src, t):
        return pltpu.make_async_remote_copy(
            src_ref=src, dst_ref=rows_out.at[:, cols(t * 2 + c)],
            send_sem=pair_sems.at[0, t], recv_sem=pair_sems.at[1, t],
            device_id=(me, partner), device_id_type=MESH,
        )

    pair_copies = []

    def forward(t):
        copy = to_partner(rows_out.at[:, cols(t * 2 + c)], t)
        copy.start()
        pair_copies.append(copy)

    own = pltpu.make_async_copy(head_ref, head_out.at[x, z], local_sem.at[0])
    own.start()
    copy = to_partner(rows_ref, y)
    copy.start()
    pair_copies.append(copy)
    rows_out[:, cols(v)] = rows_ref[...]
    def halves(size, start=0):
        return lambda part: pl.ds(start, size) if part is None else pl.ds(start + part * (size // 2), size // 2)

    rows_part = halves(rows_ref.shape[0])
    lo_part, hi_part = halves(half), halves(head_ref.shape[0] - half, half)
    x_part, z_part = halves(n_x), halves(n_z)
    rows = _Ring(y, n_y, along_y, lambda t, p=None: rows_out.at[rows_part(p), cols(t * 2 + c)],
                 lambda p: rows_ref.at[rows_part(p)], sems.at[4], forward)
    first_x = _Ring(x, n_x, along_x, lambda t, p=None: head_out.at[t, z, lo_part(p)],
                    lambda p: head_ref.at[lo_part(p)], sems.at[0], split=False)
    first_z = _Ring(z, n_z, along_z, lambda t, p=None: head_out.at[x, t, hi_part(p)],
                    lambda p: head_ref.at[hi_part(p)], sems.at[1], split=False)
    rows.advance()
    first_x.advance()
    first_z.advance()
    first_x.advance()
    first_z.advance()
    own.wait()
    first_x.finish_recv()
    second_z = _Ring(z, n_z, along_z, lambda t, p=None: head_out.at[x_part(p), t, lo],
                     lambda p: head_out.at[x_part(p), z, lo], sems.at[2])
    second_x = _Ring(x, n_x, along_x, lambda t, p=None: head_out.at[t, z_part(p), hi],
                     lambda p: head_out.at[x, z_part(p), hi], sems.at[3])
    second_z.advance()
    first_z.advance()
    rows.advance()
    first_z.advance()
    first_z.finish_recv()
    second_x.advance()
    rows.advance()
    second_z.advance()
    rows.advance()
    second_z.advance()
    rows.finish_recv()
    second_x.advance()
    second_z.advance()
    for t in range(n_y):
        other = t * 2 + 1 - c
        block = rows_out.at[:, cols(other)]
        pltpu.make_async_remote_copy(
            src_ref=block, dst_ref=block,
            send_sem=pair_sems.at[0, t], recv_sem=pair_sems.at[1, t],
            device_id=(me, partner), device_id_type=MESH,
        ).wait_recv()
    chunk = 64

    def norm_chunk(i, carry):
        start = pl.multiple_of(i * chunk, chunk)
        values = rows_out[pl.ds(start, chunk), :].astype(jnp.float32)
        scale = lax.rsqrt(jnp.mean(values * values, axis=1, keepdims=True) + EPSILON)
        normed_out[pl.ds(start, chunk), :] = (values * scale * gain_ref[...]).astype(normed_out.dtype)
        return carry

    lax.fori_loop(0, rows_out.shape[0] // chunk, norm_chunk, 0)
    second_z.finish_recv()
    second_x.finish_recv()
    for ring in (first_x, first_z, second_z, second_x, rows):
        ring.finish_send()
    for copy in pair_copies:
        copy.wait_send()


def gather_both(hidden, piece, norm_gain, n_x, n_z, n_voc):
    rows, width = hidden.shape
    depth, vocab = piece.shape
    n_y = n_voc // 2
    steps = max(n_x, n_z, n_y)
    gain = norm_gain.astype(jnp.float32)[None, :]
    full_rows, full_head = pl.pallas_call(
        functools.partial(_gather_kernel, n_x, n_z, n_y),
        out_shape=(jax.ShapeDtypeStruct((rows, width * n_voc), hidden.dtype),
                   jax.ShapeDtypeStruct((n_x, n_z, depth, vocab), piece.dtype)),
        in_specs=[pl.BlockSpec(memory_space=pltpu.VMEM)] * 3,
        out_specs=(pl.BlockSpec(memory_space=pltpu.VMEM), pl.BlockSpec(memory_space=pltpu.VMEM)),
        scratch_shapes=[pltpu.VMEM((rows, width * n_voc), hidden.dtype),
                        pltpu.SemaphoreType.DMA((1,)), pltpu.SemaphoreType.DMA((5, 4, steps)),
                        pltpu.SemaphoreType.DMA((2, n_y))],
        compiler_params=pltpu.CompilerParams(collective_id=3, has_side_effects=True),
    )(hidden, piece, gain)
    return full_rows, full_head.reshape(n_x * n_z * depth, vocab)


def local(hidden, targets, row_count, norm_gain, head_weight, return_from, *, n_voc, n_grp, n_x, n_z):
    tok_rows = hidden.shape[0]
    normed, piece = gather_both(hidden, head_weight, norm_gain, n_x, n_z, n_voc)
    vocab_local = head_weight.shape[1]
    logits = jnp.dot(normed, piece, preferred_element_type=jnp.float32)
    peak = jnp.max(logits, axis=1)
    shifted = jnp.exp(logits - peak[:, None])
    total = jnp.sum(shifted, axis=1)
    weighted = jnp.sum(shifted * logits, axis=1)
    global_columns = lax.axis_index("voc") * vocab_local + jnp.arange(vocab_local, dtype=jnp.int32)
    picked = jnp.sum(jnp.where(global_columns[None, :] == targets[:, None], logits, 0.0), axis=1)
    stats = jnp.stack([peak, total, weighted, picked])
    results = exchange(stats, row_count.reshape(1, 1), n_voc, n_grp).reshape(n_grp, 2, tok_rows)
    lanes = 128
    every = jnp.concatenate(
        [results[:, 0].reshape(-1, lanes), results[:, 1].reshape(-1, lanes)], axis=1)
    high = return_from // lanes
    low = return_from % lanes
    pick_row = (high[:, None] == jnp.arange(every.shape[0], dtype=jnp.int32)[None, :]).astype(jnp.float32)
    rows_picked = jnp.dot(pick_row, every, precision=lax.Precision.HIGHEST)
    pick_lane = low[:, None] == jnp.arange(lanes, dtype=jnp.int32)[None, :]
    token_logp = jnp.sum(jnp.where(pick_lane, rows_picked[:, :lanes], 0.0), axis=1)
    token_entropy = jnp.sum(jnp.where(pick_lane, rows_picked[:, lanes:], 0.0), axis=1)
    return (token_logp, token_entropy)


def solution(mesh):
    placed = (P("grp", "voc"), P("grp"), P("grp"), P(), P("grp", "voc"), P("grp"))
    n_grp = mesh.shape["grp"]
    n_z = len({device.coords[2] for device in mesh.devices[:, 0]})
    body = functools.partial(local, n_voc=mesh.shape["voc"], n_grp=n_grp, n_x=n_grp // n_z, n_z=n_z)
    return jax.shard_map(
        body, mesh=mesh, in_specs=placed, out_specs=(P("grp"), P("grp")), check_vma=False
    )
```

```python
import functools

import jax
import jax.numpy as jnp
from jax import lax
from jax.experimental import pallas as pl
from jax.experimental.pallas import tpu as pltpu
from jax.sharding import PartitionSpec as P

MESH = pl.DeviceIdType.MESH

EPSILON = 1e-05


def _exchange_kernel(n_voc, n_grp, stats_ref, count_ref, out_ref, parts, voc_sems, grp_sems):
    g = lax.axis_index("grp")
    v = lax.axis_index("voc")

    def along_voc(t):
        return (g, t)

    def along_grp(t):
        return (t, v)

    barrier = pltpu.get_barrier_semaphore()
    for k in range(1, n_voc):
        pl.semaphore_signal(barrier, inc=1, device_id=along_voc(lax.rem(v + k, n_voc)), device_id_type=MESH)
    for k in range(1, n_grp):
        pl.semaphore_signal(barrier, inc=1, device_id=along_grp(lax.rem(g + k, n_grp)), device_id_type=MESH)
    pl.semaphore_wait(barrier, n_voc + n_grp - 2)

    def send_all(src, buffer, me, n, sems, device, fill):
        copies = []
        for k in range(1, n):
            copy = pltpu.make_async_remote_copy(
                src_ref=src, dst_ref=buffer.at[me],
                send_sem=sems.at[0, k], recv_sem=sems.at[1, k],
                device_id=device(lax.rem(me + k, n)), device_id_type=MESH,
            )
            copy.start()
            copies.append(copy)
        fill()
        for k in range(1, n):
            source = lax.rem(me + n - k, n)
            pltpu.make_async_remote_copy(
                src_ref=src, dst_ref=buffer.at[source],
                send_sem=sems.at[0, k], recv_sem=sems.at[1, k],
                device_id=device(source), device_id_type=MESH,
            ).wait_recv()
        for copy in copies:
            copy.wait_send()

    def keep_stats():
        parts[v] = stats_ref[...]

    send_all(stats_ref, parts, v, n_voc, voc_sems, along_voc, keep_stats)
    every = parts[...]
    quarter = every.shape[1] // 4
    peaks = every[:, :quarter]
    peak = jnp.max(peaks, axis=0)
    factor = jnp.exp(peaks - peak[None])
    total = jnp.sum(every[:, quarter:2 * quarter] * factor, axis=0)
    weighted = jnp.sum(every[:, 2 * quarter:3 * quarter] * factor, axis=0)
    picked = jnp.sum(every[:, 3 * quarter:], axis=0)
    log_total = peak + jnp.log(total)
    shape = peak.shape
    row = lax.broadcasted_iota(jnp.int32, shape, 0) * shape[1] + lax.broadcasted_iota(jnp.int32, shape, 1)
    live = row < count_ref[...]
    out_ref[g, :quarter] = jnp.where(live, picked - log_total, 0.0)
    out_ref[g, quarter:] = jnp.where(live, log_total - weighted / total, 0.0)
    send_all(out_ref.at[g], out_ref, g, n_grp, grp_sems, along_grp, lambda: None)


def exchange(stats, count, n_voc, n_grp):
    rows, lanes = stats.shape
    return pl.pallas_call(
        functools.partial(_exchange_kernel, n_voc, n_grp),
        out_shape=jax.ShapeDtypeStruct((n_grp, rows // 2, lanes), stats.dtype),
        in_specs=[pl.BlockSpec(memory_space=pltpu.VMEM)] * 2,
        out_specs=pl.BlockSpec(memory_space=pltpu.VMEM),
        scratch_shapes=[pltpu.VMEM((n_voc, rows, lanes), stats.dtype),
                        pltpu.SemaphoreType.DMA((2, n_voc)), pltpu.SemaphoreType.DMA((2, n_grp))],
        compiler_params=pltpu.CompilerParams(collective_id=0, has_side_effects=True),
    )(stats, count)


class _Ring:
    def __init__(self, pos, n, device, slot, own, sems, on_arrival=None):
        self.pos, self.n, self.device, self.slot, self.own = pos, n, device, slot, own
        self.sems = sems
        self.on_arrival = on_arrival
        self.steps = n // 2
        self.split = n % 2 == 0
        self.copies = []
        self.next = 1

    def advance(self):
        if self.next <= self.steps:
            self.step(self.next)
            self.next += 1

    def _part(self, s, kind):
        return kind // 2 if self.split and s == self.steps else None

    def _origin(self, step, sign):
        return lax.rem(self.pos + sign * step + 2 * self.n, self.n)

    def _desc(self, src, origin, kind, s, target):
        return pltpu.make_async_remote_copy(
            src_ref=src, dst_ref=self.slot(origin, self._part(s, kind)),
            send_sem=self.sems.at[kind, s - 1], recv_sem=self.sems.at[kind + 1, s - 1],
            device_id=self.device(target), device_id_type=MESH,
        )

    def step(self, s):
        if s > self.steps:
            return
        for kind, sign in ((0, 1), (2, -1)):
            target = self._origin(1, sign)
            origin = self._origin(s - 1, -sign)
            part = self._part(s, kind)
            if s == 1:
                src = self.own(part)
            else:
                self._desc(self.slot(origin), origin, kind, s - 1, target).wait_recv()
                if self.on_arrival is not None:
                    self.on_arrival(origin)
                src = self.slot(origin, part)
            copy = self._desc(src, origin, kind, s, target)
            copy.start()
            self.copies.append(copy)

    def finish_recv(self):
        while self.next <= self.steps:
            self.advance()
        if not self.steps:
            return
        last = []
        for kind, sign in ((0, 1), (2, -1)):
            origin = self._origin(self.steps, -sign)
            view = self.slot(origin, self._part(self.steps, kind))
            self._desc(view, origin, kind, self.steps, self._origin(1, sign)).wait_recv()
            last.append(origin)
        if self.on_arrival is not None:
            for origin in last[:1] if self.split else last:
                self.on_arrival(origin)

    def finish_send(self):
        for copy in self.copies:
            copy.wait_send()


class _Direct:
    def __init__(self, pos, n, device, slot, own, sems):
        self.pos, self.n, self.device, self.slot, self.own = pos, n, device, slot, own
        self.sems = sems
        self.copies = []

    def _desc(self, src, origin, k, target):
        return pltpu.make_async_remote_copy(
            src_ref=src, dst_ref=self.slot(origin),
            send_sem=self.sems.at[0, k - 1], recv_sem=self.sems.at[1, k - 1],
            device_id=self.device(target), device_id_type=MESH,
        )

    def advance(self):
        if self.copies:
            return
        for k in range(1, self.n):
            copy = self._desc(self.own(None), self.pos, k, lax.rem(self.pos + k, self.n))
            copy.start()
            self.copies.append(copy)

    def finish_recv(self):
        self.advance()
        for k in range(1, self.n):
            origin = lax.rem(self.pos + self.n - k, self.n)
            self._desc(self.slot(origin), origin, k, origin).wait_recv()

    def finish_send(self):
        for copy in self.copies:
            copy.wait_send()


def _gather_kernel(n_x, n_z, n_y, rows_ref, head_ref, gain_ref, normed_out, head_out, rows_out,
                   local_sem, sems, pair_sems):
    me = lax.axis_index("grp")
    v = lax.axis_index("voc")
    x = me // n_z
    z = me % n_z
    y = v // 2
    c = v % 2
    partner = y * 2 + 1 - c
    half = head_ref.shape[0] // 2
    lo, hi = pl.ds(0, half), pl.ds(half, half)
    width = rows_ref.shape[1]

    def cols(t):
        return pl.ds(pl.multiple_of(t * width, width), width)

    def along_x(t):
        return (t * n_z + z, v)

    def along_z(t):
        return (x * n_z + t, v)

    def along_y(t):
        return (me, t * 2 + c)

    barrier = pltpu.get_barrier_semaphore()
    neighbours = ([along_x(lax.rem(x + k, n_x)) for k in range(1, n_x)]
                  + [along_z(lax.rem(z + k, n_z)) for k in range(1, n_z)]
                  + [along_y(lax.rem(y + 1, n_y)), along_y(lax.rem(y + n_y - 1, n_y)), (me, partner)])
    for target in neighbours:
        pl.semaphore_signal(barrier, inc=1, device_id=target, device_id_type=MESH)
    pl.semaphore_wait(barrier, len(neighbours))

    def to_partner(src, t):
        return pltpu.make_async_remote_copy(
            src_ref=src, dst_ref=rows_out.at[:, cols(t * 2 + c)],
            send_sem=pair_sems.at[0, t], recv_sem=pair_sems.at[1, t],
            device_id=(me, partner), device_id_type=MESH,
        )

    pair_copies = []

    def forward(t):
        copy = to_partner(rows_out.at[:, cols(t * 2 + c)], t)
        copy.start()
        pair_copies.append(copy)

    own = pltpu.make_async_copy(head_ref, head_out.at[x, z], local_sem.at[0])
    own.start()
    copy = to_partner(rows_ref, y)
    copy.start()
    pair_copies.append(copy)
    rows_out[:, cols(v)] = rows_ref[...]
    def halves(size, start=0):
        return lambda part: pl.ds(start, size) if part is None else pl.ds(start + part * (size // 2), size // 2)

    rows_part = halves(rows_ref.shape[0])
    x_part, z_part = halves(n_x), halves(n_z)
    rows = _Ring(y, n_y, along_y, lambda t, p=None: rows_out.at[rows_part(p), cols(t * 2 + c)],
                 lambda p: rows_ref.at[rows_part(p)], sems.at[4], forward)
    first_x = _Direct(x, n_x, along_x, lambda t: head_out.at[t, z, lo],
                      lambda p: head_ref.at[lo], sems.at[0])
    first_z = _Direct(z, n_z, along_z, lambda t: head_out.at[x, t, hi],
                      lambda p: head_ref.at[hi], sems.at[1])
    rows.advance()
    first_x.advance()
    first_z.advance()
    own.wait()
    first_x.finish_recv()
    second_z = _Ring(z, n_z, along_z, lambda t, p=None: head_out.at[x_part(p), t, lo],
                     lambda p: head_out.at[x_part(p), z, lo], sems.at[2])
    second_x = _Ring(x, n_x, along_x, lambda t, p=None: head_out.at[t, z_part(p), hi],
                     lambda p: head_out.at[x, z_part(p), hi], sems.at[3])
    second_z.advance()
    first_z.finish_recv()
    second_x.advance()
    rows.advance()
    second_z.advance()
    rows.advance()
    second_z.advance()
    rows.finish_recv()
    second_x.advance()
    second_z.advance()
    for t in range(n_y):
        other = t * 2 + 1 - c
        block = rows_out.at[:, cols(other)]
        pltpu.make_async_remote_copy(
            src_ref=block, dst_ref=block,
            send_sem=pair_sems.at[0, t], recv_sem=pair_sems.at[1, t],
            device_id=(me, partner), device_id_type=MESH,
        ).wait_recv()
    chunk = 64

    def norm_chunk(i, carry):
        start = pl.multiple_of(i * chunk, chunk)
        values = rows_out[pl.ds(start, chunk), :].astype(jnp.float32)
        scale = lax.rsqrt(jnp.mean(values * values, axis=1, keepdims=True) + EPSILON)
        normed_out[pl.ds(start, chunk), :] = (values * scale * gain_ref[...]).astype(normed_out.dtype)
        return carry

    lax.fori_loop(0, rows_out.shape[0] // chunk, norm_chunk, 0)
    second_z.finish_recv()
    second_x.finish_recv()
    for ring in (first_x, first_z, second_z, second_x, rows):
        ring.finish_send()
    for copy in pair_copies:
        copy.wait_send()


def gather_both(hidden, piece, norm_gain, n_x, n_z, n_voc):
    rows, width = hidden.shape
    depth, vocab = piece.shape
    n_y = n_voc // 2
    steps = max(n_x, n_z, n_y)
    gain = norm_gain.astype(jnp.float32)[None, :]
    full_rows, full_head = pl.pallas_call(
        functools.partial(_gather_kernel, n_x, n_z, n_y),
        out_shape=(jax.ShapeDtypeStruct((rows, width * n_voc), hidden.dtype),
                   jax.ShapeDtypeStruct((n_x, n_z, depth, vocab), piece.dtype)),
        in_specs=[pl.BlockSpec(memory_space=pltpu.VMEM)] * 3,
        out_specs=(pl.BlockSpec(memory_space=pltpu.VMEM), pl.BlockSpec(memory_space=pltpu.VMEM)),
        scratch_shapes=[pltpu.VMEM((rows, width * n_voc), hidden.dtype),
                        pltpu.SemaphoreType.DMA((1,)), pltpu.SemaphoreType.DMA((5, 4, steps)),
                        pltpu.SemaphoreType.DMA((2, n_y))],
        compiler_params=pltpu.CompilerParams(collective_id=3, has_side_effects=True),
    )(hidden, piece, gain)
    return full_rows, full_head.reshape(n_x * n_z * depth, vocab)


def local(hidden, targets, row_count, norm_gain, head_weight, return_from, *, n_voc, n_grp, n_x, n_z):
    tok_rows = hidden.shape[0]
    normed, piece = gather_both(hidden, head_weight, norm_gain, n_x, n_z, n_voc)
    vocab_local = head_weight.shape[1]
    logits = jnp.dot(normed, piece, preferred_element_type=jnp.float32)
    peak = jnp.max(logits, axis=1)
    shifted = jnp.exp(logits - peak[:, None])
    total = jnp.sum(shifted, axis=1)
    weighted = jnp.sum(shifted * logits, axis=1)
    global_columns = lax.axis_index("voc") * vocab_local + jnp.arange(vocab_local, dtype=jnp.int32)
    picked = jnp.sum(jnp.where(global_columns[None, :] == targets[:, None], logits, 0.0), axis=1)
    stats = jnp.stack([peak, total, weighted, picked])
    results = exchange(stats, row_count.reshape(1, 1), n_voc, n_grp).reshape(n_grp, 2, tok_rows)
    lanes = 128
    every = jnp.concatenate(
        [results[:, 0].reshape(-1, lanes), results[:, 1].reshape(-1, lanes)], axis=1)
    high = return_from // lanes
    low = return_from % lanes
    pick_row = (high[:, None] == jnp.arange(every.shape[0], dtype=jnp.int32)[None, :]).astype(jnp.float32)
    rows_picked = jnp.dot(pick_row, every, precision=lax.Precision.HIGHEST)
    pick_lane = low[:, None] == jnp.arange(lanes, dtype=jnp.int32)[None, :]
    token_logp = jnp.sum(jnp.where(pick_lane, rows_picked[:, :lanes], 0.0), axis=1)
    token_entropy = jnp.sum(jnp.where(pick_lane, rows_picked[:, lanes:], 0.0), axis=1)
    return (token_logp, token_entropy)


def solution(mesh):
    placed = (P("grp", "voc"), P("grp"), P("grp"), P(), P("grp", "voc"), P("grp"))
    n_grp = mesh.shape["grp"]
    n_z = len({device.coords[2] for device in mesh.devices[:, 0]})
    body = functools.partial(local, n_voc=mesh.shape["voc"], n_grp=n_grp, n_x=n_grp // n_z, n_z=n_z)
    return jax.shard_map(
        body, mesh=mesh, in_specs=placed, out_specs=(P("grp"), P("grp")), check_vma=False
    )
```

```python
import functools

import jax
import jax.numpy as jnp
from jax import lax
from jax.experimental import pallas as pl
from jax.experimental.pallas import tpu as pltpu
from jax.sharding import PartitionSpec as P

MESH = pl.DeviceIdType.MESH

EPSILON = 1e-05


def _exchange_kernel(n_voc, n_grp, peak_ref, total_ref, weighted_ref, picked_ref, count_ref, out_ref,
                     mine, parts, voc_sems, grp_sems):
    g = lax.axis_index("grp")
    v = lax.axis_index("voc")

    def along_voc(t):
        return (g, t)

    def along_grp(t):
        return (t, v)

    barrier = pltpu.get_barrier_semaphore()
    for k in range(1, n_voc):
        pl.semaphore_signal(barrier, inc=1, device_id=along_voc(lax.rem(v + k, n_voc)), device_id_type=MESH)
    for k in range(1, n_grp):
        pl.semaphore_signal(barrier, inc=1, device_id=along_grp(lax.rem(g + k, n_grp)), device_id_type=MESH)
    pl.semaphore_wait(barrier, n_voc + n_grp - 2)

    def send_all(src, buffer, me, n, sems, device, fill):
        copies = []
        for k in range(1, n):
            copy = pltpu.make_async_remote_copy(
                src_ref=src, dst_ref=buffer.at[me],
                send_sem=sems.at[0, k], recv_sem=sems.at[1, k],
                device_id=device(lax.rem(me + k, n)), device_id_type=MESH,
            )
            copy.start()
            copies.append(copy)
        fill()
        for k in range(1, n):
            source = lax.rem(me + n - k, n)
            pltpu.make_async_remote_copy(
                src_ref=src, dst_ref=buffer.at[source],
                send_sem=sems.at[0, k], recv_sem=sems.at[1, k],
                device_id=device(source), device_id_type=MESH,
            ).wait_recv()
        for copy in copies:
            copy.wait_send()

    for i, ref in enumerate((peak_ref, total_ref, weighted_ref, picked_ref)):
        mine[pl.ds(i, 1), :] = ref[...]

    def keep_stats():
        parts[v] = mine[...]

    send_all(mine, parts, v, n_voc, voc_sems, along_voc, keep_stats)
    every = parts[...]
    quarter = every.shape[1] // 4
    peaks = every[:, :quarter]
    peak = jnp.max(peaks, axis=0)
    factor = jnp.exp(peaks - peak[None])
    total = jnp.sum(every[:, quarter:2 * quarter] * factor, axis=0)
    weighted = jnp.sum(every[:, 2 * quarter:3 * quarter] * factor, axis=0)
    picked = jnp.sum(every[:, 3 * quarter:], axis=0)
    log_total = peak + jnp.log(total)
    shape = peak.shape
    row = lax.broadcasted_iota(jnp.int32, shape, 0) * shape[1] + lax.broadcasted_iota(jnp.int32, shape, 1)
    live = row < count_ref[...]
    out_ref[g, :quarter] = jnp.where(live, picked - log_total, 0.0)
    out_ref[g, quarter:] = jnp.where(live, log_total - weighted / total, 0.0)
    send_all(out_ref.at[g], out_ref, g, n_grp, grp_sems, along_grp, lambda: None)


def exchange(stats, count, n_voc, n_grp):
    rows, lanes = len(stats), stats[0].shape[1]
    dtype = stats[0].dtype
    return pl.pallas_call(
        functools.partial(_exchange_kernel, n_voc, n_grp),
        out_shape=jax.ShapeDtypeStruct((n_grp, rows // 2, lanes), dtype),
        in_specs=[pl.BlockSpec(memory_space=pltpu.VMEM)] * (rows + 1),
        out_specs=pl.BlockSpec(memory_space=pltpu.VMEM),
        scratch_shapes=[pltpu.VMEM((rows, lanes), dtype), pltpu.VMEM((n_voc, rows, lanes), dtype),
                        pltpu.SemaphoreType.DMA((2, n_voc)), pltpu.SemaphoreType.DMA((2, n_grp))],
        compiler_params=pltpu.CompilerParams(collective_id=0, has_side_effects=True),
    )(*stats, count)


class _Ring:
    def __init__(self, pos, n, device, slot, own, sems, on_arrival=None):
        self.pos, self.n, self.device, self.slot, self.own = pos, n, device, slot, own
        self.sems = sems
        self.on_arrival = on_arrival
        self.steps = n // 2
        self.split = n % 2 == 0
        self.copies = []
        self.next = 1

    def advance(self):
        if self.next <= self.steps:
            self.step(self.next)
            self.next += 1

    def _part(self, s, kind):
        return kind // 2 if self.split and s == self.steps else None

    def _origin(self, step, sign):
        return lax.rem(self.pos + sign * step + 2 * self.n, self.n)

    def _desc(self, src, origin, kind, s, target):
        return pltpu.make_async_remote_copy(
            src_ref=src, dst_ref=self.slot(origin, self._part(s, kind)),
            send_sem=self.sems.at[kind, s - 1], recv_sem=self.sems.at[kind + 1, s - 1],
            device_id=self.device(target), device_id_type=MESH,
        )

    def step(self, s):
        if s > self.steps:
            return
        for kind, sign in ((0, 1), (2, -1)):
            target = self._origin(1, sign)
            origin = self._origin(s - 1, -sign)
            part = self._part(s, kind)
            if s == 1:
                src = self.own(part)
            else:
                self._desc(self.slot(origin), origin, kind, s - 1, target).wait_recv()
                if self.on_arrival is not None:
                    self.on_arrival(origin)
                src = self.slot(origin, part)
            copy = self._desc(src, origin, kind, s, target)
            copy.start()
            self.copies.append(copy)

    def finish_recv(self):
        while self.next <= self.steps:
            self.advance()
        if not self.steps:
            return
        last = []
        for kind, sign in ((0, 1), (2, -1)):
            origin = self._origin(self.steps, -sign)
            view = self.slot(origin, self._part(self.steps, kind))
            self._desc(view, origin, kind, self.steps, self._origin(1, sign)).wait_recv()
            last.append(origin)
        if self.on_arrival is not None:
            for origin in last[:1] if self.split else last:
                self.on_arrival(origin)

    def finish_send(self):
        for copy in self.copies:
            copy.wait_send()


def _gather_kernel(n_x, n_z, n_y, rows_ref, head_ref, gain_ref, normed_out, head_out, rows_out,
                   local_sem, sems, pair_sems):
    me = lax.axis_index("grp")
    v = lax.axis_index("voc")
    x = me // n_z
    z = me % n_z
    y = v // 2
    c = v % 2
    partner = y * 2 + 1 - c
    half = head_ref.shape[0] // 2
    lo, hi = pl.ds(0, half), pl.ds(half, half)
    width = rows_ref.shape[1]

    def cols(t):
        return pl.ds(pl.multiple_of(t * width, width), width)

    def along_x(t):
        return (t * n_z + z, v)

    def along_z(t):
        return (x * n_z + t, v)

    def along_y(t):
        return (me, t * 2 + c)

    barrier = pltpu.get_barrier_semaphore()
    neighbours = [along_x(lax.rem(x + 1, n_x)), along_x(lax.rem(x + n_x - 1, n_x)),
                  along_z(lax.rem(z + 1, n_z)), along_z(lax.rem(z + n_z - 1, n_z)),
                  along_y(lax.rem(y + 1, n_y)), along_y(lax.rem(y + n_y - 1, n_y)),
                  (me, partner)]
    for target in neighbours:
        pl.semaphore_signal(barrier, inc=1, device_id=target, device_id_type=MESH)
    pl.semaphore_wait(barrier, len(neighbours))

    def to_partner(src, t):
        return pltpu.make_async_remote_copy(
            src_ref=src, dst_ref=rows_out.at[:, cols(t * 2 + c)],
            send_sem=pair_sems.at[0, t], recv_sem=pair_sems.at[1, t],
            device_id=(me, partner), device_id_type=MESH,
        )

    pair_copies = []

    def forward(t):
        copy = to_partner(rows_out.at[:, cols(t * 2 + c)], t)
        copy.start()
        pair_copies.append(copy)

    own = pltpu.make_async_copy(head_ref, head_out.at[x, z], local_sem.at[0])
    own.start()
    copy = to_partner(rows_ref, y)
    copy.start()
    pair_copies.append(copy)
    rows_out[:, cols(v)] = rows_ref[...]
    def halves(size, start=0):
        return lambda part: pl.ds(start, size) if part is None else pl.ds(start + part * (size // 2), size // 2)

    rows_part = halves(rows_ref.shape[0])
    lo_part, hi_part = halves(half), halves(half, half)
    x_part, z_part = halves(n_x), halves(n_z)
    rows = _Ring(y, n_y, along_y, lambda t, p=None: rows_out.at[rows_part(p), cols(t * 2 + c)],
                 lambda p: rows_ref.at[rows_part(p)], sems.at[4], forward)
    first_x = _Ring(x, n_x, along_x, lambda t, p=None: head_out.at[t, z, lo_part(p)],
                    lambda p: head_ref.at[lo_part(p)], sems.at[0])
    first_z = _Ring(z, n_z, along_z, lambda t, p=None: head_out.at[x, t, hi_part(p)],
                    lambda p: head_ref.at[hi_part(p)], sems.at[1])
    rows.advance()
    first_x.advance()
    first_z.advance()
    first_x.advance()
    first_z.advance()
    own.wait()
    first_x.finish_recv()
    second_z = _Ring(z, n_z, along_z, lambda t, p=None: head_out.at[x_part(p), t, lo],
                     lambda p: head_out.at[x_part(p), z, lo], sems.at[2])
    second_x = _Ring(x, n_x, along_x, lambda t, p=None: head_out.at[t, z_part(p), hi],
                     lambda p: head_out.at[x, z_part(p), hi], sems.at[3])
    second_z.advance()
    first_z.advance()
    rows.advance()
    first_z.advance()
    first_z.finish_recv()
    second_x.advance()
    rows.advance()
    second_z.advance()
    rows.advance()
    second_z.advance()
    rows.finish_recv()
    second_x.advance()
    second_z.advance()
    for t in range(n_y):
        other = t * 2 + 1 - c
        block = rows_out.at[:, cols(other)]
        pltpu.make_async_remote_copy(
            src_ref=block, dst_ref=block,
            send_sem=pair_sems.at[0, t], recv_sem=pair_sems.at[1, t],
            device_id=(me, partner), device_id_type=MESH,
        ).wait_recv()
    chunk = 64

    def norm_chunk(i, carry):
        start = pl.multiple_of(i * chunk, chunk)
        values = rows_out[pl.ds(start, chunk), :].astype(jnp.float32)
        scale = lax.rsqrt(jnp.mean(values * values, axis=1, keepdims=True) + EPSILON)
        normed_out[pl.ds(start, chunk), :] = (values * scale * gain_ref[...]).astype(normed_out.dtype)
        return carry

    lax.fori_loop(0, rows_out.shape[0] // chunk, norm_chunk, 0)
    second_z.finish_recv()
    second_x.finish_recv()
    for ring in (first_x, first_z, second_z, second_x, rows):
        ring.finish_send()
    for copy in pair_copies:
        copy.wait_send()


def gather_both(hidden, piece, norm_gain, n_x, n_z, n_voc):
    rows, width = hidden.shape
    depth, vocab = piece.shape
    n_y = n_voc // 2
    steps = max(n_x, n_z, n_y)
    gain = norm_gain.astype(jnp.float32)[None, :]
    full_rows, full_head = pl.pallas_call(
        functools.partial(_gather_kernel, n_x, n_z, n_y),
        out_shape=(jax.ShapeDtypeStruct((rows, width * n_voc), hidden.dtype),
                   jax.ShapeDtypeStruct((n_x, n_z, depth, vocab), piece.dtype)),
        in_specs=[pl.BlockSpec(memory_space=pltpu.VMEM)] * 3,
        out_specs=(pl.BlockSpec(memory_space=pltpu.VMEM), pl.BlockSpec(memory_space=pltpu.VMEM)),
        scratch_shapes=[pltpu.VMEM((rows, width * n_voc), hidden.dtype),
                        pltpu.SemaphoreType.DMA((1,)), pltpu.SemaphoreType.DMA((5, 4, steps)),
                        pltpu.SemaphoreType.DMA((2, n_y))],
        compiler_params=pltpu.CompilerParams(collective_id=3, has_side_effects=True),
    )(hidden, piece, gain)
    return full_rows, full_head.reshape(n_x * n_z * depth, vocab)


def local(hidden, targets, row_count, norm_gain, head_weight, return_from, *, n_voc, n_grp, n_x, n_z):
    tok_rows = hidden.shape[0]
    normed, piece = gather_both(hidden, head_weight, norm_gain, n_x, n_z, n_voc)
    vocab_local = head_weight.shape[1]
    logits = jnp.dot(normed, piece, preferred_element_type=jnp.float32)
    peak = jnp.max(logits, axis=1)
    shifted = jnp.exp(logits - peak[:, None])
    total = jnp.sum(shifted, axis=1)
    weighted = jnp.sum(shifted * logits, axis=1)
    global_columns = lax.axis_index("voc") * vocab_local + jnp.arange(vocab_local, dtype=jnp.int32)
    picked = jnp.sum(jnp.where(global_columns[None, :] == targets[:, None], logits, 0.0), axis=1)
    stats = [part[None, :] for part in (peak, total, weighted, picked)]
    results = exchange(stats, row_count.reshape(1, 1), n_voc, n_grp).reshape(n_grp, 2, tok_rows)
    lanes = 128
    every = jnp.concatenate(
        [results[:, 0].reshape(-1, lanes), results[:, 1].reshape(-1, lanes)], axis=1)
    high = return_from // lanes
    low = return_from % lanes
    pick_row = (high[:, None] == jnp.arange(every.shape[0], dtype=jnp.int32)[None, :]).astype(jnp.float32)
    rows_picked = jnp.dot(pick_row, every, precision=lax.Precision.HIGHEST)
    pick_lane = low[:, None] == jnp.arange(lanes, dtype=jnp.int32)[None, :]
    token_logp = jnp.sum(jnp.where(pick_lane, rows_picked[:, :lanes], 0.0), axis=1)
    token_entropy = jnp.sum(jnp.where(pick_lane, rows_picked[:, lanes:], 0.0), axis=1)
    return (token_logp, token_entropy)


def solution(mesh):
    placed = (P("grp", "voc"), P("grp"), P("grp"), P(), P("grp", "voc"), P("grp"))
    n_grp = mesh.shape["grp"]
    n_z = len({device.coords[2] for device in mesh.devices[:, 0]})
    body = functools.partial(local, n_voc=mesh.shape["voc"], n_grp=n_grp, n_x=n_grp // n_z, n_z=n_z)
    return jax.shard_map(
        body, mesh=mesh, in_specs=placed, out_specs=(P("grp"), P("grp")), check_vma=False
    )
```

```python
import functools

import jax
import jax.numpy as jnp
from jax import lax
from jax.experimental import pallas as pl
from jax.experimental.pallas import tpu as pltpu
from jax.sharding import PartitionSpec as P

MESH = pl.DeviceIdType.MESH

EPSILON = 1e-05


def _exchange_kernel(n_voc, n_grp, stats_ref, count_ref, out_ref, parts, voc_sems, grp_sems):
    g = lax.axis_index("grp")
    v = lax.axis_index("voc")

    def along_voc(t):
        return (g, t)

    def along_grp(t):
        return (t, v)

    barrier = pltpu.get_barrier_semaphore()
    for k in range(1, n_voc):
        pl.semaphore_signal(barrier, inc=1, device_id=along_voc(lax.rem(v + k, n_voc)), device_id_type=MESH)
    for k in range(1, n_grp):
        pl.semaphore_signal(barrier, inc=1, device_id=along_grp(lax.rem(g + k, n_grp)), device_id_type=MESH)
    pl.semaphore_wait(barrier, n_voc + n_grp - 2)

    def send_all(src, buffer, me, n, sems, device, fill):
        copies = []
        for k in range(1, n):
            copy = pltpu.make_async_remote_copy(
                src_ref=src, dst_ref=buffer.at[me],
                send_sem=sems.at[0, k], recv_sem=sems.at[1, k],
                device_id=device(lax.rem(me + k, n)), device_id_type=MESH,
            )
            copy.start()
            copies.append(copy)
        fill()
        for k in range(1, n):
            source = lax.rem(me + n - k, n)
            pltpu.make_async_remote_copy(
                src_ref=src, dst_ref=buffer.at[source],
                send_sem=sems.at[0, k], recv_sem=sems.at[1, k],
                device_id=device(source), device_id_type=MESH,
            ).wait_recv()
        for copy in copies:
            copy.wait_send()

    def keep_stats():
        parts[v] = stats_ref[...]

    send_all(stats_ref, parts, v, n_voc, voc_sems, along_voc, keep_stats)
    every = parts[...]
    quarter = every.shape[1] // 4
    peaks = every[:, :quarter]
    peak = jnp.max(peaks, axis=0)
    factor = jnp.exp(peaks - peak[None])
    total = jnp.sum(every[:, quarter:2 * quarter] * factor, axis=0)
    weighted = jnp.sum(every[:, 2 * quarter:3 * quarter] * factor, axis=0)
    picked = jnp.sum(every[:, 3 * quarter:], axis=0)
    log_total = peak + jnp.log(total)
    shape = peak.shape
    row = lax.broadcasted_iota(jnp.int32, shape, 0) * shape[1] + lax.broadcasted_iota(jnp.int32, shape, 1)
    live = row < count_ref[...]
    out_ref[g, :quarter] = jnp.where(live, picked - log_total, 0.0)
    out_ref[g, quarter:] = jnp.where(live, log_total - weighted / total, 0.0)
    send_all(out_ref.at[g], out_ref, g, n_grp, grp_sems, along_grp, lambda: None)


def exchange(stats, count, n_voc, n_grp):
    rows, lanes = stats.shape
    return pl.pallas_call(
        functools.partial(_exchange_kernel, n_voc, n_grp),
        out_shape=jax.ShapeDtypeStruct((n_grp, rows // 2, lanes), stats.dtype),
        in_specs=[pl.BlockSpec(memory_space=pltpu.VMEM)] * 2,
        out_specs=pl.BlockSpec(memory_space=pltpu.VMEM),
        scratch_shapes=[pltpu.VMEM((n_voc, rows, lanes), stats.dtype),
                        pltpu.SemaphoreType.DMA((2, n_voc)), pltpu.SemaphoreType.DMA((2, n_grp))],
        compiler_params=pltpu.CompilerParams(collective_id=0, has_side_effects=True),
    )(stats, count)


class _Ring:
    def __init__(self, pos, n, device, slot, own, sems, on_arrival=None):
        self.pos, self.n, self.device, self.slot, self.own = pos, n, device, slot, own
        self.sems = sems
        self.on_arrival = on_arrival
        self.steps = n // 2
        self.split = n % 2 == 0
        self.copies = []
        self.next = 1

    def advance(self):
        if self.next <= self.steps:
            self.step(self.next)
            self.next += 1

    def _part(self, s, kind):
        return kind // 2 if self.split and s == self.steps else None

    def _origin(self, step, sign):
        return lax.rem(self.pos + sign * step + 2 * self.n, self.n)

    def _desc(self, src, origin, kind, s, target):
        return pltpu.make_async_remote_copy(
            src_ref=src, dst_ref=self.slot(origin, self._part(s, kind)),
            send_sem=self.sems.at[kind, s - 1], recv_sem=self.sems.at[kind + 1, s - 1],
            device_id=self.device(target), device_id_type=MESH,
        )

    def step(self, s):
        if s > self.steps:
            return
        for kind, sign in ((0, 1), (2, -1)):
            target = self._origin(1, sign)
            origin = self._origin(s - 1, -sign)
            part = self._part(s, kind)
            if s == 1:
                src = self.own(part)
            else:
                self._desc(self.slot(origin), origin, kind, s - 1, target).wait_recv()
                if self.on_arrival is not None:
                    self.on_arrival(origin)
                src = self.slot(origin, part)
            copy = self._desc(src, origin, kind, s, target)
            copy.start()
            self.copies.append(copy)

    def finish_recv(self):
        while self.next <= self.steps:
            self.advance()
        if not self.steps:
            return
        last = []
        for kind, sign in ((0, 1), (2, -1)):
            origin = self._origin(self.steps, -sign)
            view = self.slot(origin, self._part(self.steps, kind))
            self._desc(view, origin, kind, self.steps, self._origin(1, sign)).wait_recv()
            last.append(origin)
        if self.on_arrival is not None:
            for origin in last[:1] if self.split else last:
                self.on_arrival(origin)

    def finish_send(self):
        for copy in self.copies:
            copy.wait_send()


def _gather_kernel(n_x, n_z, n_y, rows_ref, head_ref, gain_ref, normed_out, head_out, rows_out,
                   local_sem, sems, pair_sems):
    me = lax.axis_index("grp")
    v = lax.axis_index("voc")
    x = me // n_z
    z = me % n_z
    y = v // 2
    c = v % 2
    partner = y * 2 + 1 - c
    half = head_ref.shape[0] // 2
    lo, hi = pl.ds(0, half), pl.ds(half, half)
    width = rows_ref.shape[1]

    def cols(t):
        return pl.ds(pl.multiple_of(t * width, width), width)

    def along_x(t):
        return (t * n_z + z, v)

    def along_z(t):
        return (x * n_z + t, v)

    def along_y(t):
        return (me, t * 2 + c)

    barrier = pltpu.get_barrier_semaphore()
    neighbours = [along_x(lax.rem(x + 1, n_x)), along_x(lax.rem(x + n_x - 1, n_x)),
                  along_z(lax.rem(z + 1, n_z)), along_z(lax.rem(z + n_z - 1, n_z)),
                  along_y(lax.rem(y + 1, n_y)), along_y(lax.rem(y + n_y - 1, n_y)),
                  (me, partner)]
    for target in neighbours:
        pl.semaphore_signal(barrier, inc=1, device_id=target, device_id_type=MESH)
    pl.semaphore_wait(barrier, len(neighbours))

    def to_partner(src, t):
        return pltpu.make_async_remote_copy(
            src_ref=src, dst_ref=rows_out.at[:, cols(t * 2 + c)],
            send_sem=pair_sems.at[0, t], recv_sem=pair_sems.at[1, t],
            device_id=(me, partner), device_id_type=MESH,
        )

    pair_copies = []

    def forward(t):
        copy = to_partner(rows_out.at[:, cols(t * 2 + c)], t)
        copy.start()
        pair_copies.append(copy)

    own = pltpu.make_async_copy(head_ref, head_out.at[x, z], local_sem.at[0])
    own.start()
    copy = to_partner(rows_ref, y)
    copy.start()
    pair_copies.append(copy)
    own_rows = pltpu.make_async_copy(rows_ref, rows_out.at[:, cols(v)], local_sem.at[1])
    own_rows.start()
    def halves(size, start=0):
        return lambda part: pl.ds(start, size) if part is None else pl.ds(start + part * (size // 2), size // 2)

    rows_part = halves(rows_ref.shape[0])
    lo_part, hi_part = halves(half), halves(half, half)
    x_part, z_part = halves(n_x), halves(n_z)
    rows = _Ring(y, n_y, along_y, lambda t, p=None: rows_out.at[rows_part(p), cols(t * 2 + c)],
                 lambda p: rows_ref.at[rows_part(p)], sems.at[4], forward)
    first_x = _Ring(x, n_x, along_x, lambda t, p=None: head_out.at[t, z, lo_part(p)],
                    lambda p: head_ref.at[lo_part(p)], sems.at[0])
    first_z = _Ring(z, n_z, along_z, lambda t, p=None: head_out.at[x, t, hi_part(p)],
                    lambda p: head_ref.at[hi_part(p)], sems.at[1])
    rows.advance()
    first_x.advance()
    first_z.advance()
    first_x.advance()
    first_z.advance()
    own.wait()
    first_x.finish_recv()
    second_z = _Ring(z, n_z, along_z, lambda t, p=None: head_out.at[x_part(p), t, lo],
                     lambda p: head_out.at[x_part(p), z, lo], sems.at[2])
    second_x = _Ring(x, n_x, along_x, lambda t, p=None: head_out.at[t, z_part(p), hi],
                     lambda p: head_out.at[x, z_part(p), hi], sems.at[3])
    second_z.advance()
    first_z.advance()
    rows.advance()
    first_z.advance()
    first_z.finish_recv()
    second_x.advance()
    rows.advance()
    second_z.advance()
    rows.advance()
    second_z.advance()
    rows.finish_recv()
    second_x.advance()
    second_z.advance()
    for t in range(n_y):
        other = t * 2 + 1 - c
        block = rows_out.at[:, cols(other)]
        pltpu.make_async_remote_copy(
            src_ref=block, dst_ref=block,
            send_sem=pair_sems.at[0, t], recv_sem=pair_sems.at[1, t],
            device_id=(me, partner), device_id_type=MESH,
        ).wait_recv()
    own_rows.wait()
    chunk = 64

    def norm_chunk(i, carry):
        start = pl.multiple_of(i * chunk, chunk)
        values = rows_out[pl.ds(start, chunk), :].astype(jnp.float32)
        scale = lax.rsqrt(jnp.mean(values * values, axis=1, keepdims=True) + EPSILON)
        normed_out[pl.ds(start, chunk), :] = (values * scale * gain_ref[...]).astype(normed_out.dtype)
        return carry

    lax.fori_loop(0, rows_out.shape[0] // chunk, norm_chunk, 0)
    second_z.finish_recv()
    second_x.finish_recv()
    for ring in (first_x, first_z, second_z, second_x, rows):
        ring.finish_send()
    for copy in pair_copies:
        copy.wait_send()


def gather_both(hidden, piece, norm_gain, n_x, n_z, n_voc):
    rows, width = hidden.shape
    depth, vocab = piece.shape
    n_y = n_voc // 2
    steps = max(n_x, n_z, n_y)
    gain = norm_gain.astype(jnp.float32)[None, :]
    full_rows, full_head = pl.pallas_call(
        functools.partial(_gather_kernel, n_x, n_z, n_y),
        out_shape=(jax.ShapeDtypeStruct((rows, width * n_voc), hidden.dtype),
                   jax.ShapeDtypeStruct((n_x, n_z, depth, vocab), piece.dtype)),
        in_specs=[pl.BlockSpec(memory_space=pltpu.VMEM)] * 3,
        out_specs=(pl.BlockSpec(memory_space=pltpu.VMEM), pl.BlockSpec(memory_space=pltpu.VMEM)),
        scratch_shapes=[pltpu.VMEM((rows, width * n_voc), hidden.dtype),
                        pltpu.SemaphoreType.DMA((2,)), pltpu.SemaphoreType.DMA((5, 4, steps)),
                        pltpu.SemaphoreType.DMA((2, n_y))],
        compiler_params=pltpu.CompilerParams(collective_id=3, has_side_effects=True),
    )(hidden, piece, gain)
    return full_rows, full_head.reshape(n_x * n_z * depth, vocab)


def local(hidden, targets, row_count, norm_gain, head_weight, return_from, *, n_voc, n_grp, n_x, n_z):
    tok_rows = hidden.shape[0]
    normed, piece = gather_both(hidden, head_weight, norm_gain, n_x, n_z, n_voc)
    vocab_local = head_weight.shape[1]
    logits = jnp.dot(normed, piece, preferred_element_type=jnp.float32)
    peak = jnp.max(logits, axis=1)
    shifted = jnp.exp(logits - peak[:, None])
    total = jnp.sum(shifted, axis=1)
    weighted = jnp.sum(shifted * logits, axis=1)
    global_columns = lax.axis_index("voc") * vocab_local + jnp.arange(vocab_local, dtype=jnp.int32)
    picked = jnp.sum(jnp.where(global_columns[None, :] == targets[:, None], logits, 0.0), axis=1)
    stats = jnp.stack([peak, total, weighted, picked])
    results = exchange(stats, row_count.reshape(1, 1), n_voc, n_grp).reshape(n_grp, 2, tok_rows)
    lanes = 128
    every = jnp.concatenate(
        [results[:, 0].reshape(-1, lanes), results[:, 1].reshape(-1, lanes)], axis=1)
    high = return_from // lanes
    low = return_from % lanes
    pick_row = (high[:, None] == jnp.arange(every.shape[0], dtype=jnp.int32)[None, :]).astype(jnp.float32)
    rows_picked = jnp.dot(pick_row, every, precision=lax.Precision.HIGHEST)
    pick_lane = low[:, None] == jnp.arange(lanes, dtype=jnp.int32)[None, :]
    token_logp = jnp.sum(jnp.where(pick_lane, rows_picked[:, :lanes], 0.0), axis=1)
    token_entropy = jnp.sum(jnp.where(pick_lane, rows_picked[:, lanes:], 0.0), axis=1)
    return (token_logp, token_entropy)


def solution(mesh):
    placed = (P("grp", "voc"), P("grp"), P("grp"), P(), P("grp", "voc"), P("grp"))
    n_grp = mesh.shape["grp"]
    n_z = len({device.coords[2] for device in mesh.devices[:, 0]})
    body = functools.partial(local, n_voc=mesh.shape["voc"], n_grp=n_grp, n_x=n_grp // n_z, n_z=n_z)
    return jax.shard_map(
        body, mesh=mesh, in_specs=placed, out_specs=(P("grp"), P("grp")), check_vma=False
    )
```

```python
import functools

import jax
import jax.numpy as jnp
from jax import lax
from jax.experimental import pallas as pl
from jax.experimental.pallas import tpu as pltpu
from jax.sharding import PartitionSpec as P

MESH = pl.DeviceIdType.MESH

EPSILON = 1e-05


def _exchange_kernel(n_voc, n_grp, stats_ref, count_ref, out_ref, parts, voc_sems, grp_sems):
    g = lax.axis_index("grp")
    v = lax.axis_index("voc")

    def along_voc(t):
        return (g, t)

    def along_grp(t):
        return (t, v)

    barrier = pltpu.get_barrier_semaphore()
    for k in range(1, n_voc):
        pl.semaphore_signal(barrier, inc=1, device_id=along_voc(lax.rem(v + k, n_voc)), device_id_type=MESH)
    for k in range(1, n_grp):
        pl.semaphore_signal(barrier, inc=1, device_id=along_grp(lax.rem(g + k, n_grp)), device_id_type=MESH)
    pl.semaphore_wait(barrier, n_voc + n_grp - 2)

    def send_all(src, buffer, me, n, sems, device, fill):
        copies = []
        for k in range(1, n):
            copy = pltpu.make_async_remote_copy(
                src_ref=src, dst_ref=buffer.at[me],
                send_sem=sems.at[0, k], recv_sem=sems.at[1, k],
                device_id=device(lax.rem(me + k, n)), device_id_type=MESH,
            )
            copy.start()
            copies.append(copy)
        fill()
        for k in range(1, n):
            source = lax.rem(me + n - k, n)
            pltpu.make_async_remote_copy(
                src_ref=src, dst_ref=buffer.at[source],
                send_sem=sems.at[0, k], recv_sem=sems.at[1, k],
                device_id=device(source), device_id_type=MESH,
            ).wait_recv()
        for copy in copies:
            copy.wait_send()

    def keep_stats():
        parts[v] = stats_ref[...]

    send_all(stats_ref, parts, v, n_voc, voc_sems, along_voc, keep_stats)
    every = parts[...]
    quarter = every.shape[1] // 4
    peaks = every[:, :quarter]
    peak = jnp.max(peaks, axis=0)
    factor = jnp.exp(peaks - peak[None])
    total = jnp.sum(every[:, quarter:2 * quarter] * factor, axis=0)
    weighted = jnp.sum(every[:, 2 * quarter:3 * quarter] * factor, axis=0)
    picked = jnp.sum(every[:, 3 * quarter:], axis=0)
    log_total = peak + jnp.log(total)
    shape = peak.shape
    row = lax.broadcasted_iota(jnp.int32, shape, 0) * shape[1] + lax.broadcasted_iota(jnp.int32, shape, 1)
    live = row < count_ref[...]
    out_ref[g, :quarter] = jnp.where(live, picked - log_total, 0.0)
    out_ref[g, quarter:] = jnp.where(live, log_total - weighted / total, 0.0)
    send_all(out_ref.at[g], out_ref, g, n_grp, grp_sems, along_grp, lambda: None)


def exchange(stats, count, n_voc, n_grp):
    rows, lanes = stats.shape
    return pl.pallas_call(
        functools.partial(_exchange_kernel, n_voc, n_grp),
        out_shape=jax.ShapeDtypeStruct((n_grp, rows // 2, lanes), stats.dtype),
        in_specs=[pl.BlockSpec(memory_space=pltpu.VMEM)] * 2,
        out_specs=pl.BlockSpec(memory_space=pltpu.VMEM),
        scratch_shapes=[pltpu.VMEM((n_voc, rows, lanes), stats.dtype),
                        pltpu.SemaphoreType.DMA((2, n_voc)), pltpu.SemaphoreType.DMA((2, n_grp))],
        compiler_params=pltpu.CompilerParams(collective_id=0, has_side_effects=True),
    )(stats, count)


class _Ring:
    def __init__(self, pos, n, device, slot, own, sems, on_arrival=None):
        self.pos, self.n, self.device, self.slot, self.own = pos, n, device, slot, own
        self.sems = sems
        self.on_arrival = on_arrival
        self.steps = n // 2
        self.split = n % 2 == 0
        self.copies = []
        self.next = 1

    def advance(self):
        if self.next <= self.steps:
            self.step(self.next)
            self.next += 1

    def _part(self, s, kind):
        return kind // 2 if self.split and s == self.steps else None

    def _origin(self, step, sign):
        return lax.rem(self.pos + sign * step + 2 * self.n, self.n)

    def _desc(self, src, origin, kind, s, target):
        return pltpu.make_async_remote_copy(
            src_ref=src, dst_ref=self.slot(origin, self._part(s, kind)),
            send_sem=self.sems.at[kind, s - 1], recv_sem=self.sems.at[kind + 1, s - 1],
            device_id=self.device(target), device_id_type=MESH,
        )

    def step(self, s):
        if s > self.steps:
            return
        for kind, sign in ((0, 1), (2, -1)):
            target = self._origin(1, sign)
            origin = self._origin(s - 1, -sign)
            part = self._part(s, kind)
            if s == 1:
                src = self.own(part)
            else:
                self._desc(self.slot(origin), origin, kind, s - 1, target).wait_recv()
                if self.on_arrival is not None:
                    self.on_arrival(origin)
                src = self.slot(origin, part)
            copy = self._desc(src, origin, kind, s, target)
            copy.start()
            self.copies.append(copy)

    def finish_recv(self):
        while self.next <= self.steps:
            self.advance()
        if not self.steps:
            return
        last = []
        for kind, sign in ((0, 1), (2, -1)):
            origin = self._origin(self.steps, -sign)
            view = self.slot(origin, self._part(self.steps, kind))
            self._desc(view, origin, kind, self.steps, self._origin(1, sign)).wait_recv()
            last.append(origin)
        if self.on_arrival is not None:
            for origin in last[:1] if self.split else last:
                self.on_arrival(origin)

    def finish_send(self):
        for copy in self.copies:
            copy.wait_send()


def _gather_kernel(n_x, n_z, n_y, rows_ref, head_ref, gain_ref, normed_out, head_out, rows_out,
                   local_sem, sems, pair_sems):
    me = lax.axis_index("grp")
    v = lax.axis_index("voc")
    x = me // n_z
    z = me % n_z
    y = v // 2
    c = v % 2
    partner = y * 2 + 1 - c
    half = head_ref.shape[0] // 2
    lo, hi = pl.ds(0, half), pl.ds(half, half)
    width = rows_ref.shape[1]

    def cols(t):
        return pl.ds(pl.multiple_of(t * width, width), width)

    def along_x(t):
        return (t * n_z + z, v)

    def along_z(t):
        return (x * n_z + t, v)

    def along_y(t):
        return (me, t * 2 + c)

    barrier = pltpu.get_barrier_semaphore()
    neighbours = [along_x(lax.rem(x + 1, n_x)), along_x(lax.rem(x + n_x - 1, n_x)),
                  along_z(lax.rem(z + 1, n_z)), along_z(lax.rem(z + n_z - 1, n_z)),
                  along_y(lax.rem(y + 1, n_y)), along_y(lax.rem(y + n_y - 1, n_y)),
                  (me, partner)]
    for target in neighbours:
        pl.semaphore_signal(barrier, inc=1, device_id=target, device_id_type=MESH)
    pl.semaphore_wait(barrier, len(neighbours))

    def to_partner(src, t):
        return pltpu.make_async_remote_copy(
            src_ref=src, dst_ref=rows_out.at[:, cols(t * 2 + c)],
            send_sem=pair_sems.at[0, t], recv_sem=pair_sems.at[1, t],
            device_id=(me, partner), device_id_type=MESH,
        )

    pair_copies = []

    def forward(t):
        copy = to_partner(rows_out.at[:, cols(t * 2 + c)], t)
        copy.start()
        pair_copies.append(copy)

    own = pltpu.make_async_copy(head_ref, head_out.at[x, z], local_sem.at[0])
    own.start()
    copy = to_partner(rows_ref, y)
    copy.start()
    pair_copies.append(copy)
    rows_out[:, cols(v)] = rows_ref[...]
    def halves(size, start=0):
        return lambda part: pl.ds(start, size) if part is None else pl.ds(start + part * (size // 2), size // 2)

    rows_part = halves(rows_ref.shape[0])
    lo_part, hi_part = halves(half), halves(half, half)
    x_part, z_part = halves(n_x), halves(n_z)
    rows = _Ring(y, n_y, along_y, lambda t, p=None: rows_out.at[rows_part(p), cols(t * 2 + c)],
                 lambda p: rows_ref.at[rows_part(p)], sems.at[4], forward)
    first_x = _Ring(x, n_x, along_x, lambda t, p=None: head_out.at[t, z, lo_part(p)],
                    lambda p: head_ref.at[lo_part(p)], sems.at[0])
    first_z = _Ring(z, n_z, along_z, lambda t, p=None: head_out.at[x, t, hi_part(p)],
                    lambda p: head_ref.at[hi_part(p)], sems.at[1])
    first_x.advance()
    first_z.advance()
    rows.advance()
    first_x.advance()
    first_z.advance()
    own.wait()
    first_x.finish_recv()
    second_z = _Ring(z, n_z, along_z, lambda t, p=None: head_out.at[x_part(p), t, lo],
                     lambda p: head_out.at[x_part(p), z, lo], sems.at[2])
    second_x = _Ring(x, n_x, along_x, lambda t, p=None: head_out.at[t, z_part(p), hi],
                     lambda p: head_out.at[x, z_part(p), hi], sems.at[3])
    second_z.advance()
    first_z.advance()
    rows.advance()
    first_z.advance()
    first_z.finish_recv()
    second_x.advance()
    rows.advance()
    second_z.advance()
    rows.advance()
    second_z.advance()
    rows.finish_recv()
    second_x.advance()
    second_z.advance()
    for t in range(n_y):
        other = t * 2 + 1 - c
        block = rows_out.at[:, cols(other)]
        pltpu.make_async_remote_copy(
            src_ref=block, dst_ref=block,
            send_sem=pair_sems.at[0, t], recv_sem=pair_sems.at[1, t],
            device_id=(me, partner), device_id_type=MESH,
        ).wait_recv()
    chunk = 64

    def norm_chunk(i, carry):
        start = pl.multiple_of(i * chunk, chunk)
        values = rows_out[pl.ds(start, chunk), :].astype(jnp.float32)
        scale = lax.rsqrt(jnp.mean(values * values, axis=1, keepdims=True) + EPSILON)
        normed_out[pl.ds(start, chunk), :] = (values * scale * gain_ref[...]).astype(normed_out.dtype)
        return carry

    lax.fori_loop(0, rows_out.shape[0] // chunk, norm_chunk, 0)
    second_z.finish_recv()
    second_x.finish_recv()
    for ring in (first_x, first_z, second_z, second_x, rows):
        ring.finish_send()
    for copy in pair_copies:
        copy.wait_send()


def gather_both(hidden, piece, norm_gain, n_x, n_z, n_voc):
    rows, width = hidden.shape
    depth, vocab = piece.shape
    n_y = n_voc // 2
    steps = max(n_x, n_z, n_y)
    gain = norm_gain.astype(jnp.float32)[None, :]
    full_rows, full_head = pl.pallas_call(
        functools.partial(_gather_kernel, n_x, n_z, n_y),
        out_shape=(jax.ShapeDtypeStruct((rows, width * n_voc), hidden.dtype),
                   jax.ShapeDtypeStruct((n_x, n_z, depth, vocab), piece.dtype)),
        in_specs=[pl.BlockSpec(memory_space=pltpu.VMEM)] * 3,
        out_specs=(pl.BlockSpec(memory_space=pltpu.VMEM), pl.BlockSpec(memory_space=pltpu.VMEM)),
        scratch_shapes=[pltpu.VMEM((rows, width * n_voc), hidden.dtype),
                        pltpu.SemaphoreType.DMA((1,)), pltpu.SemaphoreType.DMA((5, 4, steps)),
                        pltpu.SemaphoreType.DMA((2, n_y))],
        compiler_params=pltpu.CompilerParams(collective_id=3, has_side_effects=True),
    )(hidden, piece, gain)
    return full_rows, full_head.reshape(n_x * n_z * depth, vocab)


def local(hidden, targets, row_count, norm_gain, head_weight, return_from, *, n_voc, n_grp, n_x, n_z):
    tok_rows = hidden.shape[0]
    normed, piece = gather_both(hidden, head_weight, norm_gain, n_x, n_z, n_voc)
    vocab_local = head_weight.shape[1]
    logits = jnp.dot(normed, piece, preferred_element_type=jnp.float32)
    peak = jnp.max(logits, axis=1)
    shifted = jnp.exp(logits - peak[:, None])
    total = jnp.sum(shifted, axis=1)
    weighted = jnp.sum(shifted * logits, axis=1)
    global_columns = lax.axis_index("voc") * vocab_local + jnp.arange(vocab_local, dtype=jnp.int32)
    picked = jnp.sum(jnp.where(global_columns[None, :] == targets[:, None], logits, 0.0), axis=1)
    stats = jnp.stack([peak, total, weighted, picked])
    results = exchange(stats, row_count.reshape(1, 1), n_voc, n_grp).reshape(n_grp, 2, tok_rows)
    lanes = 128
    every = jnp.concatenate(
        [results[:, 0].reshape(-1, lanes), results[:, 1].reshape(-1, lanes)], axis=1)
    high = return_from // lanes
    low = return_from % lanes
    pick_row = (high[:, None] == jnp.arange(every.shape[0], dtype=jnp.int32)[None, :]).astype(jnp.float32)
    rows_picked = jnp.dot(pick_row, every, precision=lax.Precision.HIGHEST)
    pick_lane = low[:, None] == jnp.arange(lanes, dtype=jnp.int32)[None, :]
    token_logp = jnp.sum(jnp.where(pick_lane, rows_picked[:, :lanes], 0.0), axis=1)
    token_entropy = jnp.sum(jnp.where(pick_lane, rows_picked[:, lanes:], 0.0), axis=1)
    return (token_logp, token_entropy)


def solution(mesh):
    placed = (P("grp", "voc"), P("grp"), P("grp"), P(), P("grp", "voc"), P("grp"))
    n_grp = mesh.shape["grp"]
    n_z = len({device.coords[2] for device in mesh.devices[:, 0]})
    body = functools.partial(local, n_voc=mesh.shape["voc"], n_grp=n_grp, n_x=n_grp // n_z, n_z=n_z)
    return jax.shard_map(
        body, mesh=mesh, in_specs=placed, out_specs=(P("grp"), P("grp")), check_vma=False
    )
```
